32 devices in a mesh: dp: 8 (over z, core), width: 4 (over y, x).
Axes of the slice: x: 2, y: 2, z: 4, core: 2. Of those that a mesh axis runs over, the one named last changes fastest.
Arguments:
- inputs: bfloat16 [1536, 4, 512], P('dp', 'width'), may hold values from -6 to 6
- block_weights: bfloat16 [4, 512, 3, 512], P('width'), may hold values from -0.15625 to 0.15625
- low_left: bfloat16 [4, 512, 256], P('width'), may hold values from -0.125 to 0.125
- low_right: bfloat16 [4, 256, 512], P('width'), may hold values from -0.375 to 0.375
- out_grad: bfloat16 [1536, 4, 512], P('dp', 'width'), may hold values from -6 to 6
Outputs:
- activations: bfloat16 [1536, 4, 512], P('dp', 'width')
- in_grad: bfloat16 [1536, 4, 512], P('dp', 'width')
- block_grad: float32 [4, 512, 3, 512], P('width', 'dp')
- left_grad: float32 [4, 512, 256], P('width', 'dp')
- right_grad: float32 [4, 256, 512], P('width', 'dp')
The draws below stay inside these ranges and needn't reach their ends.
All inputs are finite; a program needn't handle non-finite values.
Results may differ from the reference program's by a relative error of at most 0.0061.
Values may be sent and summed in bfloat16 or wider, within the bound.
A program may use at most 64 MiB of HBM per device.

```python
import jax
import jax.numpy as jnp
from jax import lax

BLOCK = 512
OUT_WIN = 512
RANK = 256
BLOCKS = 4
LEVELS = 2
D = 2048
TOKENS = 1536
N_WIDTH = 4


def block_levels(own_key, dims, shards, least, top_value):
    def one(position, shards_of):
        heights = jax.random.uniform(jax.random.fold_in(jax.random.fold_in(own_key, 6), position), (shards_of,), jnp.float32, least / len(shards), top_value / len(shards))
        return jnp.repeat(jnp.exp(heights), dims[position] // shards_of).reshape((-1,) + (1,) * (len(dims) - position - 1))

    level = one(*shards[0])
    for cut in shards[1:]:
        level = level * one(*cut)
    return level


def noise(key, shape, spread, limit, shards=(), held_as=jnp.bfloat16):
    result = jax.random.normal(key, shape, jnp.float32) * spread
    if len(shards) > 0:
        result = block_levels(key, shape, shards, -0.22, 0.18) * result
    return jnp.clip(result, min=-limit, max=limit).astype(held_as)


def setup_inputs(seed: int = 0) -> dict:
    arg_keys = jax.random.split(jax.random.key(seed), 6)
    inputs = noise(arg_keys[0], (TOKENS, BLOCKS, BLOCK), 1.0, 6.0, ((0, 8), (1, 4)))
    block_weights = noise(arg_keys[1], (BLOCKS, OUT_WIN, LEVELS + 1, BLOCK), ((LEVELS + 1) * BLOCK) ** -0.5, 0.15625, ((0, 4),))
    low_left = noise(arg_keys[2], (BLOCKS, BLOCK, RANK), D ** -0.5, 0.125, ((0, 4),))
    low_right = noise(arg_keys[3], (BLOCKS, RANK, OUT_WIN), RANK ** -0.5, 0.375, ((0, 4),))
    out_grad = noise(arg_keys[4], (TOKENS, BLOCKS, OUT_WIN), 1.0, 6.0, ((0, 8), (1, 4)))
    return {"inputs": inputs, "block_weights": block_weights, "low_left": low_left, "low_right": low_right, "out_grad": out_grad}


root_half = 0.7071067811865476
inv_root_two_pi = 0.3989422804014327


def gelu_value(pre):
    return 0.5 * pre * (1.0 + lax.erf(pre * root_half))


def gelu_slope(pre):
    return 0.5 * (1.0 + lax.erf(pre * root_half)) + pre * jnp.exp(-0.5 * pre * pre) * inv_root_two_pi


def reference(inputs, block_weights, low_left, low_right, out_grad):
    blocks = N_WIDTH
    distances = [0] + [1 << level for level in range(LEVELS)]
    scale = 1.0 / (float(TOKENS) ** 0.5)
    latent_sum = jnp.zeros((inputs.shape[0], RANK), jnp.float32)
    for block in range(blocks):
        latent_sum = latent_sum + jnp.dot(inputs[:, block], low_left[block], preferred_element_type=jnp.float32)
    latent = latent_sum.astype(jnp.bfloat16)
    acts_list = []
    hidden_list = []
    right_list = []
    back_list = []
    block_list = []
    latent_grad_sum = jnp.zeros((inputs.shape[0], RANK), jnp.float32)
    for block in range(blocks):
        pre = jnp.dot(latent, low_right[block], preferred_element_type=jnp.float32)
        for level in range(LEVELS + 1):
            mate_x = inputs[:, block ^ distances[level]]
            pre = pre + jnp.dot(mate_x, block_weights[block, :, level, :].T, preferred_element_type=jnp.float32)
        acts_list.append(gelu_value(pre).astype(jnp.bfloat16))
        hidden = (out_grad[:, block].astype(jnp.float32) * gelu_slope(pre)).astype(jnp.bfloat16)
        hidden_list.append(hidden)
        latent_grad_sum = latent_grad_sum + jnp.dot(hidden, low_right[block].T, preferred_element_type=jnp.float32)
        backs = []
        for level in range(LEVELS + 1):
            backs.append(jnp.dot(hidden, block_weights[block, :, level, :], preferred_element_type=jnp.float32).astype(jnp.bfloat16))
        back_list.append(backs)
        right_list.append(jnp.dot(latent.T, hidden, preferred_element_type=jnp.float32) * scale)
        terms = []
        for level in range(LEVELS + 1):
            mate_x = inputs[:, block ^ distances[level]]
            terms.append(jnp.dot(hidden.T, mate_x, preferred_element_type=jnp.float32) * scale)
        block_list.append(jnp.stack(terms, axis=1))
    latent_grad = latent_grad_sum.astype(jnp.bfloat16)
    in_list = []
    left_list = []
    for block in range(blocks):
        own_x = inputs[:, block]
        total = jnp.dot(hidden_list[block], block_weights[block, :, 0, :], preferred_element_type=jnp.float32)
        total = total + jnp.dot(latent_grad, low_left[block].T, preferred_element_type=jnp.float32)
        for level in range(1, LEVELS + 1):
            total = total + back_list[block ^ distances[level]][level].astype(jnp.float32)
        in_list.append(total.astype(jnp.bfloat16))
        left_list.append(jnp.dot(own_x.T, latent_grad, preferred_element_type=jnp.float32) * scale)
    activations = jnp.stack(acts_list, axis=1)
    in_grad = jnp.stack(in_list, axis=1)
    block_grad = jnp.stack(block_list, axis=0)
    left_grad = jnp.stack(left_list, axis=0)
    right_grad = jnp.stack(right_list, axis=0)
    return activations, in_grad, block_grad, left_grad, right_grad
```

```python
import functools
import math

import jax
import jax.numpy as jnp
from jax import lax
from jax.experimental import pallas as pl
from jax.experimental.pallas import tpu as pltpu
from jax.sharding import PartitionSpec as P

root_half = 0.7071067811865476
inv_root_two_pi = 0.3989422804014327
chips_in_line = 4


def swapped(array, axis, apart):
    return lax.ppermute(array, axis, [(i, i ^ 1 << apart) for i in range(lax.axis_size(axis))])


def gelu_value(pre):
    return 0.5 * pre * (1.0 + lax.erf(pre * root_half))


def gelu_slope(pre):
    return (
        0.5 * (1.0 + lax.erf(pre * root_half)) + pre * jnp.exp(-0.5 * pre * pre) * inv_root_two_pi
    )


def plain_shards(inputs, block_weights, low_left, low_right, out_grad):
    own_x = inputs[:, 0]
    weights = block_weights[0]
    left = low_left[0]
    right = low_right[0]
    grad_out = out_grad[:, 0]
    levels = lax.axis_size("width").bit_length() - 1
    block_size = own_x.shape[1]
    scale = 1.0 / math.sqrt(own_x.shape[0] * lax.axis_size("dp"))
    pieces = [own_x]
    for bit in range(levels):
        pieces.append(swapped(own_x, "width", bit))
    all_x = jnp.stack(pieces, axis=1)
    latent = lax.psum(jnp.dot(own_x, left, preferred_element_type=jnp.float32), "width").astype(
        jnp.bfloat16
    )
    pre = lax.dot_general(
        all_x, weights, (((1, 2), (1, 2)), ((), ())), preferred_element_type=jnp.float32
    )
    pre = pre + jnp.dot(latent, right, preferred_element_type=jnp.float32)
    activations = gelu_value(pre).astype(jnp.bfloat16)
    hidden = (grad_out.astype(jnp.float32) * gelu_slope(pre)).astype(jnp.bfloat16)
    latent_term = lax.dot_general(
        hidden, right, (((1,), (1,)), ((), ())), preferred_element_type=jnp.float32
    )
    latent_grad = lax.psum(latent_term, "width").astype(jnp.bfloat16)
    partner_w = weights[:, 1:, :].reshape(weights.shape[0], levels * block_size)
    backs = jnp.dot(hidden, partner_w, preferred_element_type=jnp.float32).astype(jnp.bfloat16)
    returned = jnp.zeros(own_x.shape, jnp.float32)
    for bit in range(levels):
        piece = backs[:, bit * block_size : (bit + 1) * block_size]
        returned = returned + swapped(piece, "width", bit).astype(jnp.float32)
    own_back = jnp.dot(hidden, weights[:, 0, :], preferred_element_type=jnp.float32)
    own_back = own_back + lax.dot_general(
        latent_grad, left, (((1,), (1,)), ((), ())), preferred_element_type=jnp.float32
    )
    in_grad = (own_back + returned).astype(jnp.bfloat16)
    left_term = (
        lax.dot_general(
            own_x, latent_grad, (((0,), (0,)), ((), ())), preferred_element_type=jnp.float32
        )
        * scale
    )
    right_term = (
        lax.dot_general(
            latent, hidden, (((0,), (0,)), ((), ())), preferred_element_type=jnp.float32
        )
        * scale
    )
    block_term = (
        lax.dot_general(hidden, all_x, (((0,), (0,)), ((), ())), preferred_element_type=jnp.float32)
        * scale
    )
    block_grad, left_grad, right_grad = (
        lax.psum_scatter(block_term, "dp", scatter_dimension=0, tiled=True),
        lax.psum_scatter(left_term, "dp", scatter_dimension=0, tiled=True),
        lax.psum_scatter(right_term, "dp", scatter_dimension=0, tiled=True),
    )
    return (
        activations[:, None],
        in_grad[:, None],
        block_grad[None],
        left_grad[None],
        right_grad[None],
    )


f32 = jnp.float32
bf16 = jnp.bfloat16


def dot_nn(a, b):
    return jnp.dot(a, b, preferred_element_type=f32)


def dot_nt(a, b):
    return lax.dot_general(a, b, (((1,), (1,)), ((), ())), preferred_element_type=f32)


def remote(src, dst, send, recv, dp, width):
    return pltpu.make_async_remote_copy(
        src_ref=src,
        dst_ref=dst,
        send_sem=send,
        recv_sem=recv,
        device_id={"dp": dp, "width": width},
        device_id_type=pl.DeviceIdType.MESH,
    )


def step_kernel(
    n_dp, n_width, scale,
    x_hbm, w_hbm, left_hbm, right_hbm, g_hbm,
    act_out, in_out, block_out, left_out, right_out,
    x, w, left, right, g,
    lat_sum, lat_own, lat_got, lat, lg_own, lg_got, lg, hidden,
    x_t, x_u, h_t, h_u, lat_t, lat_u, far_acc,
    back_own, back_got, pre,
    away_b, own_b, core_b, far_b, near_b, end_b, fin_b,
    away_r, own_r, core_r, far_r, near_r, end_r, fin_r,
    away_l, own_l, core_l, far_l, near_l, end_l, fin_l,
    load_sem, x_send, x_recv, lat_send, lat_recv, lg_send, lg_recv, back_send, back_recv,
    up_send, up_recv, side_send, side_recv,
    core_send, core_recv, mid_send, mid_recv, end_send, end_recv,
):
    levels = n_width.bit_length() - 1
    chips = n_dp // 2
    dp = lax.axis_index("dp")
    me = lax.axis_index("width")
    chip, core = dp // 2, dp % 2
    other_core = 1 - core
    twin = dp + 1 - 2 * core
    side = chip // 2
    outer = (chip + side) % 2
    is_end = outer == 0
    is_hub = outer == 1
    step = 2 - 4 * side
    hub_dp = dp + step
    end_dp = dp - step
    far_dp = dp + step

    def mate(k):
        at = me
        for bit in range(levels):
            if k >> bit & 1:
                at = at + (1 << bit) * (1 - 2 * ((me // (1 << bit)) % 2))
        return at

    def shard(p):
        first = (3, 2, 0, 1)[p]
        return first + side * (chips - 1 - 2 * first)

    barrier = pltpu.get_barrier_semaphore()

    def greet(to_dp, to_width):
        pl.semaphore_signal(
            barrier,
            inc=1,
            device_id={"dp": to_dp, "width": to_width},
            device_id_type=pl.DeviceIdType.MESH,
        )

    for k in range(1, n_width):
        greet(dp, mate(k))
    greet(twin, me)

    @pl.when(chip > 0)
    def _():
        greet(dp - 2, me)

    @pl.when(chip < chips - 1)
    def _():
        greet(dp + 2, me)

    rows = x_hbm.shape[0]
    mine, theirs = pl.ds(0, rows), pl.ds(rows, rows)
    loads = [
        pltpu.make_async_copy(src, dst, load_sem.at[i])
        for i, (src, dst) in enumerate(
            (
                (x_hbm, x.at[0, mine]),
                (left_hbm, left),
                (w_hbm, w),
                (right_hbm, right),
                (g_hbm, g),
            )
        )
    ]
    for load in loads:
        load.start()

    ends = jnp.where(chip == 0, 1, 0) + jnp.where(chip == chips - 1, 1, 0)
    pl.semaphore_wait(barrier, n_width + 2 - ends)

    loads[0].wait()
    cut = rows // levels
    parts = [pl.ds(j * cut, cut) for j in range(levels)]
    beyond = [pl.ds(rows + j * cut, cut) for j in range(levels)]
    x_copies = [
        [
            remote(
                x.at[0, part], x.at[bit + 1, part], x_send.at[j, bit], x_recv.at[j, bit],
                dp, mate(1 << bit),
            )
            for bit in range(levels)
        ]
        for j, part in enumerate(parts)
    ]

    def exchange(sums, out, got, send, recv, t):
        copies = []
        for j, part in enumerate(parts):
            out[t, part] = sums[part].astype(bf16)
            copies.append(
                remote(
                    out.at[t, part], got.at[t, part], send.at[t, j], recv.at[t, j],
                    dp, mate(1 << (j + t) % levels),
                )
            )
        for copy in copies:
            copy.start()
        return copies

    def merge(copies, sums, got, t, j):
        copies[j].wait_recv()
        sums[parts[j]] += got[t, parts[j]].astype(f32)

    up_x = remote(x.at[0, mine], x.at[0, theirs], up_send.at[0], up_recv.at[0], hub_dp, me)
    side_copies = [
        remote(
            x.at[0, theirs], x.at[bit + 1, theirs], side_send.at[bit], side_recv.at[bit],
            dp, mate(1 << bit),
        )
        for bit in range(levels)
    ]

    @pl.when(is_end)
    def _():
        up_x.start()

    loads[1].wait()
    lat_sum[...] = dot_nn(x[0, mine], left[...])
    lat_copies = [exchange(lat_sum, lat_own, lat_got, lat_send, lat_recv, 0)]
    for copy in x_copies[0]:
        copy.start()
    loads[2].wait()
    pre[...] = dot_nt(x[0, mine], w[0])
    for t in range(1, levels):
        for j in range(levels):
            merge(lat_copies[-1], lat_sum, lat_got, t - 1, j)
        lat_copies.append(exchange(lat_sum, lat_own, lat_got, lat_send, lat_recv, t))
        for copy in x_copies[t]:
            copy.start()
    loads[3].wait()
    loads[4].wait()

    ob, rb, ib = h_t.shape[2], lat_t.shape[2], x_t.shape[2]
    last = levels + 1

    def span(p, size):
        return pl.ds(pl.multiple_of(shard(p) * size, size), size)

    up_h = [
        [
            remote(
                hidden.at[part, span(p, 2 * ob)], hidden.at[away_part, span(p, 2 * ob)],
                up_send.at[2 + levels + chips * j + p], up_recv.at[2 + levels + chips * j + p],
                hub_dp, me,
            )
            for p in range(chips)
        ]
        for j, (part, away_part) in enumerate(zip(parts, beyond))
    ]
    up_lat = [
        remote(
            lat.at[part], lat.at[away_part], up_send.at[2 + j], up_recv.at[2 + j], hub_dp, me
        )
        for j, (part, away_part) in enumerate(zip(parts, beyond))
    ]
    up_lg = remote(lg.at[mine], lg.at[theirs], up_send.at[1], up_recv.at[1], hub_dp, me)

    for j, part in enumerate(parts):
        merge(lat_copies[-1], lat_sum, lat_got, levels - 1, j)
        lat[part, :] = lat_sum[part, :].astype(bf16)
        v = pre[part, :] + dot_nn(lat[part, :], right[...])
        for bit in range(levels):
            x_copies[j][bit].wait_recv()
            v = v + dot_nt(x[bit + 1, part], w[bit + 1])
        half = 0.5 * (1.0 + lax.erf(v * root_half))
        act_out[part, :] = (v * half).astype(bf16)
        slope = half + v * jnp.exp(-0.5 * v * v) * inv_root_two_pi
        hidden[part, :] = (g[part, :].astype(f32) * slope).astype(bf16)

        @pl.when(is_end)
        def _():
            for p in range(2):
                up_h[j][p].start()
            up_lat[j].start()

        if j == 0:

            @pl.when(is_hub)
            def _():
                up_x.wait_recv()
                for copy in side_copies:
                    copy.start()


    lat_sum[...] = dot_nt(hidden[mine, :], right[...])
    lg_copies = [exchange(lat_sum, lg_own, lg_got, lg_send, lg_recv, 0)]

    def pick(kind, s):
        block, low_right, low_left = kind
        if s < last:
            return block.at[s]
        return low_right if s == last else low_left

    away = (away_b, away_r, away_l)
    own = (own_b, own_r, own_l)
    cored = (core_b, core_r, core_l)
    far = (far_b, far_r, far_l)
    near = (near_b, near_r, near_l)
    ended = (end_b, end_r, end_l)
    fin = (fin_b, fin_r, fin_l)
    segments = range(last + 2)

    def core_copy(s, p):
        return remote(
            pick(away, s).at[p], pick(cored, s).at[p], core_send.at[s, p], core_recv.at[s, p],
            twin, me,
        )

    def mid_copy(s, p):
        return remote(
            pick(far, s).at[p], pick(near, s).at[p], mid_send.at[s, p], mid_recv.at[s, p],
            far_dp, me,
        )

    def end_copy(s):
        return remote(
            pick(ended, s), pick(fin, s), end_send.at[s], end_recv.at[s], end_dp, me
        )

    def put(s, total):
        if s < last:
            block_out[s] = total * scale
        elif s == last:
            right_out[...] = total * scale
        else:
            left_out[...] = total * scale

    back_copies = [
        remote(
            back_own.at[bit], back_got.at[bit], back_send.at[bit], back_recv.at[bit],
            dp, mate(1 << bit),
        )
        for bit in range(levels)
    ]

    def lg_step(t):
        for j in range(levels):
            merge(lg_copies[-1], lat_sum, lg_got, t - 1, j)
        if t < levels:
            lg_copies.append(exchange(lat_sum, lg_own, lg_got, lg_send, lg_recv, t))
        else:
            lg[mine, :] = lat_sum[...].astype(bf16)

    def send_back():
        for bit in range(levels):
            back_own[bit] = dot_nn(hidden[mine, :], w[bit + 1]).astype(bf16)
            back_copies[bit].start()

    def back_ready():
        total = dot_nn(hidden[mine, :], w[0]) + dot_nt(lg[mine, :], left[...])
        for bit in range(levels):
            back_copies[bit].wait_recv()
            total = total + back_got[bit].astype(f32)
        in_out[...] = total.astype(bf16)

    def sent():
        for group in x_copies + lat_copies + lg_copies + [back_copies]:
            for copy in group:
                copy.wait_send()

    @pl.when(is_end)
    def _():
        for j in range(levels):
            for p in range(2, chips):
                up_h[j][p].start()
        for t in range(1, levels + 1):
            lg_step(t)
            if t == levels - 1:
                send_back()
        up_lg.start()
        back_ready()
        sent()
        up_x.wait_send()
        up_lg.wait_send()
        for j in range(levels):
            up_lat[j].wait_send()
            for p in range(chips):
                up_h[j][p].wait_send()
        for s in segments:
            end_copy(s).wait_recv()
            put(s, pick(fin, s)[...].astype(f32))

    del lg_copies[1:]

    @pl.when(is_hub)
    def _():
        def turn(ref, which, p, size):
            tall = ref[which, span(p, size)].astype(f32).T.astype(bf16)
            return tall.reshape(2, size // 2, rows)

        def stack(ref, which, positions):
            return jnp.concatenate([ref[p, which] for p in positions], axis=0)

        def own_rows(s, which, positions):
            if s < last:
                return dot_nn(stack(h_t, which, positions), x[s, mine])
            if s == last:
                return dot_nn(stack(lat_t, which, [shard(p) for p in positions]), hidden[mine, :])
            return dot_nn(stack(x_t, which, positions), lg[mine, :])

        def their_rows(s, which, positions):
            if s < last:
                return dot_nn(stack(h_u, which, positions), x[s, theirs])
            if s == last:
                return dot_nn(stack(lat_u, which, [shard(p) for p in positions]), hidden[theirs, :])
            return dot_nn(stack(x_u, which, positions), lg[theirs, :])

        def put_terms(s, positions, to_other, to_own):
            shape = pick(own, s).shape[1:]
            for i, p in enumerate(positions):
                these = slice(i * shape[0], (i + 1) * shape[0])
                pick(away, s)[p] = to_other[these].astype(bf16)
                core_copy(s, p).start()
            for i, p in enumerate(positions):
                these = slice(i * shape[0], (i + 1) * shape[0])
                pick(own, s)[p] = to_own[these]

        def terms(s, positions):
            first = own_rows(s, other_core, positions) + their_rows(s, other_core, positions)
            put_terms(
                s, positions, first, own_rows(s, core, positions) + their_rows(s, core, positions)
            )

        def far_terms(s, positions):
            size = len(positions) * ob
            held = slice(positions[0], positions[0] + len(positions))
            first = far_acc[s, held].reshape(size, far_acc.shape[3])
            second = own_b[s, held].reshape(size, far_acc.shape[3])
            put_terms(
                s, positions, first + their_rows(s, other_core, positions),
                second + their_rows(s, core, positions),
            )

        def pair(s, p):
            return pick(own, s)[p] + pick(cored, s)[p].astype(f32)

        def send_far(s, p):
            core_copy(s, p).wait_recv()
            pick(far, s)[p] = pair(s, p).astype(bf16)
            mid_copy(s, p).start()

        for p in range(2):
            h_t[p] = turn(hidden, mine, p, 2 * ob)
        for s in range(last):
            shape = (2, ob, far_acc.shape[3])
            far_acc[s] = own_rows(s, other_core, range(2)).reshape(shape)
            own_b[s, 0:2] = own_rows(s, core, range(2)).reshape(shape)
        for p in range(2):
            for j in range(levels):
                up_h[j][p].wait_recv()
            h_u[p] = turn(hidden, theirs, p, 2 * ob)
            far_terms(0, [p])
        for p in range(2):
            send_far(0, p)
        for bit in range(levels):
            side_copies[bit].wait_recv()
            far_terms(bit + 1, [0, 1])
        for t in range(1, levels):
            lg_step(t)
        send_back()
        for s in range(1, last):
            for p in range(2):
                send_far(s, p)
        for j in range(levels):
            up_lat[j].wait_recv()
        lat_t[...] = lat[mine, :].astype(f32).T.astype(bf16).reshape(lat_t.shape)
        lat_u[...] = lat[theirs, :].astype(f32).T.astype(bf16).reshape(lat_t.shape)
        for p in range(2, chips):
            for j in range(levels):
                up_h[j][p].wait_recv()
        terms(last, range(2))
        for p in range(2, chips):
            h_t[p] = turn(hidden, mine, p, 2 * ob)
            h_u[p] = turn(hidden, theirs, p, 2 * ob)
        for s in range(last):
            terms(s, range(2, chips))
        terms(last, range(2, chips))
        for p in range(chips):
            x_t[p] = turn(x.at[0], mine, p, 2 * ib)
            x_u[p] = turn(x.at[0], theirs, p, 2 * ib)
        lg_step(levels)
        up_lg.wait_recv()
        terms(last + 1, range(2))
        for p in range(2):
            send_far(last, p)
            send_far(last + 1, p)
        terms(last + 1, range(2, chips))

        def send_end(s):
            core_copy(s, 2).wait_recv()
            mid_copy(s, 0).wait_recv()
            pick(ended, s)[...] = (pair(s, 2) + pick(near, s)[0].astype(f32)).astype(bf16)
            end_copy(s).start()

        def keep(s):
            core_copy(s, 3).wait_recv()
            mid_copy(s, 1).wait_recv()
            put(s, pair(s, 3) + pick(near, s)[1].astype(f32))

        for s in range(last):
            send_end(s)
            keep(s)
        back_ready()
        sent()
        for copy in side_copies:
            copy.wait_send()
        for s in segments:
            for p in range(chips):
                core_copy(s, p).wait_send()
        send_end(last)
        send_end(last + 1)
        keep(last)
        keep(last + 1)
        for s in segments:
            for p in range(2):
                mid_copy(s, p).wait_send()
            end_copy(s).wait_send()


def hand_over(*refs):
    copies = [pltpu.make_async_copy(refs[i], refs[5 + i], refs[10].at[i]) for i in range(5)]
    for copy in copies:
        copy.start()
    for copy in copies:
        copy.wait()


def shards(inputs, block_weights, low_left, low_right, out_grad):
    n_dp, n_width = lax.axis_size("dp"), lax.axis_size("width")
    levels = n_width.bit_length() - 1
    rows, _, width_in = inputs.shape
    width_out = block_weights.shape[1]
    rank = low_left.shape[2]
    ob, ib, rb = width_out // n_dp, width_in // n_dp, rank // n_dp
    fits = n_dp == 2 * chips_in_line and rows % (16 * n_width) == 0 and rows % 32 == 0 and width_in == width_out
    if not fits or ob % 64 or ib % 64 or rb % 16 or levels < 1 or rows % (16 * levels) or rank % 128:
        return plain_shards(inputs, block_weights, low_left, low_right, out_grad)
    chips = n_dp // 2
    scale = 1.0 / math.sqrt(rows * n_dp)
    vm, dma = pltpu.VMEM, pltpu.SemaphoreType.DMA

    def line_scratch(lead, r, c):
        return [
            vm((*lead, chips, r, c), bf16),
            vm((*lead, chips, r, c), f32),
            vm((*lead, chips, r, c), bf16),
            vm((*lead, 2, r, c), bf16),
            vm((*lead, 2, r, c), bf16),
            vm((*lead, r, c), bf16),
            vm((*lead, r, c), bf16),
        ]

    outs = pl.pallas_call(
        functools.partial(step_kernel, n_dp, n_width, scale),
        out_shape=(
            jax.ShapeDtypeStruct((rows, width_out), bf16),
            jax.ShapeDtypeStruct((rows, width_in), bf16),
            jax.ShapeDtypeStruct((levels + 1, ob, width_in), f32),
            jax.ShapeDtypeStruct((ib, rank), f32),
            jax.ShapeDtypeStruct((rb, width_out), f32),
        ),
        in_specs=[pl.BlockSpec(memory_space=pltpu.HBM)] * 5,
        out_specs=(pl.BlockSpec(memory_space=pltpu.VMEM),) * 5,
        scratch_shapes=[
            vm((levels + 1, 2 * rows, width_in), bf16),
            vm((levels + 1, width_out, width_in), bf16),
            vm((width_in, rank), bf16),
            vm((rank, width_out), bf16),
            vm((rows, width_out), bf16),
            vm((rows, rank), f32),
            vm((levels, rows, rank), bf16),
            vm((levels, rows, rank), bf16),
            vm((2 * rows, rank), bf16),
            vm((levels, rows, rank), bf16),
            vm((levels, rows, rank), bf16),
            vm((2 * rows, rank), bf16),
            vm((2 * rows, width_out), bf16),
            vm((chips, 2, ib, rows), bf16),
            vm((chips, 2, ib, rows), bf16),
            vm((chips, 2, ob, rows), bf16),
            vm((chips, 2, ob, rows), bf16),
            vm((chips, 2, rb, rows), bf16),
            vm((chips, 2, rb, rows), bf16),
            vm((levels + 1, 2, ob, width_in), f32),
            vm((levels, rows, width_in), bf16),
            vm((levels, rows, width_in), bf16),
            vm((rows, width_out), f32),
            *line_scratch((levels + 1,), ob, width_in),
            *line_scratch((), rb, width_out),
            *line_scratch((), ib, rank),
            dma((5,)),
            dma((levels, levels)),
            dma((levels, levels)),
            dma((levels, levels)),
            dma((levels, levels)),
            dma((levels, levels)),
            dma((levels, levels)),
            dma((levels,)),
            dma((levels,)),
            dma((2 + levels * (1 + chips),)),
            dma((2 + levels * (1 + chips),)),
            dma((levels,)),
            dma((levels,)),
            dma((levels + 3, chips)),
            dma((levels + 3, chips)),
            dma((levels + 3, 2)),
            dma((levels + 3, 2)),
            dma((levels + 3,)),
            dma((levels + 3,)),
        ],
        compiler_params=pltpu.CompilerParams(
            collective_id=0, has_side_effects=True, vmem_limit_bytes=40 * 1024 * 1024
        ),
    )(
        *(
            pltpu.with_memory_space_constraint(array, pltpu.HBM)
            for array in (
                inputs[:, 0],
                block_weights[0].transpose(1, 0, 2),
                low_left[0],
                low_right[0],
                out_grad[:, 0],
            )
        )
    )
    act, in_grad, block, left, right = pl.pallas_call(
        hand_over,
        out_shape=tuple(jax.ShapeDtypeStruct(out.shape, out.dtype) for out in outs),
        in_specs=[pl.BlockSpec(memory_space=pltpu.VMEM)] * 5,
        out_specs=(pl.BlockSpec(memory_space=pl.ANY),) * 5,
        scratch_shapes=[dma((5,))],
        compiler_params=pltpu.CompilerParams(vmem_limit_bytes=4 * 1024 * 1024),
    )(*outs)
    return (
        act[:, None],
        in_grad[:, None],
        block.transpose(1, 0, 2)[None],
        left[None],
        right[None],
    )


def solution(mesh):
    placed = (
        P("dp", "width", None),
        P("width", None, None, None),
        P("width", None, None),
        P("width", None, None),
        P("dp", "width", None),
    )
    return jax.shard_map(
        shards,
        mesh=mesh,
        in_specs=placed,
        out_specs=(
            P("dp", "width", None),
            P("dp", "width", None),
            P("width", "dp", None, None),
            P("width", "dp", None),
            P("width", "dp", None),
        ),
        check_vma=False,
    )
```

```python
import functools
import math

import jax
import jax.numpy as jnp
from jax import lax
from jax.experimental import pallas as pl
from jax.experimental.pallas import tpu as pltpu
from jax.sharding import PartitionSpec as P

root_half = 0.7071067811865476
inv_root_two_pi = 0.3989422804014327
chips_in_line = 4


def swapped(array, axis, apart):
    return lax.ppermute(array, axis, [(i, i ^ 1 << apart) for i in range(lax.axis_size(axis))])


def gelu_value(pre):
    return 0.5 * pre * (1.0 + lax.erf(pre * root_half))


def gelu_slope(pre):
    return (
        0.5 * (1.0 + lax.erf(pre * root_half)) + pre * jnp.exp(-0.5 * pre * pre) * inv_root_two_pi
    )


def plain_shards(inputs, block_weights, low_left, low_right, out_grad):
    own_x = inputs[:, 0]
    weights = block_weights[0]
    left = low_left[0]
    right = low_right[0]
    grad_out = out_grad[:, 0]
    levels = lax.axis_size("width").bit_length() - 1
    block_size = own_x.shape[1]
    scale = 1.0 / math.sqrt(own_x.shape[0] * lax.axis_size("dp"))
    pieces = [own_x]
    for bit in range(levels):
        pieces.append(swapped(own_x, "width", bit))
    all_x = jnp.stack(pieces, axis=1)
    latent = lax.psum(jnp.dot(own_x, left, preferred_element_type=jnp.float32), "width").astype(
        jnp.bfloat16
    )
    pre = lax.dot_general(
        all_x, weights, (((1, 2), (1, 2)), ((), ())), preferred_element_type=jnp.float32
    )
    pre = pre + jnp.dot(latent, right, preferred_element_type=jnp.float32)
    activations = gelu_value(pre).astype(jnp.bfloat16)
    hidden = (grad_out.astype(jnp.float32) * gelu_slope(pre)).astype(jnp.bfloat16)
    latent_term = lax.dot_general(
        hidden, right, (((1,), (1,)), ((), ())), preferred_element_type=jnp.float32
    )
    latent_grad = lax.psum(latent_term, "width").astype(jnp.bfloat16)
    partner_w = weights[:, 1:, :].reshape(weights.shape[0], levels * block_size)
    backs = jnp.dot(hidden, partner_w, preferred_element_type=jnp.float32).astype(jnp.bfloat16)
    returned = jnp.zeros(own_x.shape, jnp.float32)
    for bit in range(levels):
        piece = backs[:, bit * block_size : (bit + 1) * block_size]
        returned = returned + swapped(piece, "width", bit).astype(jnp.float32)
    own_back = jnp.dot(hidden, weights[:, 0, :], preferred_element_type=jnp.float32)
    own_back = own_back + lax.dot_general(
        latent_grad, left, (((1,), (1,)), ((), ())), preferred_element_type=jnp.float32
    )
    in_grad = (own_back + returned).astype(jnp.bfloat16)
    left_term = (
        lax.dot_general(
            own_x, latent_grad, (((0,), (0,)), ((), ())), preferred_element_type=jnp.float32
        )
        * scale
    )
    right_term = (
        lax.dot_general(
            latent, hidden, (((0,), (0,)), ((), ())), preferred_element_type=jnp.float32
        )
        * scale
    )
    block_term = (
        lax.dot_general(hidden, all_x, (((0,), (0,)), ((), ())), preferred_element_type=jnp.float32)
        * scale
    )
    block_grad, left_grad, right_grad = (
        lax.psum_scatter(block_term, "dp", scatter_dimension=0, tiled=True),
        lax.psum_scatter(left_term, "dp", scatter_dimension=0, tiled=True),
        lax.psum_scatter(right_term, "dp", scatter_dimension=0, tiled=True),
    )
    return (
        activations[:, None],
        in_grad[:, None],
        block_grad[None],
        left_grad[None],
        right_grad[None],
    )


f32 = jnp.float32
bf16 = jnp.bfloat16


def dot_nn(a, b):
    return jnp.dot(a, b, preferred_element_type=f32)


def dot_nt(a, b):
    return lax.dot_general(a, b, (((1,), (1,)), ((), ())), preferred_element_type=f32)


def remote(src, dst, send, recv, dp, width):
    return pltpu.make_async_remote_copy(
        src_ref=src,
        dst_ref=dst,
        send_sem=send,
        recv_sem=recv,
        device_id={"dp": dp, "width": width},
        device_id_type=pl.DeviceIdType.MESH,
    )


def step_kernel(
    n_dp, n_width, scale,
    x_hbm, w_hbm, left_hbm, right_hbm, g_hbm,
    act_out, in_out, block_out, left_out, right_out,
    x, w, left, right, g,
    lat_sum, lat_own, lat_got, lat, lg_own, lg_got, lg, hidden,
    x_t, x_u, h_t, h_u, lat_t, lat_u, far_acc,
    back_own, back_got, pre,
    away_b, own_b, core_b, far_b, near_b, end_b, fin_b,
    away_r, own_r, core_r, far_r, near_r, end_r, fin_r,
    away_l, own_l, core_l, far_l, near_l, end_l, fin_l,
    load_sem, x_send, x_recv, lat_send, lat_recv, lg_send, lg_recv, back_send, back_recv,
    up_sem, side_send, side_recv, core_send, core_recv, mid_send, mid_recv, end_sem,
):
    levels = n_width.bit_length() - 1
    chips = n_dp // 2
    dp = lax.axis_index("dp")
    me = lax.axis_index("width")
    chip, core = dp // 2, dp % 2
    other_core = 1 - core
    twin = dp + 1 - 2 * core
    side = chip // 2
    outer = (chip + side) % 2
    is_end = outer == 0
    is_hub = outer == 1
    step = 2 - 4 * side
    hub_dp = dp + step
    end_dp = dp - step
    far_dp = dp + step

    def mate(k):
        at = me
        for bit in range(levels):
            if k >> bit & 1:
                at = at + (1 << bit) * (1 - 2 * ((me // (1 << bit)) % 2))
        return at

    def shard(p):
        first = (3, 2, 0, 1)[p]
        return first + side * (chips - 1 - 2 * first)

    barrier = pltpu.get_barrier_semaphore()

    def greet(to_dp, to_width):
        pl.semaphore_signal(
            barrier,
            inc=1,
            device_id={"dp": to_dp, "width": to_width},
            device_id_type=pl.DeviceIdType.MESH,
        )

    for k in range(1, n_width):
        greet(dp, mate(k))
    greet(twin, me)

    @pl.when(chip > 0)
    def _():
        greet(dp - 2, me)

    @pl.when(chip < chips - 1)
    def _():
        greet(dp + 2, me)

    rows = x_hbm.shape[0]
    mine, theirs = pl.ds(0, rows), pl.ds(rows, rows)
    loads = [
        pltpu.make_async_copy(src, dst, load_sem.at[i])
        for i, (src, dst) in enumerate(
            (
                (x_hbm, x.at[0, mine]),
                (left_hbm, left),
                (w_hbm, w),
                (right_hbm, right),
                (g_hbm, g),
            )
        )
    ]
    for load in loads:
        load.start()

    ends = jnp.where(chip == 0, 1, 0) + jnp.where(chip == chips - 1, 1, 0)
    pl.semaphore_wait(barrier, n_width + 2 - ends)

    cut = rows // levels
    lead = cut // 48 * 16
    parts = [pl.ds(j * cut, cut) for j in range(levels)]
    beyond = [pl.ds(rows + j * cut, cut) for j in range(levels)]

    def x_group(part, src, j):
        return [
            remote(
                src.at[part], x.at[bit + 1, part], x_send, x_recv.at[j], dp, mate(1 << bit)
            )
            for bit in range(levels)
        ]

    x_lead = x_group(pl.ds(0, lead), x_hbm, 0)
    x_copies = [x_group(pl.ds(lead, cut - lead), x.at[0], 0)]
    for j in range(1, levels):
        x_copies.append(x_group(parts[j], x.at[0], j))

    def exchange(sums, out, got, send, recv, t):
        copies = []
        for j, part in enumerate(parts):
            out[t, part] = sums[part].astype(bf16)
            copies.append(
                remote(
                    out.at[t, part], got.at[t, part], send, recv(t, j),
                    dp, mate(1 << (j + t) % levels),
                )
            )
        for copy in copies:
            copy.start()

    def arrived(ref, sem):
        remote(ref, ref, core_send.at[0], sem, twin, me).wait_recv()

    def left_here(ref, sem):
        remote(ref, ref, sem, core_recv.at[0], twin, me).wait_send()

    def lat_sem(t, j):
        return lat_recv.at[t + (j if t == levels - 1 else 0)]

    def lg_sem(t, j):
        return lg_recv.at[t]

    up_x = remote(x_hbm, x.at[0, theirs], up_sem.at[0], up_sem.at[0], hub_dp, me)
    side_copies = [
        remote(
            x.at[0, theirs], x.at[bit + 1, theirs], side_send, side_recv, dp, mate(1 << bit)
        )
        for bit in range(levels)
    ]

    @pl.when(is_end)
    def _():
        up_x.start()

    for copy in x_lead:
        copy.start()
    loads[0].wait()
    loads[1].wait()
    lat_sum[...] = dot_nn(x[0, mine], left[...])
    exchange(lat_sum, lat_own, lat_got, lat_send, lat_sem, 0)
    for copy in x_copies[0]:
        copy.start()
    loads[2].wait()
    pre[...] = dot_nt(x[0, mine], w[0])
    for t in range(1, levels):
        arrived(lat_got.at[t - 1], lat_recv.at[t - 1])
        lat_sum[...] += lat_got[t - 1].astype(f32)
        exchange(lat_sum, lat_own, lat_got, lat_send, lat_sem, t)
        for copy in x_copies[t]:
            copy.start()
    loads[3].wait()
    loads[4].wait()

    ob, rb, ib = h_t.shape[2], lat_t.shape[2], x_t.shape[2]
    last = levels + 1

    def span(p, size):
        return pl.ds(pl.multiple_of(shard(p) * size, size), size)

    up_h = [
        [
            remote(
                hidden.at[part, span(p, 2 * ob)], hidden.at[away_part, span(p, 2 * ob)],
                up_sem.at[3 + min(p, 2)], up_sem.at[3 + min(p, 2)], hub_dp, me,
            )
            for p in range(chips)
        ]
        for part, away_part in zip(parts, beyond)
    ]
    up_lat = remote(lat.at[mine], lat.at[theirs], up_sem.at[1], up_sem.at[1], hub_dp, me)
    up_lg = remote(lg.at[mine], lg.at[theirs], up_sem.at[2], up_sem.at[2], hub_dp, me)
    up_views = [
        x.at[0, theirs], lat.at[theirs], lg.at[theirs],
        hidden.at[theirs, pl.ds(0, 2 * ob)], hidden.at[theirs, pl.ds(0, 2 * ob)],
        hidden.at[theirs, pl.ds(0, 2 * ob * (chips - 2))],
    ]

    for j, part in enumerate(parts):
        arrived(lat_got.at[levels - 1, part], lat_sem(levels - 1, j))
        lat[part, :] = (lat_sum[part, :] + lat_got[levels - 1, part].astype(f32)).astype(bf16)
        v = pre[part, :] + dot_nn(lat[part, :], right[...])
        arrived(x.at[pl.ds(1, levels), part], x_recv.at[j])
        for bit in range(levels):
            v = v + dot_nt(x[bit + 1, part], w[bit + 1])
        half = 0.5 * (1.0 + lax.erf(v * root_half))
        act_out[part, :] = (v * half).astype(bf16)
        slope = half + v * jnp.exp(-0.5 * v * v) * inv_root_two_pi
        hidden[part, :] = (g[part, :].astype(f32) * slope).astype(bf16)

        @pl.when(is_end)
        def _():
            for p in range(2):
                up_h[j][p].start()
            if j == levels - 1:
                up_lat.start()

        if j == 0:

            @pl.when(is_hub)
            def _():
                arrived(up_views[0], up_sem.at[0])
                for copy in side_copies:
                    copy.start()


    lat_sum[...] = dot_nt(hidden[mine, :], right[...])
    exchange(lat_sum, lg_own, lg_got, lg_send, lg_sem, 0)

    def pick(kind, s):
        block, low_right, low_left = kind
        if s < last:
            return block.at[s]
        return low_right if s == last else low_left

    away = (away_b, away_r, away_l)
    own = (own_b, own_r, own_l)
    cored = (core_b, core_r, core_l)
    far = (far_b, far_r, far_l)
    near = (near_b, near_r, near_l)
    ended = (end_b, end_r, end_l)
    fin = (fin_b, fin_r, fin_l)
    segments = range(last + 2)

    def kind_of(s):
        return min(max(s - last + 1, 0), 2)

    def core_slot(s, p):
        if p > 1:
            return levels + 4 + kind_of(s)
        return p if s == 0 else s + 1

    def mid_slot(s, p):
        return s if p == 0 else levels + 3 + kind_of(s)

    def core_copy(s, p):
        return remote(
            pick(away, s).at[p], pick(cored, s).at[p],
            core_send.at[kind_of(s)], core_recv.at[core_slot(s, p)], twin, me,
        )

    def mid_copy(s, p):
        return remote(
            pick(far, s).at[p], pick(near, s).at[p],
            mid_send.at[kind_of(s)], mid_recv.at[mid_slot(s, p)], far_dp, me,
        )

    def end_copy(s):
        return remote(
            pick(ended, s), pick(fin, s), end_sem.at[kind_of(s)], end_sem.at[kind_of(s)],
            end_dp, me,
        )

    def put(s, total):
        if s < last:
            block_out[s] = total * scale
        elif s == last:
            right_out[...] = total * scale
        else:
            left_out[...] = total * scale

    back_copies = [
        remote(
            back_own.at[bit], back_got.at[bit], back_send, back_recv, dp, mate(1 << bit)
        )
        for bit in range(levels)
    ]

    def lg_step(t):
        arrived(lg_got.at[t - 1], lg_recv.at[t - 1])
        if t < levels:
            lat_sum[...] += lg_got[t - 1].astype(f32)
            exchange(lat_sum, lg_own, lg_got, lg_send, lg_sem, t)
        else:
            lg[mine, :] = (lat_sum[...] + lg_got[t - 1].astype(f32)).astype(bf16)

    def send_back():
        for bit in range(levels):
            back_own[bit] = dot_nn(hidden[mine, :], w[bit + 1]).astype(bf16)
            back_copies[bit].start()

    def back_ready():
        total = dot_nn(hidden[mine, :], w[0]) + dot_nt(lg[mine, :], left[...])
        arrived(back_got, back_recv)
        for bit in range(levels):
            total = total + back_got[bit].astype(f32)
        in_out[...] = total.astype(bf16)

    def sent():
        left_here(x.at[pl.ds(1, levels), mine], x_send)
        left_here(lat_own, lat_send)
        left_here(lg_own, lg_send)
        left_here(back_own, back_send)

    @pl.when(is_end)
    def _():
        for j in range(levels):
            for p in range(2, chips):
                up_h[j][p].start()
        for t in range(1, levels + 1):
            lg_step(t)
            if t == levels - 1:
                send_back()
        up_lg.start()
        back_ready()
        sent()
        for i, view in enumerate(up_views):
            left_here(view, up_sem.at[i])
        arrived(fin_b, end_sem.at[0])
        for s in range(last):
            put(s, fin_b[s].astype(f32))
        for s in range(last, last + 2):
            arrived(pick(fin, s), end_sem.at[kind_of(s)])
            put(s, pick(fin, s)[...].astype(f32))

    @pl.when(is_hub)
    def _():
        def turn(ref, which, p, size):
            tall = ref[which, span(p, size)].astype(f32).T.astype(bf16)
            return tall.reshape(2, size // 2, rows)

        def stack(ref, which, positions):
            return jnp.concatenate([ref[p, which] for p in positions], axis=0)

        def own_rows(s, which, positions):
            if s < last:
                return dot_nn(stack(h_t, which, positions), x[s, mine])
            if s == last:
                return dot_nn(stack(lat_t, which, [shard(p) for p in positions]), hidden[mine, :])
            return dot_nn(stack(x_t, which, positions), lg[mine, :])

        def their_rows(s, which, positions):
            if s < last:
                return dot_nn(stack(h_u, which, positions), x[s, theirs])
            if s == last:
                return dot_nn(stack(lat_u, which, [shard(p) for p in positions]), hidden[theirs, :])
            return dot_nn(stack(x_u, which, positions), lg[theirs, :])

        def put_terms(s, positions, to_other, to_own):
            shape = pick(own, s).shape[1:]
            for i, p in enumerate(positions):
                these = slice(i * shape[0], (i + 1) * shape[0])
                pick(away, s)[p] = to_other[these].astype(bf16)
                core_copy(s, p).start()
            for i, p in enumerate(positions):
                these = slice(i * shape[0], (i + 1) * shape[0])
                pick(own, s)[p] = to_own[these]

        def terms(s, positions):
            first = own_rows(s, other_core, positions) + their_rows(s, other_core, positions)
            put_terms(
                s, positions, first, own_rows(s, core, positions) + their_rows(s, core, positions)
            )

        def far_terms(s, positions):
            size = len(positions) * ob
            held = slice(positions[0], positions[0] + len(positions))
            first = far_acc[s, held].reshape(size, far_acc.shape[3])
            second = own_b[s, held].reshape(size, far_acc.shape[3])
            put_terms(
                s, positions, first + their_rows(s, other_core, positions),
                second + their_rows(s, core, positions),
            )

        def pair(s, p):
            return pick(own, s)[p] + pick(cored, s)[p].astype(f32)

        def core_here(s, p):
            both = pl.ds(0, 2)
            if p > 1:
                view = pick(cored, s).at[pl.ds(2, 2)] if s >= last else core_b.at[:, pl.ds(2, 2)]
            else:
                view = pick(cored, s).at[p if s == 0 else both]
            arrived(view, core_recv.at[core_slot(s, p)])

        def send_far(s, p):
            pick(far, s)[p] = pair(s, p).astype(bf16)
            mid_copy(s, p).start()

        for p in range(2):
            h_t[p] = turn(hidden, mine, p, 2 * ob)
        for s in range(last):
            shape = (2, ob, far_acc.shape[3])
            far_acc[s] = own_rows(s, other_core, range(2)).reshape(shape)
            own_b[s, 0:2] = own_rows(s, core, range(2)).reshape(shape)
        for p in range(2):
            arrived(up_views[3 + p], up_sem.at[3 + p])
            h_u[p] = turn(hidden, theirs, p, 2 * ob)
            far_terms(0, [p])
        for p in range(2):
            core_here(0, p)
            send_far(0, p)
        arrived(x.at[pl.ds(1, levels), theirs], side_recv)
        for bit in range(levels):
            far_terms(bit + 1, [0, 1])
        for t in range(1, levels):
            lg_step(t)
        send_back()
        for s in range(1, last):
            core_here(s, 0)
            send_far(s, 0)
        for s in range(1, levels):
            send_far(s, 1)
        arrived(up_views[1], up_sem.at[1])
        lat_t[...] = lat[mine, :].astype(f32).T.astype(bf16).reshape(lat_t.shape)
        lat_u[...] = lat[theirs, :].astype(f32).T.astype(bf16).reshape(lat_t.shape)
        arrived(up_views[5], up_sem.at[5])
        terms(last, range(2))
        for p in range(2, chips):
            h_t[p] = turn(hidden, mine, p, 2 * ob)
            h_u[p] = turn(hidden, theirs, p, 2 * ob)
        for s in range(last):
            terms(s, range(2, chips))
        terms(last, range(2, chips))
        core_here(last, 0)
        send_far(last, 0)
        for p in range(chips):
            x_t[p] = turn(x.at[0], mine, p, 2 * ib)
            x_u[p] = turn(x.at[0], theirs, p, 2 * ib)
        lg_step(levels)
        arrived(up_views[2], up_sem.at[2])
        terms(last + 1, range(2))
        core_here(last + 1, 0)
        send_far(last + 1, 0)
        for s in range(levels, last + 2):
            send_far(s, 1)
        terms(last + 1, range(2, chips))

        def send_end(s):
            arrived(pick(near, s).at[0], mid_recv.at[mid_slot(s, 0)])
            pick(ended, s)[...] = (pair(s, 2) + pick(near, s)[0].astype(f32)).astype(bf16)
            end_copy(s).start()

        def keep(s):
            put(s, pair(s, 3) + pick(near, s)[1].astype(f32))

        core_here(0, 2)
        for s in range(last):
            send_end(s)
        back_ready()
        sent()
        left_here(x.at[pl.ds(1, levels), theirs], side_send)
        for s in (0, last, last + 1):
            left_here(away[kind_of(s)], core_send.at[kind_of(s)])
        for s in (last, last + 1):
            core_here(s, 2)
            send_end(s)
        arrived(near_b.at[:, 1], mid_recv.at[mid_slot(0, 1)])
        for s in range(last):
            keep(s)
        for s in (last, last + 1):
            arrived(pick(near, s).at[1], mid_recv.at[mid_slot(s, 1)])
            keep(s)
        for i in range(3):
            left_here(far[i], mid_send.at[i])
            left_here(ended[i], end_sem.at[i])


def hand_over(*refs):
    copies = [pltpu.make_async_copy(refs[i], refs[5 + i], refs[10].at[i]) for i in range(5)]
    for copy in copies:
        copy.start()
    for copy in copies:
        copy.wait()


def shards(inputs, block_weights, low_left, low_right, out_grad):
    n_dp, n_width = lax.axis_size("dp"), lax.axis_size("width")
    levels = n_width.bit_length() - 1
    rows, _, width_in = inputs.shape
    width_out = block_weights.shape[1]
    rank = low_left.shape[2]
    ob, ib, rb = width_out // n_dp, width_in // n_dp, rank // n_dp
    fits = n_dp == 2 * chips_in_line and rows % (16 * n_width) == 0 and rows % 32 == 0 and width_in == width_out
    if not fits or ob % 64 or ib % 64 or rb % 16 or levels < 1 or rows % (16 * levels) or rank % 128:
        return plain_shards(inputs, block_weights, low_left, low_right, out_grad)
    chips = n_dp // 2
    scale = 1.0 / math.sqrt(rows * n_dp)
    vm, dma = pltpu.VMEM, pltpu.SemaphoreType.DMA

    def line_scratch(lead, r, c):
        return [
            vm((*lead, chips, r, c), bf16),
            vm((*lead, chips, r, c), f32),
            vm((*lead, chips, r, c), bf16),
            vm((*lead, 2, r, c), bf16),
            vm((*lead, 2, r, c), bf16),
            vm((*lead, r, c), bf16),
            vm((*lead, r, c), bf16),
        ]

    outs = pl.pallas_call(
        functools.partial(step_kernel, n_dp, n_width, scale),
        out_shape=(
            jax.ShapeDtypeStruct((rows, width_out), bf16),
            jax.ShapeDtypeStruct((rows, width_in), bf16),
            jax.ShapeDtypeStruct((levels + 1, ob, width_in), f32),
            jax.ShapeDtypeStruct((ib, rank), f32),
            jax.ShapeDtypeStruct((rb, width_out), f32),
        ),
        in_specs=[pl.BlockSpec(memory_space=pltpu.HBM)] * 5,
        out_specs=(pl.BlockSpec(memory_space=pltpu.VMEM),) * 5,
        scratch_shapes=[
            vm((levels + 1, 2 * rows, width_in), bf16),
            vm((levels + 1, width_out, width_in), bf16),
            vm((width_in, rank), bf16),
            vm((rank, width_out), bf16),
            vm((rows, width_out), bf16),
            vm((rows, rank), f32),
            vm((levels, rows, rank), bf16),
            vm((levels, rows, rank), bf16),
            vm((2 * rows, rank), bf16),
            vm((levels, rows, rank), bf16),
            vm((levels, rows, rank), bf16),
            vm((2 * rows, rank), bf16),
            vm((2 * rows, width_out), bf16),
            vm((chips, 2, ib, rows), bf16),
            vm((chips, 2, ib, rows), bf16),
            vm((chips, 2, ob, rows), bf16),
            vm((chips, 2, ob, rows), bf16),
            vm((chips, 2, rb, rows), bf16),
            vm((chips, 2, rb, rows), bf16),
            vm((levels + 1, 2, ob, width_in), f32),
            vm((levels, rows, width_in), bf16),
            vm((levels, rows, width_in), bf16),
            vm((rows, width_out), f32),
            *line_scratch((levels + 1,), ob, width_in),
            *line_scratch((), rb, width_out),
            *line_scratch((), ib, rank),
            dma((5,)),
            dma,
            dma((levels,)),
            dma,
            dma((2 * levels - 1,)),
            dma,
            dma((levels,)),
            dma,
            dma,
            dma((6,)),
            dma,
            dma,
            dma((3,)),
            dma((levels + 7,)),
            dma((3,)),
            dma((levels + 6,)),
            dma((3,)),
        ],
        compiler_params=pltpu.CompilerParams(
            collective_id=0, has_side_effects=True, vmem_limit_bytes=40 * 1024 * 1024
        ),
    )(
        *(
            pltpu.with_memory_space_constraint(array, pltpu.HBM)
            for array in (
                inputs[:, 0],
                block_weights[0].transpose(1, 0, 2),
                low_left[0],
                low_right[0],
                out_grad[:, 0],
            )
        )
    )
    act, in_grad, block, left, right = pl.pallas_call(
        hand_over,
        out_shape=tuple(jax.ShapeDtypeStruct(out.shape, out.dtype) for out in outs),
        in_specs=[pl.BlockSpec(memory_space=pltpu.VMEM)] * 5,
        out_specs=(pl.BlockSpec(memory_space=pl.ANY),) * 5,
        scratch_shapes=[dma((5,))],
        compiler_params=pltpu.CompilerParams(vmem_limit_bytes=4 * 1024 * 1024),
    )(*outs)
    return (
        act[:, None],
        in_grad[:, None],
        block.transpose(1, 0, 2)[None],
        left[None],
        right[None],
    )


def solution(mesh):
    placed = (
        P("dp", "width", None),
        P("width", None, None, None),
        P("width", None, None),
        P("width", None, None),
        P("dp", "width", None),
    )
    return jax.shard_map(
        shards,
        mesh=mesh,
        in_specs=placed,
        out_specs=(
            P("dp", "width", None),
            P("dp", "width", None),
            P("width", "dp", None, None),
            P("width", "dp", None),
            P("width", "dp", None),
        ),
        check_vma=False,
    )
```

```python
import functools
import math

import jax
import jax.numpy as jnp
from jax import lax
from jax.experimental import pallas as pl
from jax.experimental.pallas import tpu as pltpu
from jax.sharding import PartitionSpec as P

root_half = 0.7071067811865476
inv_root_two_pi = 0.3989422804014327
chips_in_line = 4


def swapped(array, axis, apart):
    return lax.ppermute(array, axis, [(i, i ^ 1 << apart) for i in range(lax.axis_size(axis))])


def gelu_value(pre):
    return 0.5 * pre * (1.0 + lax.erf(pre * root_half))


def gelu_slope(pre):
    return (
        0.5 * (1.0 + lax.erf(pre * root_half)) + pre * jnp.exp(-0.5 * pre * pre) * inv_root_two_pi
    )


def plain_shards(inputs, block_weights, low_left, low_right, out_grad):
    own_x = inputs[:, 0]
    weights = block_weights[0]
    left = low_left[0]
    right = low_right[0]
    grad_out = out_grad[:, 0]
    levels = lax.axis_size("width").bit_length() - 1
    block_size = own_x.shape[1]
    scale = 1.0 / math.sqrt(own_x.shape[0] * lax.axis_size("dp"))
    pieces = [own_x]
    for bit in range(levels):
        pieces.append(swapped(own_x, "width", bit))
    all_x = jnp.stack(pieces, axis=1)
    latent = lax.psum(jnp.dot(own_x, left, preferred_element_type=jnp.float32), "width").astype(
        jnp.bfloat16
    )
    pre = lax.dot_general(
        all_x, weights, (((1, 2), (1, 2)), ((), ())), preferred_element_type=jnp.float32
    )
    pre = pre + jnp.dot(latent, right, preferred_element_type=jnp.float32)
    activations = gelu_value(pre).astype(jnp.bfloat16)
    hidden = (grad_out.astype(jnp.float32) * gelu_slope(pre)).astype(jnp.bfloat16)
    latent_term = lax.dot_general(
        hidden, right, (((1,), (1,)), ((), ())), preferred_element_type=jnp.float32
    )
    latent_grad = lax.psum(latent_term, "width").astype(jnp.bfloat16)
    partner_w = weights[:, 1:, :].reshape(weights.shape[0], levels * block_size)
    backs = jnp.dot(hidden, partner_w, preferred_element_type=jnp.float32).astype(jnp.bfloat16)
    returned = jnp.zeros(own_x.shape, jnp.float32)
    for bit in range(levels):
        piece = backs[:, bit * block_size : (bit + 1) * block_size]
        returned = returned + swapped(piece, "width", bit).astype(jnp.float32)
    own_back = jnp.dot(hidden, weights[:, 0, :], preferred_element_type=jnp.float32)
    own_back = own_back + lax.dot_general(
        latent_grad, left, (((1,), (1,)), ((), ())), preferred_element_type=jnp.float32
    )
    in_grad = (own_back + returned).astype(jnp.bfloat16)
    left_term = (
        lax.dot_general(
            own_x, latent_grad, (((0,), (0,)), ((), ())), preferred_element_type=jnp.float32
        )
        * scale
    )
    right_term = (
        lax.dot_general(
            latent, hidden, (((0,), (0,)), ((), ())), preferred_element_type=jnp.float32
        )
        * scale
    )
    block_term = (
        lax.dot_general(hidden, all_x, (((0,), (0,)), ((), ())), preferred_element_type=jnp.float32)
        * scale
    )
    block_grad, left_grad, right_grad = (
        lax.psum_scatter(block_term, "dp", scatter_dimension=0, tiled=True),
        lax.psum_scatter(left_term, "dp", scatter_dimension=0, tiled=True),
        lax.psum_scatter(right_term, "dp", scatter_dimension=0, tiled=True),
    )
    return (
        activations[:, None],
        in_grad[:, None],
        block_grad[None],
        left_grad[None],
        right_grad[None],
    )


f32 = jnp.float32
bf16 = jnp.bfloat16


def dot_nn(a, b):
    return jnp.dot(a, b, preferred_element_type=f32)


def dot_nt(a, b):
    return lax.dot_general(a, b, (((1,), (1,)), ((), ())), preferred_element_type=f32)


def remote(src, dst, send, recv, dp, width):
    return pltpu.make_async_remote_copy(
        src_ref=src,
        dst_ref=dst,
        send_sem=send,
        recv_sem=recv,
        device_id={"dp": dp, "width": width},
        device_id_type=pl.DeviceIdType.MESH,
    )


def step_kernel(
    n_dp, n_width, scale,
    x_hbm, w_hbm, left_hbm, right_hbm, g_hbm,
    act_out, in_out, block_out, left_out, right_out,
    x, w, left, right, g,
    lat_sum, lat_own, lat_got, lat, lg_own, lg_got, lg, hidden,
    x_t, x_u, h_t, h_u, lat_t, lat_u, far_acc,
    back_own, back_got, pre,
    away_b, own_b, core_b, far_b, near_b, end_b, fin_b,
    away_r, own_r, core_r, far_r, near_r, end_r, fin_r,
    away_l, own_l, core_l, far_l, near_l, end_l, fin_l,
    load_sem, x_send, x_recv, lat_send, lat_recv, lg_send, lg_recv, back_send, back_recv,
    up_sem, side_send, side_recv, core_send, core_recv, mid_send, mid_recv, end_sem,
    pace,
):
    levels = n_width.bit_length() - 1
    chips = n_dp // 2
    dp = lax.axis_index("dp")
    me = lax.axis_index("width")
    chip, core = dp // 2, dp % 2
    other_core = 1 - core
    twin = dp + 1 - 2 * core
    side = chip // 2
    outer = (chip + side) % 2
    is_end = outer == 0
    is_hub = outer == 1
    step = 2 - 4 * side
    hub_dp = dp + step
    end_dp = dp - step
    far_dp = dp + step

    def mate(k):
        at = me
        for bit in range(levels):
            if k >> bit & 1:
                at = at + (1 << bit) * (1 - 2 * ((me // (1 << bit)) % 2))
        return at

    def shard(p):
        first = (3, 2, 0, 1)[p]
        return first + side * (chips - 1 - 2 * first)

    barrier = pltpu.get_barrier_semaphore()

    def greet(to_dp, to_width):
        pl.semaphore_signal(
            barrier,
            inc=1,
            device_id={"dp": to_dp, "width": to_width},
            device_id_type=pl.DeviceIdType.MESH,
        )

    rows = x_hbm.shape[0]
    mine, theirs = pl.ds(0, rows), pl.ds(rows, rows)
    loads = [
        pltpu.make_async_copy(src, dst, load_sem.at[i])
        for i, (src, dst) in enumerate(
            (
                (x_hbm, x.at[0, mine]),
                (left_hbm, left),
                (w_hbm, w),
                (right_hbm, right),
                (g_hbm, g),
            )
        )
    ]
    for load in loads[:2]:
        load.start()
    for k in range(1, n_width):
        greet(dp, mate(k))
    greet(twin, me)

    @pl.when(chip > 0)
    def _():
        greet(dp - 2, me)

    @pl.when(chip < chips - 1)
    def _():
        greet(dp + 2, me)

    ends = jnp.where(chip == 0, 1, 0) + jnp.where(chip == chips - 1, 1, 0)
    loads[0].wait()
    loads[1].wait()
    for load in loads[2:]:
        load.start()
    lat_sum[...] = dot_nn(x[0, mine], left[...])
    pl.semaphore_wait(barrier, n_width + 2 - ends)

    cut = rows // levels
    lead = cut // 48 * 16
    parts = [pl.ds(j * cut, cut) for j in range(levels)]
    beyond = [pl.ds(rows + j * cut, cut) for j in range(levels)]

    def x_group(part, src, j):
        return [
            remote(
                src.at[part], x.at[bit + 1, part], x_send, x_recv.at[j], dp, mate(1 << bit)
            )
            for bit in range(levels)
        ]

    x_copies = [x_group(part, x.at[0], j) for j, part in enumerate(parts)]

    def exchange(sums, out, got, send, recv, t):
        copies = []
        for j, part in enumerate(parts):
            out[t, part] = sums[part].astype(bf16)
            copies.append(
                remote(
                    out.at[t, part], got.at[t, part], send, recv(t, j),
                    dp, mate(1 << (j + t) % levels),
                )
            )
        for copy in copies:
            copy.start()

    def arrived(ref, sem):
        remote(ref, ref, core_send.at[0], sem, twin, me).wait_recv()

    def left_here(ref, sem):
        remote(ref, ref, sem, core_recv.at[0], twin, me).wait_send()

    def keep_pace():
        pl.semaphore_signal(
            pace, inc=1, device_id={"dp": twin, "width": me}, device_id_type=pl.DeviceIdType.MESH
        )
        pl.semaphore_wait(pace, 1)

    def lat_sem(t, j):
        return lat_recv.at[t + (j if t == levels - 1 else 0)]

    def lg_sem(t, j):
        return lg_recv.at[t]

    up_x = remote(x_hbm, x.at[0, theirs], up_sem.at[0], up_sem.at[0], hub_dp, me)
    side_copies = [
        remote(
            x.at[0, theirs], x.at[bit + 1, theirs], side_send, side_recv, dp, mate(1 << bit)
        )
        for bit in range(levels)
    ]

    @pl.when(is_end)
    def _():
        up_x.start()

    exchange(lat_sum, lat_own, lat_got, lat_send, lat_sem, 0)
    keep_pace()
    for copy in x_copies[0]:
        copy.start()
    loads[2].wait()
    pre[...] = dot_nt(x[0, mine], w[0])
    for t in range(1, levels):
        arrived(lat_got.at[t - 1], lat_recv.at[t - 1])
        lat_sum[...] += lat_got[t - 1].astype(f32)
        exchange(lat_sum, lat_own, lat_got, lat_send, lat_sem, t)
        for copy in x_copies[t]:
            copy.start()
    loads[3].wait()
    loads[4].wait()

    ob, rb, ib = h_t.shape[2], lat_t.shape[2], x_t.shape[2]
    last = levels + 1

    def span(p, size):
        return pl.ds(pl.multiple_of(shard(p) * size, size), size)

    up_h = [
        [
            remote(
                hidden.at[part, span(p, 2 * ob)], hidden.at[away_part, span(p, 2 * ob)],
                up_sem.at[3 + min(p, 2)], up_sem.at[3 + min(p, 2)], hub_dp, me,
            )
            for p in range(chips)
        ]
        for part, away_part in zip(parts, beyond)
    ]
    up_lat = remote(lat.at[mine], lat.at[theirs], up_sem.at[1], up_sem.at[1], hub_dp, me)
    up_lg = remote(lg.at[mine], lg.at[theirs], up_sem.at[2], up_sem.at[2], hub_dp, me)
    up_views = [
        x.at[0, theirs], lat.at[theirs], lg.at[theirs],
        hidden.at[theirs, pl.ds(0, 2 * ob)], hidden.at[theirs, pl.ds(0, 2 * ob)],
        hidden.at[theirs, pl.ds(0, 2 * ob * (chips - 2))],
    ]

    def add_mates(j):
        arrived(x.at[pl.ds(1, levels), parts[j]], x_recv.at[j])
        v = pre[parts[j], :]
        for bit in range(levels):
            v = v + dot_nt(x[bit + 1, parts[j]], w[bit + 1])
        return v

    pre[parts[0], :] = add_mates(0)
    for j, part in enumerate(parts):
        arrived(lat_got.at[levels - 1, part], lat_sem(levels - 1, j))
        lat[part, :] = (lat_sum[part, :] + lat_got[levels - 1, part].astype(f32)).astype(bf16)
        pre[part, :] += dot_nn(lat[part, :], right[...])
        v = add_mates(j) if j > 0 else pre[part, :]
        half = 0.5 * (1.0 + lax.erf(v * root_half))
        act_out[part, :] = (v * half).astype(bf16)
        slope = half + v * jnp.exp(-0.5 * v * v) * inv_root_two_pi
        hidden[part, :] = (g[part, :].astype(f32) * slope).astype(bf16)

        @pl.when(is_end)
        def _():
            for p in range(2):
                up_h[j][p].start()
            if j == levels - 1:
                up_lat.start()

        if j == 0:

            @pl.when(is_hub)
            def _():
                arrived(up_views[0], up_sem.at[0])
                for copy in side_copies:
                    copy.start()


    lat_sum[...] = dot_nt(hidden[mine, :], right[...])
    exchange(lat_sum, lg_own, lg_got, lg_send, lg_sem, 0)

    def pick(kind, s):
        block, low_right, low_left = kind
        if s < last:
            return block.at[s]
        return low_right if s == last else low_left

    away = (away_b, away_r, away_l)
    own = (own_b, own_r, own_l)
    cored = (core_b, core_r, core_l)
    far = (far_b, far_r, far_l)
    near = (near_b, near_r, near_l)
    ended = (end_b, end_r, end_l)
    fin = (fin_b, fin_r, fin_l)
    segments = range(last + 2)

    def kind_of(s):
        return min(max(s - last + 1, 0), 2)

    def core_slot(s, p):
        if p > 1:
            return levels + 4 + kind_of(s)
        return p if s == 0 else s + 1

    def mid_slot(s, p):
        return s if p == 0 else levels + 3 + kind_of(s)

    def core_copy(s, p):
        return remote(
            pick(away, s).at[p], pick(cored, s).at[p],
            core_send.at[kind_of(s)], core_recv.at[core_slot(s, p)], twin, me,
        )

    def mid_copy(s, p):
        return remote(
            pick(far, s).at[p], pick(near, s).at[p],
            mid_send.at[kind_of(s)], mid_recv.at[mid_slot(s, p)], far_dp, me,
        )

    def end_copy(s):
        return remote(
            pick(ended, s), pick(fin, s), end_sem.at[kind_of(s)], end_sem.at[kind_of(s)],
            end_dp, me,
        )

    def put(s, total):
        if s < last:
            block_out[s] = total * scale
        elif s == last:
            right_out[...] = total * scale
        else:
            left_out[...] = total * scale

    back_copies = [
        remote(
            back_own.at[bit], back_got.at[bit], back_send, back_recv, dp, mate(1 << bit)
        )
        for bit in range(levels)
    ]

    def lg_step(t):
        arrived(lg_got.at[t - 1], lg_recv.at[t - 1])
        if t < levels:
            lat_sum[...] += lg_got[t - 1].astype(f32)
            exchange(lat_sum, lg_own, lg_got, lg_send, lg_sem, t)
        else:
            lg[mine, :] = (lat_sum[...] + lg_got[t - 1].astype(f32)).astype(bf16)

    def send_back():
        for bit in range(levels):
            back_own[bit] = dot_nn(hidden[mine, :], w[bit + 1]).astype(bf16)
            back_copies[bit].start()

    def back_ready():
        total = dot_nn(hidden[mine, :], w[0]) + dot_nt(lg[mine, :], left[...])
        arrived(back_got, back_recv)
        for bit in range(levels):
            total = total + back_got[bit].astype(f32)
        in_out[...] = total.astype(bf16)

    def sent():
        left_here(x.at[pl.ds(1, levels), mine], x_send)
        left_here(lat_own, lat_send)
        left_here(lg_own, lg_send)
        left_here(back_own, back_send)

    @pl.when(is_end)
    def _():
        for j in range(levels):
            for p in range(2, chips):
                up_h[j][p].start()
        for t in range(1, levels + 1):
            lg_step(t)
        up_lg.start()
        keep_pace()
        send_back()
        back_ready()
        sent()
        for i, view in enumerate(up_views):
            left_here(view, up_sem.at[i])
        arrived(fin_b, end_sem.at[0])
        for s in range(last):
            put(s, fin_b[s].astype(f32))
        for s in range(last, last + 2):
            arrived(pick(fin, s), end_sem.at[kind_of(s)])
            put(s, pick(fin, s)[...].astype(f32))

    @pl.when(is_hub)
    def _():
        def turn(ref, which, p, size):
            tall = ref[which, span(p, size)].astype(f32).T.astype(bf16)
            return tall.reshape(2, size // 2, rows)

        def stack(ref, which, positions):
            return jnp.concatenate([ref[p, which] for p in positions], axis=0)

        def own_rows(s, which, positions):
            if s < last:
                return dot_nn(stack(h_t, which, positions), x[s, mine])
            if s == last:
                return dot_nn(stack(lat_t, which, [shard(p) for p in positions]), hidden[mine, :])
            return dot_nn(stack(x_t, which, positions), lg[mine, :])

        def their_rows(s, which, positions):
            if s < last:
                return dot_nn(stack(h_u, which, positions), x[s, theirs])
            if s == last:
                return dot_nn(stack(lat_u, which, [shard(p) for p in positions]), hidden[theirs, :])
            return dot_nn(stack(x_u, which, positions), lg[theirs, :])

        def put_terms(s, positions, to_other, to_own):
            shape = pick(own, s).shape[1:]
            for i, p in enumerate(positions):
                these = slice(i * shape[0], (i + 1) * shape[0])
                pick(away, s)[p] = to_other[these].astype(bf16)
                core_copy(s, p).start()
            for i, p in enumerate(positions):
                these = slice(i * shape[0], (i + 1) * shape[0])
                pick(own, s)[p] = to_own[these]

        def terms(s, positions):
            first = own_rows(s, other_core, positions) + their_rows(s, other_core, positions)
            put_terms(
                s, positions, first, own_rows(s, core, positions) + their_rows(s, core, positions)
            )

        def far_terms(s, positions):
            size = len(positions) * ob
            held = slice(positions[0], positions[0] + len(positions))
            first = far_acc[s, held].reshape(size, far_acc.shape[3])
            second = own_b[s, held].reshape(size, far_acc.shape[3])
            put_terms(
                s, positions, first + their_rows(s, other_core, positions),
                second + their_rows(s, core, positions),
            )

        def pair(s, p):
            return pick(own, s)[p] + pick(cored, s)[p].astype(f32)

        def core_here(s, p):
            both = pl.ds(0, 2)
            if p > 1:
                view = pick(cored, s).at[pl.ds(2, 2)] if s >= last else core_b.at[:, pl.ds(2, 2)]
            else:
                view = pick(cored, s).at[p if s == 0 else both]
            arrived(view, core_recv.at[core_slot(s, p)])

        def send_far(s, p):
            pick(far, s)[p] = pair(s, p).astype(bf16)
            mid_copy(s, p).start()

        for p in range(2):
            h_t[p] = turn(hidden, mine, p, 2 * ob)
        for s in range(last):
            shape = (2, ob, far_acc.shape[3])
            far_acc[s] = own_rows(s, other_core, range(2)).reshape(shape)
            own_b[s, 0:2] = own_rows(s, core, range(2)).reshape(shape)
        for p in range(2):
            arrived(up_views[3 + p], up_sem.at[3 + p])
            h_u[p] = turn(hidden, theirs, p, 2 * ob)
            far_terms(0, [p])
        core_here(0, 0)
        send_far(0, 0)
        arrived(x.at[pl.ds(1, levels), theirs], side_recv)
        for bit in range(levels):
            far_terms(bit + 1, [0, 1])
        for t in range(1, levels):
            lg_step(t)
        send_back()
        for s in range(1, last):
            core_here(s, 0)
            send_far(s, 0)
        arrived(up_views[1], up_sem.at[1])
        lat_t[...] = lat[mine, :].astype(f32).T.astype(bf16).reshape(lat_t.shape)
        lat_u[...] = lat[theirs, :].astype(f32).T.astype(bf16).reshape(lat_t.shape)
        arrived(up_views[5], up_sem.at[5])
        terms(last, range(2))
        for p in range(2, chips):
            h_t[p] = turn(hidden, mine, p, 2 * ob)
            h_u[p] = turn(hidden, theirs, p, 2 * ob)
        for s in range(last):
            terms(s, range(2, chips))
        terms(last, range(2, chips))
        core_here(last, 0)
        send_far(last, 0)
        core_here(0, 1)
        send_far(0, 1)
        for p in range(chips):
            x_t[p] = turn(x.at[0], mine, p, 2 * ib)
            x_u[p] = turn(x.at[0], theirs, p, 2 * ib)
        lg_step(levels)
        own_first = own_rows(last + 1, other_core, range(chips))
        own_second = own_rows(last + 1, core, range(chips))

        def send_end(s):
            arrived(pick(near, s).at[0], mid_recv.at[mid_slot(s, 0)])
            pick(ended, s)[...] = (pair(s, 2) + pick(near, s)[0].astype(f32)).astype(bf16)
            end_copy(s).start()

        def keep(s):
            put(s, pair(s, 3) + pick(near, s)[1].astype(f32))

        core_here(0, 2)
        send_end(0)
        arrived(up_views[2], up_sem.at[2])
        put_terms(
            last + 1, range(chips), own_first + their_rows(last + 1, other_core, range(chips)),
            own_second + their_rows(last + 1, core, range(chips)),
        )
        send_end(1)
        core_here(last + 1, 0)
        send_far(last + 1, 0)
        for s in range(1, last + 2):
            send_far(s, 1)
        for s in range(2, last):
            send_end(s)
        back_ready()
        sent()
        left_here(x.at[pl.ds(1, levels), theirs], side_send)
        for s in (0, last, last + 1):
            left_here(away[kind_of(s)], core_send.at[kind_of(s)])
        for s in (last, last + 1):
            core_here(s, 2)
            send_end(s)
        arrived(near_b.at[:, 1], mid_recv.at[mid_slot(0, 1)])
        for s in range(last):
            keep(s)
        for s in (last, last + 1):
            arrived(pick(near, s).at[1], mid_recv.at[mid_slot(s, 1)])
            keep(s)
        for i in range(3):
            left_here(far[i], mid_send.at[i])
            left_here(ended[i], end_sem.at[i])


def hand_over(*refs):
    copies = [pltpu.make_async_copy(refs[i], refs[5 + i], refs[10].at[i]) for i in range(5)]
    for copy in copies:
        copy.start()
    for copy in copies:
        copy.wait()


def shards(inputs, block_weights, low_left, low_right, out_grad):
    n_dp, n_width = lax.axis_size("dp"), lax.axis_size("width")
    levels = n_width.bit_length() - 1
    rows, _, width_in = inputs.shape
    width_out = block_weights.shape[1]
    rank = low_left.shape[2]
    ob, ib, rb = width_out // n_dp, width_in // n_dp, rank // n_dp
    fits = n_dp == 2 * chips_in_line and rows % (16 * n_width) == 0 and rows % 32 == 0 and width_in == width_out
    if not fits or ob % 64 or ib % 64 or rb % 16 or levels < 1 or rows % (16 * levels) or rank % 128:
        return plain_shards(inputs, block_weights, low_left, low_right, out_grad)
    chips = n_dp // 2
    scale = 1.0 / math.sqrt(rows * n_dp)
    vm, dma = pltpu.VMEM, pltpu.SemaphoreType.DMA

    def line_scratch(lead, r, c):
        return [
            vm((*lead, chips, r, c), bf16),
            vm((*lead, chips, r, c), f32),
            vm((*lead, chips, r, c), bf16),
            vm((*lead, 2, r, c), bf16),
            vm((*lead, 2, r, c), bf16),
            vm((*lead, r, c), bf16),
            vm((*lead, r, c), bf16),
        ]

    outs = pl.pallas_call(
        functools.partial(step_kernel, n_dp, n_width, scale),
        out_shape=(
            jax.ShapeDtypeStruct((rows, width_out), bf16),
            jax.ShapeDtypeStruct((rows, width_in), bf16),
            jax.ShapeDtypeStruct((levels + 1, ob, width_in), f32),
            jax.ShapeDtypeStruct((ib, rank), f32),
            jax.ShapeDtypeStruct((rb, width_out), f32),
        ),
        in_specs=[pl.BlockSpec(memory_space=pltpu.HBM)] * 5,
        out_specs=(pl.BlockSpec(memory_space=pltpu.VMEM),) * 5,
        scratch_shapes=[
            vm((levels + 1, 2 * rows, width_in), bf16),
            vm((levels + 1, width_out, width_in), bf16),
            vm((width_in, rank), bf16),
            vm((rank, width_out), bf16),
            vm((rows, width_out), bf16),
            vm((rows, rank), f32),
            vm((levels, rows, rank), bf16),
            vm((levels, rows, rank), bf16),
            vm((2 * rows, rank), bf16),
            vm((levels, rows, rank), bf16),
            vm((levels, rows, rank), bf16),
            vm((2 * rows, rank), bf16),
            vm((2 * rows, width_out), bf16),
            vm((chips, 2, ib, rows), bf16),
            vm((chips, 2, ib, rows), bf16),
            vm((chips, 2, ob, rows), bf16),
            vm((chips, 2, ob, rows), bf16),
            vm((chips, 2, rb, rows), bf16),
            vm((chips, 2, rb, rows), bf16),
            vm((levels + 1, 2, ob, width_in), f32),
            vm((levels, rows, width_in), bf16),
            vm((levels, rows, width_in), bf16),
            vm((rows, width_out), f32),
            *line_scratch((levels + 1,), ob, width_in),
            *line_scratch((), rb, width_out),
            *line_scratch((), ib, rank),
            dma((5,)),
            dma,
            dma((levels,)),
            dma,
            dma((2 * levels - 1,)),
            dma,
            dma((levels,)),
            dma,
            dma,
            dma((6,)),
            dma,
            dma,
            dma((3,)),
            dma((levels + 7,)),
            dma((3,)),
            dma((levels + 6,)),
            dma((3,)),
            pltpu.SemaphoreType.REGULAR,
        ],
        compiler_params=pltpu.CompilerParams(
            collective_id=0, has_side_effects=True, vmem_limit_bytes=40 * 1024 * 1024
        ),
    )(
        *(
            pltpu.with_memory_space_constraint(array, pltpu.HBM)
            for array in (
                inputs[:, 0],
                block_weights[0].transpose(1, 0, 2),
                low_left[0],
                low_right[0],
                out_grad[:, 0],
            )
        )
    )
    act, in_grad, block, left, right = pl.pallas_call(
        hand_over,
        out_shape=tuple(jax.ShapeDtypeStruct(out.shape, out.dtype) for out in outs),
        in_specs=[pl.BlockSpec(memory_space=pltpu.VMEM)] * 5,
        out_specs=(pl.BlockSpec(memory_space=pl.ANY),) * 5,
        scratch_shapes=[dma((5,))],
        compiler_params=pltpu.CompilerParams(vmem_limit_bytes=4 * 1024 * 1024),
    )(*outs)
    return (
        act[:, None],
        in_grad[:, None],
        block.transpose(1, 0, 2)[None],
        left[None],
        right[None],
    )


def solution(mesh):
    placed = (
        P("dp", "width", None),
        P("width", None, None, None),
        P("width", None, None),
        P("width", None, None),
        P("dp", "width", None),
    )
    return jax.shard_map(
        shards,
        mesh=mesh,
        in_specs=placed,
        out_specs=(
            P("dp", "width", None),
            P("dp", "width", None),
            P("width", "dp", None, None),
            P("width", "dp", None),
            P("width", "dp", None),
        ),
        check_vma=False,
    )
```

```python
import functools
import math

import jax
import jax.numpy as jnp
from jax import lax
from jax.experimental import pallas as pl
from jax.experimental.pallas import tpu as pltpu
from jax.sharding import PartitionSpec as P

root_half = 0.7071067811865476
inv_root_two_pi = 0.3989422804014327
chips_in_line = 4


def swapped(array, axis, apart):
    return lax.ppermute(array, axis, [(i, i ^ 1 << apart) for i in range(lax.axis_size(axis))])


def gelu_value(pre):
    return 0.5 * pre * (1.0 + lax.erf(pre * root_half))


def gelu_slope(pre):
    return (
        0.5 * (1.0 + lax.erf(pre * root_half)) + pre * jnp.exp(-0.5 * pre * pre) * inv_root_two_pi
    )


def plain_shards(inputs, block_weights, low_left, low_right, out_grad):
    own_x = inputs[:, 0]
    weights = block_weights[0]
    left = low_left[0]
    right = low_right[0]
    grad_out = out_grad[:, 0]
    levels = lax.axis_size("width").bit_length() - 1
    block_size = own_x.shape[1]
    scale = 1.0 / math.sqrt(own_x.shape[0] * lax.axis_size("dp"))
    pieces = [own_x]
    for bit in range(levels):
        pieces.append(swapped(own_x, "width", bit))
    all_x = jnp.stack(pieces, axis=1)
    latent = lax.psum(jnp.dot(own_x, left, preferred_element_type=jnp.float32), "width").astype(
        jnp.bfloat16
    )
    pre = lax.dot_general(
        all_x, weights, (((1, 2), (1, 2)), ((), ())), preferred_element_type=jnp.float32
    )
    pre = pre + jnp.dot(latent, right, preferred_element_type=jnp.float32)
    activations = gelu_value(pre).astype(jnp.bfloat16)
    hidden = (grad_out.astype(jnp.float32) * gelu_slope(pre)).astype(jnp.bfloat16)
    latent_term = lax.dot_general(
        hidden, right, (((1,), (1,)), ((), ())), preferred_element_type=jnp.float32
    )
    latent_grad = lax.psum(latent_term, "width").astype(jnp.bfloat16)
    partner_w = weights[:, 1:, :].reshape(weights.shape[0], levels * block_size)
    backs = jnp.dot(hidden, partner_w, preferred_element_type=jnp.float32).astype(jnp.bfloat16)
    returned = jnp.zeros(own_x.shape, jnp.float32)
    for bit in range(levels):
        piece = backs[:, bit * block_size : (bit + 1) * block_size]
        returned = returned + swapped(piece, "width", bit).astype(jnp.float32)
    own_back = jnp.dot(hidden, weights[:, 0, :], preferred_element_type=jnp.float32)
    own_back = own_back + lax.dot_general(
        latent_grad, left, (((1,), (1,)), ((), ())), preferred_element_type=jnp.float32
    )
    in_grad = (own_back + returned).astype(jnp.bfloat16)
    left_term = (
        lax.dot_general(
            own_x, latent_grad, (((0,), (0,)), ((), ())), preferred_element_type=jnp.float32
        )
        * scale
    )
    right_term = (
        lax.dot_general(
            latent, hidden, (((0,), (0,)), ((), ())), preferred_element_type=jnp.float32
        )
        * scale
    )
    block_term = (
        lax.dot_general(hidden, all_x, (((0,), (0,)), ((), ())), preferred_element_type=jnp.float32)
        * scale
    )
    block_grad, left_grad, right_grad = (
        lax.psum_scatter(block_term, "dp", scatter_dimension=0, tiled=True),
        lax.psum_scatter(left_term, "dp", scatter_dimension=0, tiled=True),
        lax.psum_scatter(right_term, "dp", scatter_dimension=0, tiled=True),
    )
    return (
        activations[:, None],
        in_grad[:, None],
        block_grad[None],
        left_grad[None],
        right_grad[None],
    )


f32 = jnp.float32
bf16 = jnp.bfloat16


def dot_nn(a, b):
    return jnp.dot(a, b, preferred_element_type=f32)


def dot_nt(a, b):
    return lax.dot_general(a, b, (((1,), (1,)), ((), ())), preferred_element_type=f32)


def remote(src, dst, send, recv, dp, width):
    return pltpu.make_async_remote_copy(
        src_ref=src,
        dst_ref=dst,
        send_sem=send,
        recv_sem=recv,
        device_id={"dp": dp, "width": width},
        device_id_type=pl.DeviceIdType.MESH,
    )


def step_kernel(
    n_dp, n_width, scale,
    x_hbm, w_hbm, left_hbm, right_hbm, g_hbm,
    act_out, in_out, block_out, left_out, right_out,
    x, w, left, right, g,
    lat_sum, lat_own, lat_got, lat, lg_own, lg_got, lg, hidden,
    x_t, x_u, h_t, h_u, lat_t, lat_u, far_acc, x_far, h_far, h_v, h_w,
    back_own, back_got, pre,
    away_b, own_b, core_b, far_b, near_b, end_b, fin_b,
    away_r, own_r, core_r, far_r, near_r, end_r, fin_r,
    away_l, own_l, core_l, far_l, near_l, end_l, fin_l,
    load_sem, x_send, x_recv, lat_send, lat_recv, lg_send, lg_recv, back_send, back_recv,
    up_sem, side_send, side_recv, core_send, core_recv, mid_send, mid_recv, end_sem,
    pace, over_send, over_recv,
):
    levels = n_width.bit_length() - 1
    chips = n_dp // 2
    dp = lax.axis_index("dp")
    me = lax.axis_index("width")
    chip, core = dp // 2, dp % 2
    other_core = 1 - core
    twin = dp + 1 - 2 * core
    side = chip // 2
    outer = (chip + side) % 2
    is_end = outer == 0
    is_hub = outer == 1
    step = 2 - 4 * side
    hub_dp = dp + step
    end_dp = dp - step
    far_dp = dp + step

    def mate(k):
        at = me
        for bit in range(levels):
            if k >> bit & 1:
                at = at + (1 << bit) * (1 - 2 * ((me // (1 << bit)) % 2))
        return at

    def shard(p):
        first = (3, 2, 0, 1)[p]
        return first + side * (chips - 1 - 2 * first)

    barrier = pltpu.get_barrier_semaphore()

    def greet(to_dp, to_width):
        pl.semaphore_signal(
            barrier,
            inc=1,
            device_id={"dp": to_dp, "width": to_width},
            device_id_type=pl.DeviceIdType.MESH,
        )

    rows = x_hbm.shape[0]
    mine, theirs = pl.ds(0, rows), pl.ds(rows, rows)
    loads = [
        pltpu.make_async_copy(src, dst, load_sem.at[i])
        for i, (src, dst) in enumerate(
            (
                (x_hbm, x.at[0, mine]),
                (left_hbm, left),
                (w_hbm, w),
                (right_hbm, right),
                (g_hbm, g),
            )
        )
    ]
    for load in loads[:2]:
        load.start()
    for k in range(1, n_width):
        greet(dp, mate(k))
    greet(twin, me)

    @pl.when(chip > 0)
    def _():
        greet(dp - 2, me)

    @pl.when(chip < chips - 1)
    def _():
        greet(dp + 2, me)

    ends = jnp.where(chip == 0, 1, 0) + jnp.where(chip == chips - 1, 1, 0)
    loads[0].wait()
    loads[1].wait()
    for load in loads[2:]:
        load.start()
    lat_sum[...] = dot_nn(x[0, mine], left[...])
    pl.semaphore_wait(barrier, n_width + 2 - ends)

    cut = rows // levels
    lead = cut // 48 * 16
    parts = [pl.ds(j * cut, cut) for j in range(levels)]
    beyond = [pl.ds(rows + j * cut, cut) for j in range(levels)]

    def x_group(part, src, j):
        return [
            remote(
                src.at[part], x.at[bit + 1, part], x_send, x_recv.at[j], dp, mate(1 << bit)
            )
            for bit in range(levels)
        ]

    x_copies = [x_group(part, x.at[0], j) for j, part in enumerate(parts)]

    def exchange(sums, out, got, send, recv, t):
        copies = []
        for j, part in enumerate(parts):
            out[t, part] = sums[part].astype(bf16)
            copies.append(
                remote(
                    out.at[t, part], got.at[t, part], send, recv(t, j),
                    dp, mate(1 << (j + t) % levels),
                )
            )
        for copy in copies:
            copy.start()

    def arrived(ref, sem):
        remote(ref, ref, core_send.at[0], sem, twin, me).wait_recv()

    def left_here(ref, sem):
        remote(ref, ref, sem, core_recv.at[0], twin, me).wait_send()

    def keep_pace():
        pl.semaphore_signal(
            pace, inc=1, device_id={"dp": twin, "width": me}, device_id_type=pl.DeviceIdType.MESH
        )
        pl.semaphore_wait(pace, 1)

    def lat_sem(t, j):
        return lat_recv.at[t + (j if t == levels - 1 else 0)]

    def lg_sem(t, j):
        return lg_recv.at[t]

    up_x = remote(x_hbm, x.at[0, theirs], up_sem.at[0], up_sem.at[0], hub_dp, me)
    side_copies = [
        remote(
            x.at[0, theirs], x.at[bit + 1, theirs], side_send, side_recv, dp, mate(1 << bit)
        )
        for bit in range(levels)
    ]

    over_x = [
        remote(
            x.at[0, these], x_far.at[these], over_send.at[0], over_recv.at[0], far_dp, me
        )
        for these in (mine, theirs)
    ]

    @pl.when(is_end)
    def _():
        up_x.start()

    @pl.when(is_hub)
    def _():
        over_x[0].start()

    exchange(lat_sum, lat_own, lat_got, lat_send, lat_sem, 0)
    keep_pace()
    for copy in x_copies[0]:
        copy.start()
    loads[2].wait()
    pre[...] = dot_nt(x[0, mine], w[0])
    for t in range(1, levels):
        arrived(lat_got.at[t - 1], lat_recv.at[t - 1])
        lat_sum[...] += lat_got[t - 1].astype(f32)
        exchange(lat_sum, lat_own, lat_got, lat_send, lat_sem, t)
        for copy in x_copies[t]:
            copy.start()
    loads[3].wait()
    loads[4].wait()

    ob, rb, ib = h_t.shape[2], lat_t.shape[2], x_t.shape[2]
    last = levels + 1

    def span(p, size):
        return pl.ds(pl.multiple_of(shard(p) * size, size), size)

    up_h = [
        [
            remote(
                hidden.at[part, span(p, 2 * ob)], hidden.at[away_part, span(p, 2 * ob)],
                up_sem.at[3 + min(p, 2)], up_sem.at[3 + min(p, 2)], hub_dp, me,
            )
            for p in range(chips)
        ]
        for part, away_part in zip(parts, beyond)
    ]
    def over_h(these, p):
        return remote(
            hidden.at[these, span(p, 2 * ob)], h_far.at[these, pl.ds(2 * ob * p, 2 * ob)],
            over_send.at[1], over_recv.at[1], far_dp, me,
        )

    up_lat = remote(lat.at[mine], lat.at[theirs], up_sem.at[1], up_sem.at[1], hub_dp, me)
    up_lg = remote(lg.at[mine], lg.at[theirs], up_sem.at[2], up_sem.at[2], hub_dp, me)
    up_views = [
        x.at[0, theirs], lat.at[theirs], lg.at[theirs],
        hidden.at[theirs, pl.ds(0, 2 * ob)], hidden.at[theirs, pl.ds(0, 2 * ob)],
        hidden.at[theirs, pl.ds(0, 2 * ob * (chips - 2))],
    ]

    def add_mates(j):
        arrived(x.at[pl.ds(1, levels), parts[j]], x_recv.at[j])
        v = pre[parts[j], :]
        for bit in range(levels):
            v = v + dot_nt(x[bit + 1, parts[j]], w[bit + 1])
        return v

    pre[parts[0], :] = add_mates(0)
    for j, part in enumerate(parts):
        arrived(lat_got.at[levels - 1, part], lat_sem(levels - 1, j))
        lat[part, :] = (lat_sum[part, :] + lat_got[levels - 1, part].astype(f32)).astype(bf16)
        pre[part, :] += dot_nn(lat[part, :], right[...])
        v = add_mates(j) if j > 0 else pre[part, :]
        half = 0.5 * (1.0 + lax.erf(v * root_half))
        act_out[part, :] = (v * half).astype(bf16)
        slope = half + v * jnp.exp(-0.5 * v * v) * inv_root_two_pi
        hidden[part, :] = (g[part, :].astype(f32) * slope).astype(bf16)

        @pl.when(is_end)
        def _():
            for p in range(2):
                up_h[j][p].start()
            if j == levels - 1:
                up_lat.start()

        @pl.when(is_hub)
        def _():
            for p in range(2):
                over_h(part, p).start()

        if j == 0:

            @pl.when(is_hub)
            def _():
                arrived(up_views[0], up_sem.at[0])
                over_x[1].start()
                for copy in side_copies:
                    copy.start()


    lat_sum[...] = dot_nt(hidden[mine, :], right[...])
    spread = [
        remote(lg_own.at[0], lg_got.at[k - 1], lg_send, lg_recv.at[0], dp, mate(k))
        for k in reversed(range(1, n_width))
    ]

    @pl.when(is_hub)
    def _():
        exchange(lat_sum, lg_own, lg_got, lg_send, lg_sem, 0)

    @pl.when(is_end)
    def _():
        lg_own[0] = lat_sum[...].astype(bf16)
        for copy in spread:
            copy.start()


    def pick(kind, s):
        block, low_right, low_left = kind
        if s < last:
            return block.at[s]
        return low_right if s == last else low_left

    away = (away_b, away_r, away_l)
    own = (own_b, own_r, own_l)
    cored = (core_b, core_r, core_l)
    far = (far_b, far_r, far_l)
    near = (near_b, near_r, near_l)
    ended = (end_b, end_r, end_l)
    fin = (fin_b, fin_r, fin_l)
    segments = range(last + 2)

    def kind_of(s):
        return min(max(s - last + 1, 0), 2)

    def core_slot(s, p):
        return s - 1 if p < 2 else levels + 2 + kind_of(s)

    def mid_slot(s, p):
        return s - 1 if p == 0 else levels + 2 + kind_of(s)

    def core_copy(s, p):
        return remote(
            pick(away, s).at[p], pick(cored, s).at[p],
            core_send.at[kind_of(s) if s else 3], core_recv.at[core_slot(s, p)], twin, me,
        )

    def mid_copy(s, p):
        return remote(
            pick(far, s).at[p], pick(near, s).at[p],
            mid_send.at[kind_of(s)], mid_recv.at[mid_slot(s, p)], far_dp, me,
        )

    def end_copy(s):
        return remote(
            pick(ended, s), pick(fin, s), end_sem.at[kind_of(s)], end_sem.at[kind_of(s)],
            end_dp, me,
        )

    def put(s, total):
        if s < last:
            block_out[s] = total * scale
        elif s == last:
            right_out[...] = total * scale
        else:
            left_out[...] = total * scale

    back_copies = [
        remote(
            back_own.at[bit], back_got.at[bit], back_send, back_recv, dp, mate(1 << bit)
        )
        for bit in range(levels)
    ]

    def lg_step(t):
        arrived(lg_got.at[t - 1], lg_recv.at[t - 1])
        if t < levels:
            lat_sum[...] += lg_got[t - 1].astype(f32)
            exchange(lat_sum, lg_own, lg_got, lg_send, lg_sem, t)
        else:
            lg[mine, :] = (lat_sum[...] + lg_got[t - 1].astype(f32)).astype(bf16)

    def send_back():
        for bit in range(levels):
            back_own[bit] = dot_nn(hidden[mine, :], w[bit + 1]).astype(bf16)
            back_copies[bit].start()

    def back_ready():
        total = dot_nn(hidden[mine, :], w[0]) + dot_nt(lg[mine, :], left[...])
        arrived(back_got, back_recv)
        for bit in range(levels):
            total = total + back_got[bit].astype(f32)
        in_out[...] = total.astype(bf16)

    def sent():
        left_here(x.at[pl.ds(1, levels), mine], x_send)
        left_here(lat_own, lat_send)
        left_here(back_own, back_send)

    @pl.when(is_end)
    def _():
        for j in range(levels):
            for p in range(2, chips):
                up_h[j][p].start()
        arrived(lg_got, lg_recv.at[0])
        total = lat_sum[...]
        for k in range(n_width - 1):
            total = total + lg_got[k].astype(f32)
        lg[mine, :] = total.astype(bf16)
        up_lg.start()
        keep_pace()
        send_back()
        back_ready()
        sent()
        left_here(lg_got, lg_send)
        for i, view in enumerate(up_views):
            left_here(view, up_sem.at[i])
        arrived(fin_b, end_sem.at[0])
        for s in range(last):
            put(s, fin_b[s].astype(f32))
        for s in range(last, last + 2):
            arrived(pick(fin, s), end_sem.at[kind_of(s)])
            put(s, pick(fin, s)[...].astype(f32))

    @pl.when(is_hub)
    def _():
        def turn(ref, which, p, size):
            tall = ref[which, span(p, size)].astype(f32).T.astype(bf16)
            return tall.reshape(2, size // 2, rows)

        def stack(ref, which, positions):
            return jnp.concatenate([ref[p, which] for p in positions], axis=0)

        def own_rows(s, which, positions):
            if s < last:
                return dot_nn(stack(h_t, which, positions), x[s, mine])
            if s == last:
                return dot_nn(stack(lat_t, which, [shard(p) for p in positions]), hidden[mine, :])
            return dot_nn(stack(x_t, which, positions), lg[mine, :])

        def their_rows(s, which, positions):
            if s < last:
                return dot_nn(stack(h_u, which, positions), x[s, theirs])
            if s == last:
                return dot_nn(stack(lat_u, which, [shard(p) for p in positions]), hidden[theirs, :])
            return dot_nn(stack(x_u, which, positions), lg[theirs, :])

        def put_terms(s, positions, to_other, to_own):
            shape = pick(own, s).shape[1:]
            for i, p in enumerate(positions):
                these = slice(i * shape[0], (i + 1) * shape[0])
                pick(away, s)[p] = to_other[these].astype(bf16)
                core_copy(s, p).start()
            for i, p in enumerate(positions):
                these = slice(i * shape[0], (i + 1) * shape[0])
                pick(own, s)[p] = to_own[these]

        def terms(s, positions):
            first = own_rows(s, other_core, positions) + their_rows(s, other_core, positions)
            put_terms(
                s, positions, first, own_rows(s, core, positions) + their_rows(s, core, positions)
            )

        def far_terms(s, positions):
            size = len(positions) * ob
            held = slice(positions[0], positions[0] + len(positions))
            first = far_acc[s, held].reshape(size, far_acc.shape[3])
            second = own_b[s, held].reshape(size, far_acc.shape[3])
            put_terms(
                s, positions, first + their_rows(s, other_core, positions),
                second + their_rows(s, core, positions),
            )

        def pair(s, p):
            return pick(own, s)[p] + pick(cored, s)[p].astype(f32)

        def core_here(s, p):
            both = pl.ds(0, 2)
            if p > 1:
                view = pick(cored, s).at[pl.ds(2, 2)] if s >= last else core_b.at[:, pl.ds(2, 2)]
            else:
                view = pick(cored, s).at[both]
            arrived(view, core_recv.at[core_slot(s, p)])

        def send_far(s, p):
            pick(far, s)[p] = pair(s, p).astype(bf16)
            mid_copy(s, p).start()

        for p in range(2):
            h_t[p] = turn(hidden, mine, p, 2 * ob)
        for s in range(1, last):
            shape = (2, ob, far_acc.shape[3])
            far_acc[s] = own_rows(s, other_core, range(2)).reshape(shape)
            own_b[s, 0:2] = own_rows(s, core, range(2)).reshape(shape)
        for p in range(2):
            arrived(up_views[3 + p], up_sem.at[3 + p])
            over_h(theirs, p).start()
            h_u[p] = turn(hidden, theirs, p, 2 * ob)
        arrived(x.at[pl.ds(1, levels), theirs], side_recv)
        for bit in range(levels):
            far_terms(bit + 1, [0, 1])
        for t in range(1, levels):
            lg_step(t)
        send_back()
        for s in range(1, last):
            core_here(s, 0)
            send_far(s, 0)
        arrived(up_views[1], up_sem.at[1])
        lat_t[...] = lat[mine, :].astype(f32).T.astype(bf16).reshape(lat_t.shape)
        lat_u[...] = lat[theirs, :].astype(f32).T.astype(bf16).reshape(lat_t.shape)
        arrived(up_views[5], up_sem.at[5])
        terms(last, range(2))
        for p in range(2, chips):
            h_t[p] = turn(hidden, mine, p, 2 * ob)
            h_u[p] = turn(hidden, theirs, p, 2 * ob)
        for s in range(1, last):
            terms(s, range(2, chips))
        terms(last, range(2, chips))
        core_here(last, 0)
        send_far(last, 0)
        send_far(1, 1)
        arrived(x_far, over_recv.at[0])
        arrived(h_far, over_recv.at[1])
        for i in range(2):
            cols = pl.ds(2 * ob * i, 2 * ob)
            for these, ref in ((mine, h_v), (theirs, h_w)):
                ref[i] = h_far[these, cols].astype(f32).T.astype(bf16).reshape(2, ob, rows)

        def near_zero(which):
            total = own_rows(0, which, range(2, chips)) + their_rows(0, which, range(2, chips))
            total = total + dot_nn(stack(h_v, which, range(2)), x_far[mine, :])
            return total + dot_nn(stack(h_w, which, range(2)), x_far[theirs, :])

        put_terms(0, range(2, chips), near_zero(other_core), near_zero(core))
        for p in range(chips):
            x_t[p] = turn(x.at[0], mine, p, 2 * ib)
            x_u[p] = turn(x.at[0], theirs, p, 2 * ib)
        lg_step(levels)
        own_first = own_rows(last + 1, other_core, range(chips))
        own_second = own_rows(last + 1, core, range(chips))

        def send_end(s):
            total = pair(s, 2)
            if s > 0:
                arrived(pick(near, s).at[0], mid_recv.at[mid_slot(s, 0)])
                total = total + pick(near, s)[0].astype(f32)
            pick(ended, s)[...] = total.astype(bf16)
            end_copy(s).start()

        def keep(s):
            total = pair(s, 3)
            put(s, total + pick(near, s)[1].astype(f32) if s > 0 else total)

        core_here(0, 2)
        send_end(0)
        arrived(up_views[2], up_sem.at[2])
        put_terms(
            last + 1, range(chips), own_first + their_rows(last + 1, other_core, range(chips)),
            own_second + their_rows(last + 1, core, range(chips)),
        )
        send_end(1)
        core_here(last + 1, 0)
        send_far(last + 1, 0)
        for s in range(2, last + 2):
            send_far(s, 1)
        for s in range(2, last):
            send_end(s)
        back_ready()
        sent()
        left_here(lg_own, lg_send)
        left_here(x.at[pl.ds(1, levels), theirs], side_send)
        left_here(away_b.at[0, pl.ds(2, 2)], core_send.at[3])
        left_here(away_b.at[pl.ds(1, levels)], core_send.at[0])
        left_here(away_r, core_send.at[1])
        left_here(away_l, core_send.at[2])
        left_here(x_far, over_send.at[0])
        left_here(h_far, over_send.at[1])
        for s in (last, last + 1):
            core_here(s, 2)
            send_end(s)
        keep(0)
        arrived(near_b.at[pl.ds(1, levels), 1], mid_recv.at[mid_slot(1, 1)])
        for s in range(1, last):
            keep(s)
        for s in (last, last + 1):
            arrived(pick(near, s).at[1], mid_recv.at[mid_slot(s, 1)])
            keep(s)
        for i in range(3):
            left_here(far_b.at[pl.ds(1, levels)] if i == 0 else far[i], mid_send.at[i])
            left_here(ended[i], end_sem.at[i])


def hand_over(*refs):
    copies = [pltpu.make_async_copy(refs[i], refs[5 + i], refs[10].at[i]) for i in range(5)]
    for copy in copies:
        copy.start()
    for copy in copies:
        copy.wait()


def shards(inputs, block_weights, low_left, low_right, out_grad):
    n_dp, n_width = lax.axis_size("dp"), lax.axis_size("width")
    levels = n_width.bit_length() - 1
    rows, _, width_in = inputs.shape
    width_out = block_weights.shape[1]
    rank = low_left.shape[2]
    ob, ib, rb = width_out // n_dp, width_in // n_dp, rank // n_dp
    fits = n_dp == 2 * chips_in_line and rows % (16 * n_width) == 0 and rows % 32 == 0 and width_in == width_out
    if not fits or ob % 64 or ib % 64 or rb % 16 or levels < 1 or rows % (16 * levels) or rank % 128:
        return plain_shards(inputs, block_weights, low_left, low_right, out_grad)
    chips = n_dp // 2
    scale = 1.0 / math.sqrt(rows * n_dp)
    vm, dma = pltpu.VMEM, pltpu.SemaphoreType.DMA

    def line_scratch(lead, r, c):
        return [
            vm((*lead, chips, r, c), bf16),
            vm((*lead, chips, r, c), f32),
            vm((*lead, chips, r, c), bf16),
            vm((*lead, 2, r, c), bf16),
            vm((*lead, 2, r, c), bf16),
            vm((*lead, r, c), bf16),
            vm((*lead, r, c), bf16),
        ]

    outs = pl.pallas_call(
        functools.partial(step_kernel, n_dp, n_width, scale),
        out_shape=(
            jax.ShapeDtypeStruct((rows, width_out), bf16),
            jax.ShapeDtypeStruct((rows, width_in), bf16),
            jax.ShapeDtypeStruct((levels + 1, ob, width_in), f32),
            jax.ShapeDtypeStruct((ib, rank), f32),
            jax.ShapeDtypeStruct((rb, width_out), f32),
        ),
        in_specs=[pl.BlockSpec(memory_space=pltpu.HBM)] * 5,
        out_specs=(pl.BlockSpec(memory_space=pltpu.VMEM),) * 5,
        scratch_shapes=[
            vm((levels + 1, 2 * rows, width_in), bf16),
            vm((levels + 1, width_out, width_in), bf16),
            vm((width_in, rank), bf16),
            vm((rank, width_out), bf16),
            vm((rows, width_out), bf16),
            vm((rows, rank), f32),
            vm((levels, rows, rank), bf16),
            vm((levels, rows, rank), bf16),
            vm((2 * rows, rank), bf16),
            vm((levels, rows, rank), bf16),
            vm((n_width - 1, rows, rank), bf16),
            vm((2 * rows, rank), bf16),
            vm((2 * rows, width_out), bf16),
            vm((chips, 2, ib, rows), bf16),
            vm((chips, 2, ib, rows), bf16),
            vm((chips, 2, ob, rows), bf16),
            vm((chips, 2, ob, rows), bf16),
            vm((chips, 2, rb, rows), bf16),
            vm((chips, 2, rb, rows), bf16),
            vm((levels + 1, 2, ob, width_in), f32),
            vm((2 * rows, width_in), bf16),
            vm((2 * rows, 4 * ob), bf16),
            vm((2, 2, ob, rows), bf16),
            vm((2, 2, ob, rows), bf16),
            vm((levels, rows, width_in), bf16),
            vm((levels, rows, width_in), bf16),
            vm((rows, width_out), f32),
            *line_scratch((levels + 1,), ob, width_in),
            *line_scratch((), rb, width_out),
            *line_scratch((), ib, rank),
            dma((5,)),
            dma,
            dma((levels,)),
            dma,
            dma((2 * levels - 1,)),
            dma,
            dma((levels,)),
            dma,
            dma,
            dma((6,)),
            dma,
            dma,
            dma((4,)),
            dma((levels + 5,)),
            dma((3,)),
            dma((levels + 5,)),
            dma((3,)),
            pltpu.SemaphoreType.REGULAR,
            dma((2,)),
            dma((2,)),
        ],
        compiler_params=pltpu.CompilerParams(
            collective_id=0, has_side_effects=True, vmem_limit_bytes=40 * 1024 * 1024
        ),
    )(
        *(
            pltpu.with_memory_space_constraint(array, pltpu.HBM)
            for array in (
                inputs[:, 0],
                block_weights[0].transpose(1, 0, 2),
                low_left[0],
                low_right[0],
                out_grad[:, 0],
            )
        )
    )
    act, in_grad, block, left, right = pl.pallas_call(
        hand_over,
        out_shape=tuple(jax.ShapeDtypeStruct(out.shape, out.dtype) for out in outs),
        in_specs=[pl.BlockSpec(memory_space=pltpu.VMEM)] * 5,
        out_specs=(pl.BlockSpec(memory_space=pl.ANY),) * 5,
        scratch_shapes=[dma((5,))],
        compiler_params=pltpu.CompilerParams(vmem_limit_bytes=4 * 1024 * 1024),
    )(*outs)
    return (
        act[:, None],
        in_grad[:, None],
        block.transpose(1, 0, 2)[None],
        left[None],
        right[None],
    )


def solution(mesh):
    placed = (
        P("dp", "width", None),
        P("width", None, None, None),
        P("width", None, None),
        P("width", None, None),
        P("dp", "width", None),
    )
    return jax.shard_map(
        shards,
        mesh=mesh,
        in_specs=placed,
        out_specs=(
            P("dp", "width", None),
            P("dp", "width", None),
            P("width", "dp", None, None),
            P("width", "dp", None),
            P("width", "dp", None),
        ),
        check_vma=False,
    )
```

```python
import functools
import math

import jax
import jax.numpy as jnp
from jax import lax
from jax.experimental import pallas as pl
from jax.experimental.pallas import tpu as pltpu
from jax.sharding import PartitionSpec as P

root_half = 0.7071067811865476
inv_root_two_pi = 0.3989422804014327
chips_in_line = 4


def swapped(array, axis, apart):
    return lax.ppermute(array, axis, [(i, i ^ 1 << apart) for i in range(lax.axis_size(axis))])


def gelu_value(pre):
    return 0.5 * pre * (1.0 + lax.erf(pre * root_half))


def gelu_slope(pre):
    return (
        0.5 * (1.0 + lax.erf(pre * root_half)) + pre * jnp.exp(-0.5 * pre * pre) * inv_root_two_pi
    )


def plain_shards(inputs, block_weights, low_left, low_right, out_grad):
    own_x = inputs[:, 0]
    weights = block_weights[0]
    left = low_left[0]
    right = low_right[0]
    grad_out = out_grad[:, 0]
    levels = lax.axis_size("width").bit_length() - 1
    block_size = own_x.shape[1]
    scale = 1.0 / math.sqrt(own_x.shape[0] * lax.axis_size("dp"))
    pieces = [own_x]
    for bit in range(levels):
        pieces.append(swapped(own_x, "width", bit))
    all_x = jnp.stack(pieces, axis=1)
    latent = lax.psum(jnp.dot(own_x, left, preferred_element_type=jnp.float32), "width").astype(
        jnp.bfloat16
    )
    pre = lax.dot_general(
        all_x, weights, (((1, 2), (1, 2)), ((), ())), preferred_element_type=jnp.float32
    )
    pre = pre + jnp.dot(latent, right, preferred_element_type=jnp.float32)
    activations = gelu_value(pre).astype(jnp.bfloat16)
    hidden = (grad_out.astype(jnp.float32) * gelu_slope(pre)).astype(jnp.bfloat16)
    latent_term = lax.dot_general(
        hidden, right, (((1,), (1,)), ((), ())), preferred_element_type=jnp.float32
    )
    latent_grad = lax.psum(latent_term, "width").astype(jnp.bfloat16)
    partner_w = weights[:, 1:, :].reshape(weights.shape[0], levels * block_size)
    backs = jnp.dot(hidden, partner_w, preferred_element_type=jnp.float32).astype(jnp.bfloat16)
    returned = jnp.zeros(own_x.shape, jnp.float32)
    for bit in range(levels):
        piece = backs[:, bit * block_size : (bit + 1) * block_size]
        returned = returned + swapped(piece, "width", bit).astype(jnp.float32)
    own_back = jnp.dot(hidden, weights[:, 0, :], preferred_element_type=jnp.float32)
    own_back = own_back + lax.dot_general(
        latent_grad, left, (((1,), (1,)), ((), ())), preferred_element_type=jnp.float32
    )
    in_grad = (own_back + returned).astype(jnp.bfloat16)
    left_term = (
        lax.dot_general(
            own_x, latent_grad, (((0,), (0,)), ((), ())), preferred_element_type=jnp.float32
        )
        * scale
    )
    right_term = (
        lax.dot_general(
            latent, hidden, (((0,), (0,)), ((), ())), preferred_element_type=jnp.float32
        )
        * scale
    )
    block_term = (
        lax.dot_general(hidden, all_x, (((0,), (0,)), ((), ())), preferred_element_type=jnp.float32)
        * scale
    )
    block_grad, left_grad, right_grad = (
        lax.psum_scatter(block_term, "dp", scatter_dimension=0, tiled=True),
        lax.psum_scatter(left_term, "dp", scatter_dimension=0, tiled=True),
        lax.psum_scatter(right_term, "dp", scatter_dimension=0, tiled=True),
    )
    return (
        activations[:, None],
        in_grad[:, None],
        block_grad[None],
        left_grad[None],
        right_grad[None],
    )


f32 = jnp.float32
bf16 = jnp.bfloat16


def dot_nn(a, b):
    return jnp.dot(a, b, preferred_element_type=f32)


def dot_nt(a, b):
    return lax.dot_general(a, b, (((1,), (1,)), ((), ())), preferred_element_type=f32)


def remote(src, dst, send, recv, dp, width):
    return pltpu.make_async_remote_copy(
        src_ref=src,
        dst_ref=dst,
        send_sem=send,
        recv_sem=recv,
        device_id={"dp": dp, "width": width},
        device_id_type=pl.DeviceIdType.MESH,
    )


def step_kernel(
    n_dp, n_width, scale,
    x_hbm, w_hbm, left_hbm, right_hbm, g_hbm,
    act_out, in_out, block_out, left_out, right_out,
    x, w, left, right, g,
    lat_sum, lat_own, lat_got, lat, lg_own, lg_got, lg, hidden,
    x_t, x_u, h_t, h_u, lat_t, lat_u, far_acc, x_far, h_far, h_v, h_w,
    back_own, back_got, pre,
    away_b, own_b, core_b, far_b, near_b, end_b, fin_b,
    away_r, own_r, core_r, far_r, near_r, end_r, fin_r,
    away_l, own_l, core_l, far_l, near_l, end_l, fin_l,
    load_sem, x_send, x_recv, lat_send, lat_recv, lg_send, lg_recv, back_send, back_recv,
    up_sem, side_send, side_recv, core_send, core_recv, mid_send, mid_recv, end_sem,
    pace, over_send, over_recv,
):
    levels = n_width.bit_length() - 1
    chips = n_dp // 2
    dp = lax.axis_index("dp")
    me = lax.axis_index("width")
    chip, core = dp // 2, dp % 2
    other_core = 1 - core
    twin = dp + 1 - 2 * core
    side = chip // 2
    outer = (chip + side) % 2
    is_end = outer == 0
    is_hub = outer == 1
    step = 2 - 4 * side
    hub_dp = dp + step
    end_dp = dp - step
    far_dp = dp + step

    def mate(k):
        at = me
        for bit in range(levels):
            if k >> bit & 1:
                at = at + (1 << bit) * (1 - 2 * ((me // (1 << bit)) % 2))
        return at

    def shard(p):
        first = (3, 2, 0, 1)[p]
        return first + side * (chips - 1 - 2 * first)

    barrier = pltpu.get_barrier_semaphore()

    def greet(to_dp, to_width):
        pl.semaphore_signal(
            barrier,
            inc=1,
            device_id={"dp": to_dp, "width": to_width},
            device_id_type=pl.DeviceIdType.MESH,
        )

    rows = x_hbm.shape[0]
    mine, theirs = pl.ds(0, rows), pl.ds(rows, rows)
    loads = [
        pltpu.make_async_copy(src, dst, load_sem.at[i])
        for i, (src, dst) in enumerate(
            (
                (x_hbm, x.at[0, mine]),
                (left_hbm, left),
                (w_hbm, w),
                (right_hbm, right),
                (g_hbm, g),
            )
        )
    ]
    for load in loads[:2]:
        load.start()
    for k in range(1, n_width):
        greet(dp, mate(k))
    greet(twin, me)

    @pl.when(chip > 0)
    def _():
        greet(dp - 2, me)

    @pl.when(chip < chips - 1)
    def _():
        greet(dp + 2, me)

    ends = jnp.where(chip == 0, 1, 0) + jnp.where(chip == chips - 1, 1, 0)
    loads[0].wait()
    loads[1].wait()
    for load in loads[2:]:
        load.start()
    lat_sum[...] = dot_nn(x[0, mine], left[...])
    pl.semaphore_wait(barrier, n_width + 2 - ends)

    cut = rows // levels
    lead = cut // 48 * 16
    parts = [pl.ds(j * cut, cut) for j in range(levels)]
    beyond = [pl.ds(rows + j * cut, cut) for j in range(levels)]

    def x_group(part, src, j):
        return [
            remote(
                src.at[part], x.at[bit + 1, part], x_send, x_recv.at[j], dp, mate(1 << bit)
            )
            for bit in range(levels)
        ]

    x_copies = [x_group(part, x.at[0], j) for j, part in enumerate(parts)]

    def exchange(sums, out, got, send, recv, t):
        copies = []
        for j, part in enumerate(parts):
            out[t, part] = sums[part].astype(bf16)
            copies.append(
                remote(
                    out.at[t, part], got.at[t, part], send, recv(t, j),
                    dp, mate(1 << (j + t) % levels),
                )
            )
        for copy in copies:
            copy.start()

    def arrived(ref, sem):
        remote(ref, ref, core_send.at[0], sem, twin, me).wait_recv()

    def left_here(ref, sem):
        remote(ref, ref, sem, core_recv.at[0], twin, me).wait_send()

    def keep_pace():
        pl.semaphore_signal(
            pace, inc=1, device_id={"dp": twin, "width": me}, device_id_type=pl.DeviceIdType.MESH
        )
        pl.semaphore_wait(pace, 1)

    def lat_sem(t, j):
        return lat_recv.at[t + (j if t == levels - 1 else 0)]

    def lg_sem(t, j):
        return lg_recv.at[t]

    later, later_there = pl.ds(cut, rows - cut), pl.ds(rows + cut, rows - cut)
    up_x = [
        remote(x_hbm.at[part], x.at[0, there], up_sem.at[i], up_sem.at[i], hub_dp, me)
        for i, part, there in ((0, parts[0], beyond[0]), (6, later, later_there))
    ]
    side_copies = [
        remote(
            x.at[0, theirs], x.at[bit + 1, theirs], side_send, side_recv, dp, mate(1 << bit)
        )
        for bit in range(levels)
    ]

    over_x = [
        remote(
            x.at[0, these], x_far.at[these], over_send.at[0], over_recv.at[0], far_dp, me
        )
        for these in (mine, beyond[0], later_there)
    ]

    @pl.when(is_end)
    def _():
        for copy in up_x:
            copy.start()

    @pl.when(is_hub)
    def _():
        over_x[0].start()

    exchange(lat_sum, lat_own, lat_got, lat_send, lat_sem, 0)
    keep_pace()
    for copy in x_copies[0]:
        copy.start()
    loads[2].wait()
    pre[...] = dot_nt(x[0, mine], w[0])
    for t in range(1, levels):
        arrived(lat_got.at[t - 1], lat_recv.at[t - 1])
        lat_sum[...] += lat_got[t - 1].astype(f32)
        exchange(lat_sum, lat_own, lat_got, lat_send, lat_sem, t)
        for copy in x_copies[t]:
            copy.start()
    loads[3].wait()
    loads[4].wait()

    ob, rb, ib = h_t.shape[2], lat_t.shape[2], x_t.shape[2]
    last = levels + 1

    def span(p, size):
        return pl.ds(pl.multiple_of(shard(p) * size, size), size)

    up_h = [
        [
            remote(
                hidden.at[part, span(p, 2 * ob)], hidden.at[away_part, span(p, 2 * ob)],
                up_sem.at[3 + min(p, 2)], up_sem.at[3 + min(p, 2)], hub_dp, me,
            )
            for p in range(chips)
        ]
        for part, away_part in zip(parts, beyond)
    ]
    def over_h(these, p):
        return remote(
            hidden.at[these, span(p, 2 * ob)], h_far.at[these, pl.ds(2 * ob * p, 2 * ob)],
            over_send.at[1], over_recv.at[1], far_dp, me,
        )

    up_lat = [
        remote(lat.at[part], lat.at[away_part], up_sem.at[1], up_sem.at[1], hub_dp, me)
        for part, away_part in zip(parts, beyond)
    ]
    up_lg = remote(lg.at[mine], lg.at[theirs], up_sem.at[2], up_sem.at[2], hub_dp, me)
    up_views = [
        x.at[0, beyond[0]], lat.at[theirs], lg.at[theirs],
        hidden.at[theirs, pl.ds(0, 2 * ob)], hidden.at[theirs, pl.ds(0, 2 * ob)],
        hidden.at[theirs, pl.ds(0, 2 * ob * (chips - 2))], x.at[0, later_there],
    ]

    def add_mates(j):
        arrived(x.at[pl.ds(1, levels), parts[j]], x_recv.at[j])
        v = pre[parts[j], :]
        for bit in range(levels):
            v = v + dot_nt(x[bit + 1, parts[j]], w[bit + 1])
        return v

    pre[parts[0], :] = add_mates(0)

    @pl.when(is_hub)
    def _():
        arrived(up_views[0], up_sem.at[0])
        over_x[1].start()

    for j, part in enumerate(parts):
        arrived(lat_got.at[levels - 1, part], lat_sem(levels - 1, j))
        lat[part, :] = (lat_sum[part, :] + lat_got[levels - 1, part].astype(f32)).astype(bf16)

        @pl.when(is_end)
        def _():
            up_lat[j].start()

        pre[part, :] += dot_nn(lat[part, :], right[...])
        v = add_mates(j) if j > 0 else pre[part, :]
        half = 0.5 * (1.0 + lax.erf(v * root_half))
        act_out[part, :] = (v * half).astype(bf16)
        slope = half + v * jnp.exp(-0.5 * v * v) * inv_root_two_pi
        hidden[part, :] = (g[part, :].astype(f32) * slope).astype(bf16)

        @pl.when(is_end)
        def _():
            for p in range(2):
                up_h[j][p].start()

        @pl.when(is_hub)
        def _():
            for p in range(2):
                over_h(part, p).start()

        if j == 0:

            @pl.when(is_hub)
            def _():
                arrived(up_views[6], up_sem.at[6])
                over_x[2].start()
                for copy in side_copies:
                    copy.start()


    lat_sum[...] = dot_nt(hidden[mine, :], right[...])
    gathers = outer + core == 0

    @pl.when(outer + core > 0)
    def _():
        exchange(lat_sum, lg_own, lg_got, lg_send, lg_sem, 0)

    @pl.when(gathers)
    def _():
        lg_own[0] = lat_sum[...].astype(bf16)
        for at in range(n_width):

            @pl.when(me == at)
            def _():
                order = [k for k in (at, *reversed(range(1, n_width))) if k > 0]
                for k in dict.fromkeys(order):
                    remote(
                        lg_own.at[0], lg_got.at[k - 1], lg_send, lg_recv.at[0], dp, mate(k)
                    ).start()


    def pick(kind, s):
        block, low_right, low_left = kind
        if s < last:
            return block.at[s]
        return low_right if s == last else low_left

    away = (away_b, away_r, away_l)
    own = (own_b, own_r, own_l)
    cored = (core_b, core_r, core_l)
    far = (far_b, far_r, far_l)
    near = (near_b, near_r, near_l)
    ended = (end_b, end_r, end_l)
    fin = (fin_b, fin_r, fin_l)
    segments = range(last + 2)

    def kind_of(s):
        return min(max(s - last + 1, 0), 2)

    def core_slot(s, p):
        return s - 1 if p < 2 else levels + 2 + kind_of(s)

    def mid_slot(s, p):
        return s - 1 if p == 0 else levels + 2 + kind_of(s)

    def core_copy(s, p):
        return remote(
            pick(away, s).at[p], pick(cored, s).at[p],
            core_send.at[kind_of(s) if s else 3], core_recv.at[core_slot(s, p)], twin, me,
        )

    def mid_copy(s, p):
        return remote(
            pick(far, s).at[p], pick(near, s).at[p],
            mid_send.at[kind_of(s)], mid_recv.at[mid_slot(s, p)], far_dp, me,
        )

    def end_copy(s):
        return remote(
            pick(ended, s), pick(fin, s), end_sem.at[kind_of(s)], end_sem.at[kind_of(s)],
            end_dp, me,
        )

    def put(s, total):
        if s < last:
            block_out[s] = total * scale
        elif s == last:
            right_out[...] = total * scale
        else:
            left_out[...] = total * scale

    back_copies = [
        remote(
            back_own.at[bit], back_got.at[bit], back_send, back_recv, dp, mate(1 << bit)
        )
        for bit in range(levels)
    ]

    def lg_step(t):
        arrived(lg_got.at[t - 1], lg_recv.at[t - 1])
        if t < levels:
            lat_sum[...] += lg_got[t - 1].astype(f32)
            exchange(lat_sum, lg_own, lg_got, lg_send, lg_sem, t)
        else:
            lg[mine, :] = (lat_sum[...] + lg_got[t - 1].astype(f32)).astype(bf16)

    def send_back():
        for bit in range(levels):
            back_own[bit] = dot_nn(hidden[mine, :], w[bit + 1]).astype(bf16)
            back_copies[bit].start()

    def back_ready():
        total = dot_nn(hidden[mine, :], w[0]) + dot_nt(lg[mine, :], left[...])
        arrived(back_got, back_recv)
        for bit in range(levels):
            total = total + back_got[bit].astype(f32)
        in_out[...] = total.astype(bf16)

    def sent():
        left_here(x.at[pl.ds(1, levels), mine], x_send)
        left_here(lat_own, lat_send)
        left_here(back_own, back_send)

    @pl.when(is_end)
    def _():
        def send_near():
            for j in range(levels):
                for p in range(2, chips):
                    up_h[j][p].start()

        @pl.when(gathers)
        def _():
            send_near()
            arrived(lg_got, lg_recv.at[0])
            total = lat_sum[...]
            for k in range(n_width - 1):
                total = total + lg_got[k].astype(f32)
            lg[mine, :] = total.astype(bf16)

        @pl.when(outer + core > 0)
        def _():
            for t in range(1, levels + 1):
                lg_step(t)
                if t == 1:
                    send_near()

        up_lg.start()
        keep_pace()
        send_back()
        back_ready()
        sent()

        @pl.when(gathers)
        def _():
            left_here(lg_got, lg_send)

        @pl.when(outer + core > 0)
        def _():
            left_here(lg_own, lg_send)

        for i, view in enumerate(up_views):
            left_here(view, up_sem.at[i])
        arrived(fin_b, end_sem.at[0])
        for s in range(last):
            put(s, fin_b[s].astype(f32))
        for s in range(last, last + 2):
            arrived(pick(fin, s), end_sem.at[kind_of(s)])
            put(s, pick(fin, s)[...].astype(f32))

    @pl.when(is_hub)
    def _():
        def turn(ref, which, p, size):
            tall = ref[which, span(p, size)].astype(f32).T.astype(bf16)
            return tall.reshape(2, size // 2, rows)

        def stack(ref, which, positions):
            return jnp.concatenate([ref[p, which] for p in positions], axis=0)

        def own_rows(s, which, positions):
            if s < last:
                return dot_nn(stack(h_t, which, positions), x[s, mine])
            if s == last:
                return dot_nn(stack(lat_t, which, [shard(p) for p in positions]), hidden[mine, :])
            return dot_nn(stack(x_t, which, positions), lg[mine, :])

        def their_rows(s, which, positions):
            if s < last:
                return dot_nn(stack(h_u, which, positions), x[s, theirs])
            if s == last:
                return dot_nn(stack(lat_u, which, [shard(p) for p in positions]), hidden[theirs, :])
            return dot_nn(stack(x_u, which, positions), lg[theirs, :])

        def put_terms(s, positions, to_other, to_own):
            shape = pick(own, s).shape[1:]
            for i, p in enumerate(positions):
                these = slice(i * shape[0], (i + 1) * shape[0])
                pick(away, s)[p] = to_other[these].astype(bf16)
                core_copy(s, p).start()
            for i, p in enumerate(positions):
                these = slice(i * shape[0], (i + 1) * shape[0])
                pick(own, s)[p] = to_own[these]

        def terms(s, positions):
            first = own_rows(s, other_core, positions) + their_rows(s, other_core, positions)
            put_terms(
                s, positions, first, own_rows(s, core, positions) + their_rows(s, core, positions)
            )

        def far_terms(s, positions):
            size = len(positions) * ob
            held = slice(positions[0], positions[0] + len(positions))
            first = far_acc[s, held].reshape(size, far_acc.shape[3])
            second = own_b[s, held].reshape(size, far_acc.shape[3])
            put_terms(
                s, positions, first + their_rows(s, other_core, positions),
                second + their_rows(s, core, positions),
            )

        def pair(s, p):
            return pick(own, s)[p] + pick(cored, s)[p].astype(f32)

        def core_here(s, p):
            both = pl.ds(0, 2)
            if p > 1:
                view = pick(cored, s).at[pl.ds(2, 2)] if s >= last else core_b.at[:, pl.ds(2, 2)]
            else:
                view = pick(cored, s).at[both]
            arrived(view, core_recv.at[core_slot(s, p)])

        def send_far(s, p):
            pick(far, s)[p] = pair(s, p).astype(bf16)
            mid_copy(s, p).start()

        for p in range(2):
            h_t[p] = turn(hidden, mine, p, 2 * ob)
        for s in range(1, last):
            shape = (2, ob, far_acc.shape[3])
            far_acc[s] = own_rows(s, other_core, range(2)).reshape(shape)
            own_b[s, 0:2] = own_rows(s, core, range(2)).reshape(shape)
        for p in range(2):
            arrived(up_views[3 + p], up_sem.at[3 + p])
            over_h(theirs, p).start()
            h_u[p] = turn(hidden, theirs, p, 2 * ob)
        arrived(x.at[pl.ds(1, levels), theirs], side_recv)
        for bit in range(levels):
            far_terms(bit + 1, [0, 1])
        for t in range(1, levels):
            lg_step(t)
        send_back()
        for s in range(1, last):
            core_here(s, 0)
            send_far(s, 0)
        arrived(up_views[1], up_sem.at[1])
        lat_t[...] = lat[mine, :].astype(f32).T.astype(bf16).reshape(lat_t.shape)
        lat_u[...] = lat[theirs, :].astype(f32).T.astype(bf16).reshape(lat_t.shape)
        arrived(up_views[5], up_sem.at[5])
        terms(last, range(2))
        for p in range(2, chips):
            h_t[p] = turn(hidden, mine, p, 2 * ob)
            h_u[p] = turn(hidden, theirs, p, 2 * ob)
        for s in range(1, last):
            terms(s, range(2, chips))
        terms(last, range(2, chips))
        core_here(last, 0)
        send_far(last, 0)
        send_far(1, 1)
        arrived(x_far, over_recv.at[0])
        arrived(h_far, over_recv.at[1])
        for i in range(2):
            cols = pl.ds(2 * ob * i, 2 * ob)
            for these, ref in ((mine, h_v), (theirs, h_w)):
                ref[i] = h_far[these, cols].astype(f32).T.astype(bf16).reshape(2, ob, rows)

        def near_zero(which):
            total = own_rows(0, which, range(2, chips)) + their_rows(0, which, range(2, chips))
            total = total + dot_nn(stack(h_v, which, range(2)), x_far[mine, :])
            return total + dot_nn(stack(h_w, which, range(2)), x_far[theirs, :])

        put_terms(0, range(2, chips), near_zero(other_core), near_zero(core))
        for p in range(chips):
            x_t[p] = turn(x.at[0], mine, p, 2 * ib)
            x_u[p] = turn(x.at[0], theirs, p, 2 * ib)
        lg_step(levels)
        own_first = own_rows(last + 1, other_core, range(chips))
        own_second = own_rows(last + 1, core, range(chips))

        def send_end(s):
            total = pair(s, 2)
            if s > 0:
                arrived(pick(near, s).at[0], mid_recv.at[mid_slot(s, 0)])
                total = total + pick(near, s)[0].astype(f32)
            pick(ended, s)[...] = total.astype(bf16)
            end_copy(s).start()

        def keep(s):
            total = pair(s, 3)
            put(s, total + pick(near, s)[1].astype(f32) if s > 0 else total)

        core_here(0, 2)
        send_end(0)
        arrived(up_views[2], up_sem.at[2])
        for part in (range(2), range(2, chips)):
            held = slice(part[0] * ib, (part[-1] + 1) * ib)
            to_other = own_first[held] + their_rows(last + 1, other_core, part)
            for i, p in enumerate(part):
                away_l[p] = to_other[i * ib : (i + 1) * ib].astype(bf16)
                core_copy(last + 1, p).start()
        to_own = own_second + their_rows(last + 1, core, range(chips))
        for p in range(chips):
            own_l[p] = to_own[p * ib : (p + 1) * ib]
        send_end(1)
        core_here(last + 1, 0)
        send_far(last + 1, 0)
        for s in range(2, last + 2):
            send_far(s, 1)
        for s in range(2, last):
            send_end(s)
        back_ready()
        sent()
        left_here(lg_own, lg_send)
        left_here(x.at[pl.ds(1, levels), theirs], side_send)
        left_here(away_b.at[0, pl.ds(2, 2)], core_send.at[3])
        left_here(away_b.at[pl.ds(1, levels)], core_send.at[0])
        left_here(away_r, core_send.at[1])
        left_here(away_l, core_send.at[2])
        left_here(x_far, over_send.at[0])
        left_here(h_far, over_send.at[1])
        for s in (last, last + 1):
            core_here(s, 2)
            send_end(s)
        keep(0)
        arrived(near_b.at[pl.ds(1, levels), 1], mid_recv.at[mid_slot(1, 1)])
        for s in range(1, last):
            keep(s)
        for s in (last, last + 1):
            arrived(pick(near, s).at[1], mid_recv.at[mid_slot(s, 1)])
            keep(s)
        for i in range(3):
            left_here(far_b.at[pl.ds(1, levels)] if i == 0 else far[i], mid_send.at[i])
            left_here(ended[i], end_sem.at[i])


def hand_over(*refs):
    copies = [pltpu.make_async_copy(refs[i], refs[5 + i], refs[10].at[i]) for i in range(5)]
    for copy in copies:
        copy.start()
    for copy in copies:
        copy.wait()


def shards(inputs, block_weights, low_left, low_right, out_grad):
    n_dp, n_width = lax.axis_size("dp"), lax.axis_size("width")
    levels = n_width.bit_length() - 1
    rows, _, width_in = inputs.shape
    width_out = block_weights.shape[1]
    rank = low_left.shape[2]
    ob, ib, rb = width_out // n_dp, width_in // n_dp, rank // n_dp
    fits = n_dp == 2 * chips_in_line and rows % (16 * n_width) == 0 and rows % 32 == 0 and width_in == width_out
    if not fits or ob % 64 or ib % 64 or rb % 16 or levels < 2 or rows % (16 * levels) or rank % 128:
        return plain_shards(inputs, block_weights, low_left, low_right, out_grad)
    chips = n_dp // 2
    scale = 1.0 / math.sqrt(rows * n_dp)
    vm, dma = pltpu.VMEM, pltpu.SemaphoreType.DMA

    def line_scratch(lead, r, c):
        return [
            vm((*lead, chips, r, c), bf16),
            vm((*lead, chips, r, c), f32),
            vm((*lead, chips, r, c), bf16),
            vm((*lead, 2, r, c), bf16),
            vm((*lead, 2, r, c), bf16),
            vm((*lead, r, c), bf16),
            vm((*lead, r, c), bf16),
        ]

    outs = pl.pallas_call(
        functools.partial(step_kernel, n_dp, n_width, scale),
        out_shape=(
            jax.ShapeDtypeStruct((rows, width_out), bf16),
            jax.ShapeDtypeStruct((rows, width_in), bf16),
            jax.ShapeDtypeStruct((levels + 1, ob, width_in), f32),
            jax.ShapeDtypeStruct((ib, rank), f32),
            jax.ShapeDtypeStruct((rb, width_out), f32),
        ),
        in_specs=[pl.BlockSpec(memory_space=pltpu.HBM)] * 5,
        out_specs=(pl.BlockSpec(memory_space=pltpu.VMEM),) * 5,
        scratch_shapes=[
            vm((levels + 1, 2 * rows, width_in), bf16),
            vm((levels + 1, width_out, width_in), bf16),
            vm((width_in, rank), bf16),
            vm((rank, width_out), bf16),
            vm((rows, width_out), bf16),
            vm((rows, rank), f32),
            vm((levels, rows, rank), bf16),
            vm((levels, rows, rank), bf16),
            vm((2 * rows, rank), bf16),
            vm((levels, rows, rank), bf16),
            vm((n_width - 1, rows, rank), bf16),
            vm((2 * rows, rank), bf16),
            vm((2 * rows, width_out), bf16),
            vm((chips, 2, ib, rows), bf16),
            vm((chips, 2, ib, rows), bf16),
            vm((chips, 2, ob, rows), bf16),
            vm((chips, 2, ob, rows), bf16),
            vm((chips, 2, rb, rows), bf16),
            vm((chips, 2, rb, rows), bf16),
            vm((levels + 1, 2, ob, width_in), f32),
            vm((2 * rows, width_in), bf16),
            vm((2 * rows, 4 * ob), bf16),
            vm((2, 2, ob, rows), bf16),
            vm((2, 2, ob, rows), bf16),
            vm((levels, rows, width_in), bf16),
            vm((levels, rows, width_in), bf16),
            vm((rows, width_out), f32),
            *line_scratch((levels + 1,), ob, width_in),
            *line_scratch((), rb, width_out),
            *line_scratch((), ib, rank),
            dma((5,)),
            dma,
            dma((levels,)),
            dma,
            dma((2 * levels - 1,)),
            dma,
            dma((levels,)),
            dma,
            dma,
            dma((7,)),
            dma,
            dma,
            dma((4,)),
            dma((levels + 5,)),
            dma((3,)),
            dma((levels + 5,)),
            dma((3,)),
            pltpu.SemaphoreType.REGULAR,
            dma((2,)),
            dma((2,)),
        ],
        compiler_params=pltpu.CompilerParams(
            collective_id=0, has_side_effects=True, vmem_limit_bytes=40 * 1024 * 1024
        ),
    )(
        *(
            pltpu.with_memory_space_constraint(array, pltpu.HBM)
            for array in (
                inputs[:, 0],
                block_weights[0].transpose(1, 0, 2),
                low_left[0],
                low_right[0],
                out_grad[:, 0],
            )
        )
    )
    act, in_grad, block, left, right = pl.pallas_call(
        hand_over,
        out_shape=tuple(jax.ShapeDtypeStruct(out.shape, out.dtype) for out in outs),
        in_specs=[pl.BlockSpec(memory_space=pltpu.VMEM)] * 5,
        out_specs=(pl.BlockSpec(memory_space=pl.ANY),) * 5,
        scratch_shapes=[dma((5,))],
        compiler_params=pltpu.CompilerParams(vmem_limit_bytes=4 * 1024 * 1024),
    )(*outs)
    return (
        act[:, None],
        in_grad[:, None],
        block.transpose(1, 0, 2)[None],
        left[None],
        right[None],
    )


def solution(mesh):
    placed = (
        P("dp", "width", None),
        P("width", None, None, None),
        P("width", None, None),
        P("width", None, None),
        P("dp", "width", None),
    )
    return jax.shard_map(
        shards,
        mesh=mesh,
        in_specs=placed,
        out_specs=(
            P("dp", "width", None),
            P("dp", "width", None),
            P("width", "dp", None, None),
            P("width", "dp", None),
            P("width", "dp", None),
        ),
        check_vma=False,
    )
```

```python
import functools
import math

import jax
import jax.numpy as jnp
from jax import lax
from jax.experimental import pallas as pl
from jax.experimental.pallas import tpu as pltpu
from jax.sharding import PartitionSpec as P

root_half = 0.7071067811865476
inv_root_two_pi = 0.3989422804014327
chips_in_line = 4


def swapped(array, axis, apart):
    return lax.ppermute(array, axis, [(i, i ^ 1 << apart) for i in range(lax.axis_size(axis))])


def gelu_value(pre):
    return 0.5 * pre * (1.0 + lax.erf(pre * root_half))


def gelu_slope(pre):
    return (
        0.5 * (1.0 + lax.erf(pre * root_half)) + pre * jnp.exp(-0.5 * pre * pre) * inv_root_two_pi
    )


def plain_shards(inputs, block_weights, low_left, low_right, out_grad):
    own_x = inputs[:, 0]
    weights = block_weights[0]
    left = low_left[0]
    right = low_right[0]
    grad_out = out_grad[:, 0]
    levels = lax.axis_size("width").bit_length() - 1
    block_size = own_x.shape[1]
    scale = 1.0 / math.sqrt(own_x.shape[0] * lax.axis_size("dp"))
    pieces = [own_x]
    for bit in range(levels):
        pieces.append(swapped(own_x, "width", bit))
    all_x = jnp.stack(pieces, axis=1)
    latent = lax.psum(jnp.dot(own_x, left, preferred_element_type=jnp.float32), "width").astype(
        jnp.bfloat16
    )
    pre = lax.dot_general(
        all_x, weights, (((1, 2), (1, 2)), ((), ())), preferred_element_type=jnp.float32
    )
    pre = pre + jnp.dot(latent, right, preferred_element_type=jnp.float32)
    activations = gelu_value(pre).astype(jnp.bfloat16)
    hidden = (grad_out.astype(jnp.float32) * gelu_slope(pre)).astype(jnp.bfloat16)
    latent_term = lax.dot_general(
        hidden, right, (((1,), (1,)), ((), ())), preferred_element_type=jnp.float32
    )
    latent_grad = lax.psum(latent_term, "width").astype(jnp.bfloat16)
    partner_w = weights[:, 1:, :].reshape(weights.shape[0], levels * block_size)
    backs = jnp.dot(hidden, partner_w, preferred_element_type=jnp.float32).astype(jnp.bfloat16)
    returned = jnp.zeros(own_x.shape, jnp.float32)
    for bit in range(levels):
        piece = backs[:, bit * block_size : (bit + 1) * block_size]
        returned = returned + swapped(piece, "width", bit).astype(jnp.float32)
    own_back = jnp.dot(hidden, weights[:, 0, :], preferred_element_type=jnp.float32)
    own_back = own_back + lax.dot_general(
        latent_grad, left, (((1,), (1,)), ((), ())), preferred_element_type=jnp.float32
    )
    in_grad = (own_back + returned).astype(jnp.bfloat16)
    left_term = (
        lax.dot_general(
            own_x, latent_grad, (((0,), (0,)), ((), ())), preferred_element_type=jnp.float32
        )
        * scale
    )
    right_term = (
        lax.dot_general(
            latent, hidden, (((0,), (0,)), ((), ())), preferred_element_type=jnp.float32
        )
        * scale
    )
    block_term = (
        lax.dot_general(hidden, all_x, (((0,), (0,)), ((), ())), preferred_element_type=jnp.float32)
        * scale
    )
    block_grad, left_grad, right_grad = (
        lax.psum_scatter(block_term, "dp", scatter_dimension=0, tiled=True),
        lax.psum_scatter(left_term, "dp", scatter_dimension=0, tiled=True),
        lax.psum_scatter(right_term, "dp", scatter_dimension=0, tiled=True),
    )
    return (
        activations[:, None],
        in_grad[:, None],
        block_grad[None],
        left_grad[None],
        right_grad[None],
    )


f32 = jnp.float32
bf16 = jnp.bfloat16


def dot_nn(a, b):
    return jnp.dot(a, b, preferred_element_type=f32)


def dot_nt(a, b):
    return lax.dot_general(a, b, (((1,), (1,)), ((), ())), preferred_element_type=f32)


def remote(src, dst, send, recv, dp, width):
    return pltpu.make_async_remote_copy(
        src_ref=src,
        dst_ref=dst,
        send_sem=send,
        recv_sem=recv,
        device_id={"dp": dp, "width": width},
        device_id_type=pl.DeviceIdType.MESH,
    )


def step_kernel(
    n_dp, n_width, scale,
    x_hbm, w_hbm, left_hbm, right_hbm, g_hbm,
    act_out, in_out, block_out, left_out, right_out,
    x, w, left, right, g,
    lat_sum, lat_own, lat_got, lat, lg_own, lg_got, lg, hidden,
    x_t, x_u, h_t, h_u, lat_t, lat_u, far_acc, x_far, h_far, h_v, h_w,
    back_own, back_got, pre,
    away_b, own_b, core_b, far_b, near_b, end_b, fin_b,
    away_r, own_r, core_r, far_r, near_r, end_r, fin_r,
    away_l, own_l, core_l, far_l, near_l, end_l, fin_l,
    load_sem, x_send, x_recv, lat_send, lat_recv, lg_send, lg_recv, back_send, back_recv,
    up_sem, side_send, side_recv, core_send, core_recv, mid_send, mid_recv, end_sem,
    pace, over_send, over_recv,
):
    levels = n_width.bit_length() - 1
    chips = n_dp // 2
    dp = lax.axis_index("dp")
    me = lax.axis_index("width")
    chip, core = dp // 2, dp % 2
    other_core = 1 - core
    twin = dp + 1 - 2 * core
    side = chip // 2
    outer = (chip + side) % 2
    is_end = outer == 0
    is_hub = outer == 1
    step = 2 - 4 * side
    hub_dp = dp + step
    end_dp = dp - step
    far_dp = dp + step

    def mate(k):
        at = me
        for bit in range(levels):
            if k >> bit & 1:
                at = at + (1 << bit) * (1 - 2 * ((me // (1 << bit)) % 2))
        return at

    def shard(p):
        first = (3, 2, 0, 1)[p]
        return first + side * (chips - 1 - 2 * first)

    barrier = pltpu.get_barrier_semaphore()

    def greet(to_dp, to_width):
        pl.semaphore_signal(
            barrier,
            inc=1,
            device_id={"dp": to_dp, "width": to_width},
            device_id_type=pl.DeviceIdType.MESH,
        )

    rows = x_hbm.shape[0]
    mine, theirs = pl.ds(0, rows), pl.ds(rows, rows)
    loads = [
        pltpu.make_async_copy(src, dst, load_sem.at[i])
        for i, (src, dst) in enumerate(
            (
                (x_hbm, x.at[0, mine]),
                (left_hbm, left),
                (w_hbm, w),
                (right_hbm, right),
                (g_hbm, g),
            )
        )
    ]
    for load in loads[:2]:
        load.start()
    for k in range(1, n_width):
        greet(dp, mate(k))
    greet(twin, me)

    @pl.when(chip > 0)
    def _():
        greet(dp - 2, me)

    @pl.when(chip < chips - 1)
    def _():
        greet(dp + 2, me)

    ends = jnp.where(chip == 0, 1, 0) + jnp.where(chip == chips - 1, 1, 0)
    loads[0].wait()
    loads[1].wait()
    for load in loads[2:]:
        load.start()
    lat_sum[...] = dot_nn(x[0, mine], left[...])
    pl.semaphore_wait(barrier, n_width + 2 - ends)

    cut = rows // levels
    lead = cut // 48 * 16
    parts = [pl.ds(j * cut, cut) for j in range(levels)]
    beyond = [pl.ds(rows + j * cut, cut) for j in range(levels)]

    def x_group(part, src, j):
        return [
            remote(
                src.at[part], x.at[bit + 1, part], x_send, x_recv.at[j], dp, mate(1 << bit)
            )
            for bit in range(levels)
        ]

    x_copies = [x_group(part, x.at[0], j) for j, part in enumerate(parts)]

    def exchange(sums, out, got, send, recv, t):
        copies = []
        for j, part in enumerate(parts):
            out[t, part] = sums[part].astype(bf16)
            copies.append(
                remote(
                    out.at[t, part], got.at[t, part], send, recv(t, j),
                    dp, mate(1 << (j + t) % levels),
                )
            )
        for copy in copies:
            copy.start()

    def arrived(ref, sem):
        remote(ref, ref, core_send.at[0], sem, twin, me).wait_recv()

    def left_here(ref, sem):
        remote(ref, ref, sem, core_recv.at[0], twin, me).wait_send()

    def keep_pace():
        pl.semaphore_signal(
            pace, inc=1, device_id={"dp": twin, "width": me}, device_id_type=pl.DeviceIdType.MESH
        )
        pl.semaphore_wait(pace, 1)

    def lat_sem(t, j):
        return lat_recv.at[t + (j if t == levels - 1 else 0)]

    def lg_sem(t, j):
        return lg_recv.at[t]

    later, later_there = pl.ds(cut, rows - cut), pl.ds(rows + cut, rows - cut)
    up_x = [
        remote(x_hbm.at[part], x.at[0, there], up_sem.at[i], up_sem.at[i], hub_dp, me)
        for i, part, there in ((0, parts[0], beyond[0]), (6, later, later_there))
    ]
    side_copies = [
        remote(
            x.at[0, theirs], x.at[bit + 1, theirs], side_send, side_recv, dp, mate(1 << bit)
        )
        for bit in range(levels)
    ]

    over_x = [
        remote(
            x.at[0, these], x_far.at[these], over_send.at[0], over_recv.at[0], far_dp, me
        )
        for these in (mine, beyond[0], later_there)
    ]

    @pl.when(is_end)
    def _():
        for copy in up_x:
            copy.start()

    @pl.when(is_hub)
    def _():
        over_x[0].start()

    exchange(lat_sum, lat_own, lat_got, lat_send, lat_sem, 0)
    keep_pace()
    for copy in x_copies[0]:
        copy.start()
    loads[2].wait()
    pre[...] = dot_nt(x[0, mine], w[0])
    for t in range(1, levels):
        arrived(lat_got.at[t - 1], lat_recv.at[t - 1])
        lat_sum[...] += lat_got[t - 1].astype(f32)
        exchange(lat_sum, lat_own, lat_got, lat_send, lat_sem, t)
        for copy in x_copies[t]:
            copy.start()
    loads[3].wait()
    loads[4].wait()

    ob, rb, ib = h_t.shape[2], lat_t.shape[2], x_t.shape[2]
    last = levels + 1

    def span(p, size):
        return pl.ds(pl.multiple_of(shard(p) * size, size), size)

    up_h = [
        [
            remote(
                hidden.at[part, span(p, 2 * ob)], hidden.at[away_part, span(p, 2 * ob)],
                up_sem.at[3 + min(p, 2)], up_sem.at[3 + min(p, 2)], hub_dp, me,
            )
            for p in range(chips)
        ]
        for part, away_part in zip(parts, beyond)
    ]
    def over_h(these, p):
        return remote(
            hidden.at[these, span(p, 2 * ob)], h_far.at[these, pl.ds(2 * ob * p, 2 * ob)],
            over_send.at[1], over_recv.at[1], far_dp, me,
        )

    up_lat = [
        remote(lat.at[part], lat.at[away_part], up_sem.at[1], up_sem.at[1], hub_dp, me)
        for part, away_part in zip(parts, beyond)
    ]
    up_lg = remote(lg.at[mine], lg.at[theirs], up_sem.at[2], up_sem.at[2], hub_dp, me)
    up_views = [
        x.at[0, beyond[0]], lat.at[theirs], lg.at[theirs],
        hidden.at[theirs, pl.ds(0, 2 * ob)], hidden.at[theirs, pl.ds(0, 2 * ob)],
        hidden.at[theirs, pl.ds(0, 2 * ob * (chips - 2))], x.at[0, later_there],
    ]

    gathers = outer + core == 0

    def gather_part(part):
        lat_sum[part, :] = dot_nt(hidden[part, :], right[...])
        lg_own[0, part] = lat_sum[part, :].astype(bf16)
        for at in range(n_width):

            @pl.when(me == at)
            def _():
                order = [k for k in (at, *reversed(range(1, n_width))) if k > 0]
                for k in dict.fromkeys(order):
                    remote(
                        lg_own.at[0, part], lg_got.at[k - 1, part], lg_send, lg_recv.at[0],
                        dp, mate(k),
                    ).start()

    def add_mates(j):
        arrived(x.at[pl.ds(1, levels), parts[j]], x_recv.at[j])
        v = pre[parts[j], :]
        for bit in range(levels):
            v = v + dot_nt(x[bit + 1, parts[j]], w[bit + 1])
        return v

    pre[parts[0], :] = add_mates(0)

    @pl.when(is_hub)
    def _():
        arrived(up_views[0], up_sem.at[0])
        over_x[1].start()

    for j, part in enumerate(parts):
        arrived(lat_got.at[levels - 1, part], lat_sem(levels - 1, j))
        lat[part, :] = (lat_sum[part, :] + lat_got[levels - 1, part].astype(f32)).astype(bf16)

        @pl.when(is_end)
        def _():
            up_lat[j].start()

        pre[part, :] += dot_nn(lat[part, :], right[...])
        v = add_mates(j) if j > 0 else pre[part, :]
        half = 0.5 * (1.0 + lax.erf(v * root_half))
        act_out[part, :] = (v * half).astype(bf16)
        slope = half + v * jnp.exp(-0.5 * v * v) * inv_root_two_pi
        hidden[part, :] = (g[part, :].astype(f32) * slope).astype(bf16)

        @pl.when(is_end)
        def _():
            for p in range(2):
                up_h[j][p].start()

        @pl.when(gathers)
        def _():
            gather_part(part)

        @pl.when(is_hub)
        def _():
            for p in range(2):
                over_h(part, p).start()

        if j == 0:

            @pl.when(is_hub)
            def _():
                arrived(up_views[6], up_sem.at[6])
                over_x[2].start()
                for copy in side_copies:
                    copy.start()


    @pl.when(outer + core > 0)
    def _():
        lat_sum[...] = dot_nt(hidden[mine, :], right[...])
        exchange(lat_sum, lg_own, lg_got, lg_send, lg_sem, 0)


    def pick(kind, s):
        block, low_right, low_left = kind
        if s < last:
            return block.at[s]
        return low_right if s == last else low_left

    away = (away_b, away_r, away_l)
    own = (own_b, own_r, own_l)
    cored = (core_b, core_r, core_l)
    far = (far_b, far_r, far_l)
    near = (near_b, near_r, near_l)
    ended = (end_b, end_r, end_l)
    fin = (fin_b, fin_r, fin_l)
    segments = range(last + 2)

    def kind_of(s):
        return min(max(s - last + 1, 0), 2)

    def core_slot(s, p):
        return s - 1 if p < 2 else levels + 2 + kind_of(s)

    def mid_slot(s, p):
        return s - 1 if p == 0 else levels + 2 + kind_of(s)

    def core_copy(s, p):
        return remote(
            pick(away, s).at[p], pick(cored, s).at[p],
            core_send.at[kind_of(s) if s else 3], core_recv.at[core_slot(s, p)], twin, me,
        )

    def mid_copy(s, p):
        return remote(
            pick(far, s).at[p], pick(near, s).at[p],
            mid_send.at[kind_of(s)], mid_recv.at[mid_slot(s, p)], far_dp, me,
        )

    def end_copy(s):
        return remote(
            pick(ended, s), pick(fin, s), end_sem.at[kind_of(s)], end_sem.at[kind_of(s)],
            end_dp, me,
        )

    def put(s, total):
        if s < last:
            block_out[s] = total * scale
        elif s == last:
            right_out[...] = total * scale
        else:
            left_out[...] = total * scale

    back_copies = [
        remote(
            back_own.at[bit], back_got.at[bit], back_send, back_recv, dp, mate(1 << bit)
        )
        for bit in range(levels)
    ]

    def lg_step(t):
        arrived(lg_got.at[t - 1], lg_recv.at[t - 1])
        if t < levels:
            lat_sum[...] += lg_got[t - 1].astype(f32)
            exchange(lat_sum, lg_own, lg_got, lg_send, lg_sem, t)
        else:
            lg[mine, :] = (lat_sum[...] + lg_got[t - 1].astype(f32)).astype(bf16)

    def send_back():
        for bit in range(levels):
            back_own[bit] = dot_nn(hidden[mine, :], w[bit + 1]).astype(bf16)
            back_copies[bit].start()

    def back_ready():
        total = dot_nn(hidden[mine, :], w[0]) + dot_nt(lg[mine, :], left[...])
        arrived(back_got, back_recv)
        for bit in range(levels):
            total = total + back_got[bit].astype(f32)
        in_out[...] = total.astype(bf16)

    def sent():
        left_here(x.at[pl.ds(1, levels), mine], x_send)
        left_here(lat_own, lat_send)
        left_here(back_own, back_send)

    @pl.when(is_end)
    def _():
        def send_near():
            for j in range(levels):
                for p in range(2, chips):
                    up_h[j][p].start()

        @pl.when(gathers)
        def _():
            send_near()
            arrived(lg_got, lg_recv.at[0])
            total = lat_sum[...]
            for k in range(n_width - 1):
                total = total + lg_got[k].astype(f32)
            lg[mine, :] = total.astype(bf16)

        @pl.when(outer + core > 0)
        def _():
            for t in range(1, levels + 1):
                lg_step(t)
                if t == 1:
                    send_near()

        up_lg.start()
        keep_pace()
        send_back()
        back_ready()
        sent()

        @pl.when(gathers)
        def _():
            left_here(lg_got, lg_send)

        @pl.when(outer + core > 0)
        def _():
            left_here(lg_own, lg_send)

        for i, view in enumerate(up_views):
            left_here(view, up_sem.at[i])
        arrived(fin_b, end_sem.at[0])
        for s in range(last):
            put(s, fin_b[s].astype(f32))
        for s in range(last, last + 2):
            arrived(pick(fin, s), end_sem.at[kind_of(s)])
            put(s, pick(fin, s)[...].astype(f32))

    @pl.when(is_hub)
    def _():
        def turn(ref, which, p, size):
            tall = ref[which, span(p, size)].astype(f32).T.astype(bf16)
            return tall.reshape(2, size // 2, rows)

        def stack(ref, which, positions):
            return jnp.concatenate([ref[p, which] for p in positions], axis=0)

        def own_rows(s, which, positions):
            if s < last:
                return dot_nn(stack(h_t, which, positions), x[s, mine])
            if s == last:
                return dot_nn(stack(lat_t, which, [shard(p) for p in positions]), hidden[mine, :])
            return dot_nn(stack(x_t, which, positions), lg[mine, :])

        def their_rows(s, which, positions):
            if s < last:
                return dot_nn(stack(h_u, which, positions), x[s, theirs])
            if s == last:
                return dot_nn(stack(lat_u, which, [shard(p) for p in positions]), hidden[theirs, :])
            return dot_nn(stack(x_u, which, positions), lg[theirs, :])

        def put_terms(s, positions, to_other, to_own):
            shape = pick(own, s).shape[1:]
            for i, p in enumerate(positions):
                these = slice(i * shape[0], (i + 1) * shape[0])
                pick(away, s)[p] = to_other[these].astype(bf16)
                core_copy(s, p).start()
            for i, p in enumerate(positions):
                these = slice(i * shape[0], (i + 1) * shape[0])
                pick(own, s)[p] = to_own[these]

        def terms(s, positions):
            first = own_rows(s, other_core, positions) + their_rows(s, other_core, positions)
            put_terms(
                s, positions, first, own_rows(s, core, positions) + their_rows(s, core, positions)
            )

        def far_terms(s, positions):
            size = len(positions) * ob
            held = slice(positions[0], positions[0] + len(positions))
            first = far_acc[s, held].reshape(size, far_acc.shape[3])
            second = own_b[s, held].reshape(size, far_acc.shape[3])
            put_terms(
                s, positions, first + their_rows(s, other_core, positions),
                second + their_rows(s, core, positions),
            )

        def pair(s, p):
            return pick(own, s)[p] + pick(cored, s)[p].astype(f32)

        def core_here(s, p):
            both = pl.ds(0, 2)
            if p > 1:
                view = pick(cored, s).at[pl.ds(2, 2)] if s >= last else core_b.at[:, pl.ds(2, 2)]
            else:
                view = pick(cored, s).at[both]
            arrived(view, core_recv.at[core_slot(s, p)])

        def send_far(s, p):
            pick(far, s)[p] = pair(s, p).astype(bf16)
            mid_copy(s, p).start()

        for p in range(2):
            h_t[p] = turn(hidden, mine, p, 2 * ob)
        for s in range(1, last):
            shape = (2, ob, far_acc.shape[3])
            far_acc[s] = own_rows(s, other_core, range(2)).reshape(shape)
            own_b[s, 0:2] = own_rows(s, core, range(2)).reshape(shape)
        for p in range(2):
            arrived(up_views[3 + p], up_sem.at[3 + p])
            over_h(theirs, p).start()
            h_u[p] = turn(hidden, theirs, p, 2 * ob)
        arrived(x.at[pl.ds(1, levels), theirs], side_recv)
        for bit in range(levels):
            far_terms(bit + 1, [0, 1])
        for t in range(1, levels):
            lg_step(t)
        send_back()
        for s in range(1, last):
            core_here(s, 0)
            send_far(s, 0)
        arrived(up_views[1], up_sem.at[1])
        lat_t[...] = lat[mine, :].astype(f32).T.astype(bf16).reshape(lat_t.shape)
        lat_u[...] = lat[theirs, :].astype(f32).T.astype(bf16).reshape(lat_t.shape)
        arrived(up_views[5], up_sem.at[5])
        terms(last, range(2))
        for p in range(2, chips):
            h_t[p] = turn(hidden, mine, p, 2 * ob)
            h_u[p] = turn(hidden, theirs, p, 2 * ob)
        for s in range(1, last):
            terms(s, range(2, chips))
        terms(last, range(2, chips))
        core_here(last, 0)
        send_far(last, 0)
        arrived(x_far, over_recv.at[0])
        arrived(h_far, over_recv.at[1])
        for i in range(2):
            cols = pl.ds(2 * ob * i, 2 * ob)
            for these, ref in ((mine, h_v), (theirs, h_w)):
                ref[i] = h_far[these, cols].astype(f32).T.astype(bf16).reshape(2, ob, rows)

        def near_zero(which):
            total = own_rows(0, which, range(2, chips)) + their_rows(0, which, range(2, chips))
            total = total + dot_nn(stack(h_v, which, range(2)), x_far[mine, :])
            return total + dot_nn(stack(h_w, which, range(2)), x_far[theirs, :])

        put_terms(0, range(2, chips), near_zero(other_core), near_zero(core))
        for p in range(chips):
            x_t[p] = turn(x.at[0], mine, p, 2 * ib)
            x_u[p] = turn(x.at[0], theirs, p, 2 * ib)
        lg_step(levels)
        own_first = own_rows(last + 1, other_core, range(chips))
        own_second = own_rows(last + 1, core, range(chips))

        def send_end(s):
            total = pair(s, 2)
            if s > 0:
                arrived(pick(near, s).at[0], mid_recv.at[mid_slot(s, 0)])
                total = total + pick(near, s)[0].astype(f32)
            pick(ended, s)[...] = total.astype(bf16)
            end_copy(s).start()

        def keep(s):
            total = pair(s, 3)
            put(s, total + pick(near, s)[1].astype(f32) if s > 0 else total)

        core_here(0, 2)
        send_end(0)
        arrived(up_views[2], up_sem.at[2])
        for part in (range(2), range(2, chips)):
            held = slice(part[0] * ib, (part[-1] + 1) * ib)
            to_other = own_first[held] + their_rows(last + 1, other_core, part)
            for i, p in enumerate(part):
                away_l[p] = to_other[i * ib : (i + 1) * ib].astype(bf16)
                core_copy(last + 1, p).start()
        to_own = own_second + their_rows(last + 1, core, range(chips))
        for p in range(chips):
            own_l[p] = to_own[p * ib : (p + 1) * ib]
        send_end(1)
        core_here(last + 1, 0)
        send_far(last + 1, 0)
        for s in range(1, last + 2):
            send_far(s, 1)
        for s in range(2, last):
            send_end(s)
        core_here(last, 2)
        send_end(last)
        back_ready()
        sent()
        left_here(lg_own, lg_send)
        left_here(x.at[pl.ds(1, levels), theirs], side_send)
        left_here(away_b.at[0, pl.ds(2, 2)], core_send.at[3])
        left_here(away_b.at[pl.ds(1, levels)], core_send.at[0])
        left_here(away_r, core_send.at[1])
        left_here(away_l, core_send.at[2])
        left_here(x_far, over_send.at[0])
        left_here(h_far, over_send.at[1])
        core_here(last + 1, 2)
        send_end(last + 1)
        keep(0)
        arrived(near_b.at[pl.ds(1, levels), 1], mid_recv.at[mid_slot(1, 1)])
        for s in range(1, last):
            keep(s)
        for s in (last, last + 1):
            arrived(pick(near, s).at[1], mid_recv.at[mid_slot(s, 1)])
            keep(s)
        for i in range(3):
            left_here(far_b.at[pl.ds(1, levels)] if i == 0 else far[i], mid_send.at[i])
            left_here(ended[i], end_sem.at[i])


def hand_over(*refs):
    copies = [pltpu.make_async_copy(refs[i], refs[5 + i], refs[10].at[i]) for i in range(5)]
    for copy in copies:
        copy.start()
    for copy in copies:
        copy.wait()


def shards(inputs, block_weights, low_left, low_right, out_grad):
    n_dp, n_width = lax.axis_size("dp"), lax.axis_size("width")
    levels = n_width.bit_length() - 1
    rows, _, width_in = inputs.shape
    width_out = block_weights.shape[1]
    rank = low_left.shape[2]
    ob, ib, rb = width_out // n_dp, width_in // n_dp, rank // n_dp
    fits = n_dp == 2 * chips_in_line and rows % (16 * n_width) == 0 and rows % 32 == 0 and width_in == width_out
    if not fits or ob % 64 or ib % 64 or rb % 16 or levels < 2 or rows % (16 * levels) or rank % 128:
        return plain_shards(inputs, block_weights, low_left, low_right, out_grad)
    chips = n_dp // 2
    scale = 1.0 / math.sqrt(rows * n_dp)
    vm, dma = pltpu.VMEM, pltpu.SemaphoreType.DMA

    def line_scratch(lead, r, c):
        return [
            vm((*lead, chips, r, c), bf16),
            vm((*lead, chips, r, c), f32),
            vm((*lead, chips, r, c), bf16),
            vm((*lead, 2, r, c), bf16),
            vm((*lead, 2, r, c), bf16),
            vm((*lead, r, c), bf16),
            vm((*lead, r, c), bf16),
        ]

    outs = pl.pallas_call(
        functools.partial(step_kernel, n_dp, n_width, scale),
        out_shape=(
            jax.ShapeDtypeStruct((rows, width_out), bf16),
            jax.ShapeDtypeStruct((rows, width_in), bf16),
            jax.ShapeDtypeStruct((levels + 1, ob, width_in), f32),
            jax.ShapeDtypeStruct((ib, rank), f32),
            jax.ShapeDtypeStruct((rb, width_out), f32),
        ),
        in_specs=[pl.BlockSpec(memory_space=pltpu.HBM)] * 5,
        out_specs=(pl.BlockSpec(memory_space=pltpu.VMEM),) * 5,
        scratch_shapes=[
            vm((levels + 1, 2 * rows, width_in), bf16),
            vm((levels + 1, width_out, width_in), bf16),
            vm((width_in, rank), bf16),
            vm((rank, width_out), bf16),
            vm((rows, width_out), bf16),
            vm((rows, rank), f32),
            vm((levels, rows, rank), bf16),
            vm((levels, rows, rank), bf16),
            vm((2 * rows, rank), bf16),
            vm((levels, rows, rank), bf16),
            vm((n_width - 1, rows, rank), bf16),
            vm((2 * rows, rank), bf16),
            vm((2 * rows, width_out), bf16),
            vm((chips, 2, ib, rows), bf16),
            vm((chips, 2, ib, rows), bf16),
            vm((chips, 2, ob, rows), bf16),
            vm((chips, 2, ob, rows), bf16),
            vm((chips, 2, rb, rows), bf16),
            vm((chips, 2, rb, rows), bf16),
            vm((levels + 1, 2, ob, width_in), f32),
            vm((2 * rows, width_in), bf16),
            vm((2 * rows, 4 * ob), bf16),
            vm((2, 2, ob, rows), bf16),
            vm((2, 2, ob, rows), bf16),
            vm((levels, rows, width_in), bf16),
            vm((levels, rows, width_in), bf16),
            vm((rows, width_out), f32),
            *line_scratch((levels + 1,), ob, width_in),
            *line_scratch((), rb, width_out),
            *line_scratch((), ib, rank),
            dma((5,)),
            dma,
            dma((levels,)),
            dma,
            dma((2 * levels - 1,)),
            dma,
            dma((levels,)),
            dma,
            dma,
            dma((7,)),
            dma,
            dma,
            dma((4,)),
            dma((levels + 5,)),
            dma((3,)),
            dma((levels + 5,)),
            dma((3,)),
            pltpu.SemaphoreType.REGULAR,
            dma((2,)),
            dma((2,)),
        ],
        compiler_params=pltpu.CompilerParams(
            collective_id=0, has_side_effects=True, vmem_limit_bytes=40 * 1024 * 1024
        ),
    )(
        *(
            pltpu.with_memory_space_constraint(array, pltpu.HBM)
            for array in (
                inputs[:, 0],
                block_weights[0].transpose(1, 0, 2),
                low_left[0],
                low_right[0],
                out_grad[:, 0],
            )
        )
    )
    act, in_grad, block, left, right = pl.pallas_call(
        hand_over,
        out_shape=tuple(jax.ShapeDtypeStruct(out.shape, out.dtype) for out in outs),
        in_specs=[pl.BlockSpec(memory_space=pltpu.VMEM)] * 5,
        out_specs=(pl.BlockSpec(memory_space=pl.ANY),) * 5,
        scratch_shapes=[dma((5,))],
        compiler_params=pltpu.CompilerParams(vmem_limit_bytes=4 * 1024 * 1024),
    )(*outs)
    return (
        act[:, None],
        in_grad[:, None],
        block.transpose(1, 0, 2)[None],
        left[None],
        right[None],
    )


def solution(mesh):
    placed = (
        P("dp", "width", None),
        P("width", None, None, None),
        P("width", None, None),
        P("width", None, None),
        P("dp", "width", None),
    )
    return jax.shard_map(
        shards,
        mesh=mesh,
        in_specs=placed,
        out_specs=(
            P("dp", "width", None),
            P("dp", "width", None),
            P("width", "dp", None, None),
            P("width", "dp", None),
            P("width", "dp", None),
        ),
        check_vma=False,
    )
```

```python
import functools
import math

import jax
import jax.numpy as jnp
from jax import lax
from jax.experimental import pallas as pl
from jax.experimental.pallas import tpu as pltpu
from jax.sharding import PartitionSpec as P

root_half = 0.7071067811865476
inv_root_two_pi = 0.3989422804014327
chips_in_line = 4


def swapped(array, axis, apart):
    return lax.ppermute(array, axis, [(i, i ^ 1 << apart) for i in range(lax.axis_size(axis))])


def gelu_value(pre):
    return 0.5 * pre * (1.0 + lax.erf(pre * root_half))


def gelu_slope(pre):
    return (
        0.5 * (1.0 + lax.erf(pre * root_half)) + pre * jnp.exp(-0.5 * pre * pre) * inv_root_two_pi
    )


def plain_shards(inputs, block_weights, low_left, low_right, out_grad):
    own_x = inputs[:, 0]
    weights = block_weights[0]
    left = low_left[0]
    right = low_right[0]
    grad_out = out_grad[:, 0]
    levels = lax.axis_size("width").bit_length() - 1
    block_size = own_x.shape[1]
    scale = 1.0 / math.sqrt(own_x.shape[0] * lax.axis_size("dp"))
    pieces = [own_x]
    for bit in range(levels):
        pieces.append(swapped(own_x, "width", bit))
    all_x = jnp.stack(pieces, axis=1)
    latent = lax.psum(jnp.dot(own_x, left, preferred_element_type=jnp.float32), "width").astype(
        jnp.bfloat16
    )
    pre = lax.dot_general(
        all_x, weights, (((1, 2), (1, 2)), ((), ())), preferred_element_type=jnp.float32
    )
    pre = pre + jnp.dot(latent, right, preferred_element_type=jnp.float32)
    activations = gelu_value(pre).astype(jnp.bfloat16)
    hidden = (grad_out.astype(jnp.float32) * gelu_slope(pre)).astype(jnp.bfloat16)
    latent_term = lax.dot_general(
        hidden, right, (((1,), (1,)), ((), ())), preferred_element_type=jnp.float32
    )
    latent_grad = lax.psum(latent_term, "width").astype(jnp.bfloat16)
    partner_w = weights[:, 1:, :].reshape(weights.shape[0], levels * block_size)
    backs = jnp.dot(hidden, partner_w, preferred_element_type=jnp.float32).astype(jnp.bfloat16)
    returned = jnp.zeros(own_x.shape, jnp.float32)
    for bit in range(levels):
        piece = backs[:, bit * block_size : (bit + 1) * block_size]
        returned = returned + swapped(piece, "width", bit).astype(jnp.float32)
    own_back = jnp.dot(hidden, weights[:, 0, :], preferred_element_type=jnp.float32)
    own_back = own_back + lax.dot_general(
        latent_grad, left, (((1,), (1,)), ((), ())), preferred_element_type=jnp.float32
    )
    in_grad = (own_back + returned).astype(jnp.bfloat16)
    left_term = (
        lax.dot_general(
            own_x, latent_grad, (((0,), (0,)), ((), ())), preferred_element_type=jnp.float32
        )
        * scale
    )
    right_term = (
        lax.dot_general(
            latent, hidden, (((0,), (0,)), ((), ())), preferred_element_type=jnp.float32
        )
        * scale
    )
    block_term = (
        lax.dot_general(hidden, all_x, (((0,), (0,)), ((), ())), preferred_element_type=jnp.float32)
        * scale
    )
    block_grad, left_grad, right_grad = (
        lax.psum_scatter(block_term, "dp", scatter_dimension=0, tiled=True),
        lax.psum_scatter(left_term, "dp", scatter_dimension=0, tiled=True),
        lax.psum_scatter(right_term, "dp", scatter_dimension=0, tiled=True),
    )
    return (
        activations[:, None],
        in_grad[:, None],
        block_grad[None],
        left_grad[None],
        right_grad[None],
    )


f32 = jnp.float32
bf16 = jnp.bfloat16


def dot_nn(a, b):
    return jnp.dot(a, b, preferred_element_type=f32)


def dot_nt(a, b):
    return lax.dot_general(a, b, (((1,), (1,)), ((), ())), preferred_element_type=f32)


def remote(src, dst, send, recv, dp, width):
    return pltpu.make_async_remote_copy(
        src_ref=src,
        dst_ref=dst,
        send_sem=send,
        recv_sem=recv,
        device_id={"dp": dp, "width": width},
        device_id_type=pl.DeviceIdType.MESH,
    )


def step_kernel(
    n_dp, n_width, scale,
    x_hbm, w_hbm, left_hbm, right_hbm, g_hbm,
    act_out, in_out, block_out, left_out, right_out,
    x, w, left, right, g,
    lat_sum, lat_own, lat_got, lat, lg_own, lg_got, lg, hidden,
    x_t, x_u, h_t, h_u, lat_t, lat_u, far_acc, x_far, h_far, h_v, h_w,
    back_own, back_got, pre,
    away_b, own_b, core_b, far_b, near_b, end_b, fin_b,
    away_r, own_r, core_r, far_r, near_r, end_r, fin_r,
    away_l, own_l, core_l, far_l, near_l, end_l, fin_l,
    load_sem, x_send, x_recv, lat_send, lat_recv, lg_send, lg_recv, back_send, back_recv,
    up_sem, side_send, side_recv, core_send, core_recv, mid_send, mid_recv, end_sem,
    pace, over_send, over_recv,
):
    levels = n_width.bit_length() - 1
    chips = n_dp // 2
    dp = lax.axis_index("dp")
    me = lax.axis_index("width")
    chip, core = dp // 2, dp % 2
    other_core = 1 - core
    twin = dp + 1 - 2 * core
    side = chip // 2
    outer = (chip + side) % 2
    is_end = outer == 0
    is_hub = outer == 1
    step = 2 - 4 * side
    hub_dp = dp + step
    end_dp = dp - step
    far_dp = dp + step

    def mate(k):
        at = me
        for bit in range(levels):
            if k >> bit & 1:
                at = at + (1 << bit) * (1 - 2 * ((me // (1 << bit)) % 2))
        return at

    def shard(p):
        first = (3, 2, 0, 1)[p]
        return first + side * (chips - 1 - 2 * first)

    barrier = pltpu.get_barrier_semaphore()

    def greet(to_dp, to_width):
        pl.semaphore_signal(
            barrier,
            inc=1,
            device_id={"dp": to_dp, "width": to_width},
            device_id_type=pl.DeviceIdType.MESH,
        )

    rows = x_hbm.shape[0]
    mine, theirs = pl.ds(0, rows), pl.ds(rows, rows)
    loads = [
        pltpu.make_async_copy(src, dst, load_sem.at[i])
        for i, (src, dst) in enumerate(
            (
                (x_hbm, x.at[0, mine]),
                (left_hbm, left),
                (w_hbm, w),
                (right_hbm, right),
                (g_hbm, g),
            )
        )
    ]
    for load in loads[:2]:
        load.start()
    for k in range(1, n_width):
        greet(dp, mate(k))
    greet(twin, me)

    @pl.when(chip > 0)
    def _():
        greet(dp - 2, me)

    @pl.when(chip < chips - 1)
    def _():
        greet(dp + 2, me)

    ends = jnp.where(chip == 0, 1, 0) + jnp.where(chip == chips - 1, 1, 0)
    loads[0].wait()
    loads[1].wait()
    for load in loads[2:]:
        load.start()
    lat_sum[...] = dot_nn(x[0, mine], left[...])
    pl.semaphore_wait(barrier, n_width + 2 - ends)

    cut = rows // levels
    lead = cut // 48 * 16
    parts = [pl.ds(j * cut, cut) for j in range(levels)]
    beyond = [pl.ds(rows + j * cut, cut) for j in range(levels)]

    def x_group(part, src, j):
        return [
            remote(
                src.at[part], x.at[bit + 1, part], x_send, x_recv.at[j], dp, mate(1 << bit)
            )
            for bit in range(levels)
        ]

    x_copies = [x_group(part, x.at[0], j) for j, part in enumerate(parts)]

    def exchange(sums, out, got, send, recv, t):
        copies = []
        for j, part in enumerate(parts):
            out[t, part] = sums[part].astype(bf16)
            copies.append(
                remote(
                    out.at[t, part], got.at[t, part], send, recv(t, j),
                    dp, mate(1 << (j + t) % levels),
                )
            )
        for copy in copies:
            copy.start()

    def arrived(ref, sem):
        remote(ref, ref, core_send.at[0], sem, twin, me).wait_recv()

    def left_here(ref, sem):
        remote(ref, ref, sem, core_recv.at[0], twin, me).wait_send()

    def keep_pace():
        pl.semaphore_signal(
            pace, inc=1, device_id={"dp": twin, "width": me}, device_id_type=pl.DeviceIdType.MESH
        )
        pl.semaphore_wait(pace, 1)

    def lat_sem(t, j):
        return lat_recv.at[t + (j if t == levels - 1 else 0)]

    def lg_sem(t, j):
        return lg_recv.at[t]

    later, later_there = pl.ds(cut, rows - cut), pl.ds(rows + cut, rows - cut)
    up_x = [
        remote(x_hbm.at[part], x.at[0, there], up_sem.at[i], up_sem.at[i], hub_dp, me)
        for i, part, there in ((0, parts[0], beyond[0]), (6, later, later_there))
    ]
    side_copies = [
        remote(
            x.at[0, theirs], x.at[bit + 1, theirs], side_send, side_recv, dp, mate(1 << bit)
        )
        for bit in range(levels)
    ]

    over_x = [
        remote(
            x.at[0, these], x_far.at[these], over_send.at[0], over_recv.at[0], far_dp, me
        )
        for these in (mine, beyond[0], later_there)
    ]

    @pl.when(is_end)
    def _():
        for copy in up_x:
            copy.start()

    @pl.when(is_hub)
    def _():
        over_x[0].start()

    exchange(lat_sum, lat_own, lat_got, lat_send, lat_sem, 0)
    keep_pace()
    for copy in x_copies[0]:
        copy.start()
    loads[2].wait()
    pre[...] = dot_nt(x[0, mine], w[0])
    for t in range(1, levels):
        arrived(lat_got.at[t - 1], lat_recv.at[t - 1])
        lat_sum[...] += lat_got[t - 1].astype(f32)
        exchange(lat_sum, lat_own, lat_got, lat_send, lat_sem, t)
        for copy in x_copies[t]:
            copy.start()
    loads[3].wait()
    loads[4].wait()

    ob, rb, ib = h_t.shape[2], lat_t.shape[2], x_t.shape[2]
    last = levels + 1

    def span(p, size):
        return pl.ds(pl.multiple_of(shard(p) * size, size), size)

    up_h = [
        [
            remote(
                hidden.at[part, span(p, 2 * ob)], hidden.at[away_part, span(p, 2 * ob)],
                up_sem.at[3 + min(p, 2)], up_sem.at[3 + min(p, 2)], hub_dp, me,
            )
            for p in range(chips)
        ]
        for part, away_part in zip(parts, beyond)
    ]
    def over_h(these, p):
        return remote(
            hidden.at[these, span(p, 2 * ob)], h_far.at[these, pl.ds(2 * ob * p, 2 * ob)],
            over_send.at[1], over_recv.at[1], far_dp, me,
        )

    up_lat = [
        remote(lat.at[part], lat.at[away_part], up_sem.at[1], up_sem.at[1], hub_dp, me)
        for part, away_part in zip(parts, beyond)
    ]
    up_lg = remote(lg.at[mine], lg.at[theirs], up_sem.at[2], up_sem.at[2], hub_dp, me)
    up_views = [
        x.at[0, beyond[0]], lat.at[theirs], lg.at[theirs],
        hidden.at[theirs, pl.ds(0, 2 * ob)], hidden.at[theirs, pl.ds(0, 2 * ob)],
        hidden.at[theirs, pl.ds(0, 2 * ob * (chips - 2))], x.at[0, later_there],
    ]

    gathers = outer + core == 0

    def gather_part(part):
        lat_sum[part, :] = dot_nt(hidden[part, :], right[...])
        lg_own[0, part] = lat_sum[part, :].astype(bf16)
        for at in range(n_width):

            @pl.when(me == at)
            def _():
                order = [k for k in (at, *reversed(range(1, n_width))) if k > 0]
                for k in dict.fromkeys(order):
                    remote(
                        lg_own.at[0, part], lg_got.at[k - 1, part], lg_send, lg_recv.at[0],
                        dp, mate(k),
                    ).start()

    def add_mates(j):
        arrived(x.at[pl.ds(1, levels), parts[j]], x_recv.at[j])
        v = pre[parts[j], :]
        for bit in range(levels):
            v = v + dot_nt(x[bit + 1, parts[j]], w[bit + 1])
        return v

    pre[parts[0], :] = add_mates(0)

    @pl.when(is_hub)
    def _():
        arrived(up_views[0], up_sem.at[0])
        over_x[1].start()

    for j, part in enumerate(parts):
        arrived(lat_got.at[levels - 1, part], lat_sem(levels - 1, j))
        lat[part, :] = (lat_sum[part, :] + lat_got[levels - 1, part].astype(f32)).astype(bf16)

        @pl.when(is_end)
        def _():
            up_lat[j].start()

        pre[part, :] += dot_nn(lat[part, :], right[...])
        v = add_mates(j) if j > 0 else pre[part, :]
        half = 0.5 * (1.0 + lax.erf(v * root_half))
        act_out[part, :] = (v * half).astype(bf16)
        slope = half + v * jnp.exp(-0.5 * v * v) * inv_root_two_pi
        hidden[part, :] = (g[part, :].astype(f32) * slope).astype(bf16)

        @pl.when(is_end)
        def _():
            for p in range(2):
                up_h[j][p].start()

        @pl.when(gathers)
        def _():
            gather_part(part)

        @pl.when(is_hub)
        def _():
            for p in range(2):
                over_h(part, p).start()

        if j == 0:

            @pl.when(is_hub)
            def _():
                arrived(up_views[6], up_sem.at[6])
                over_x[2].start()
                for copy in side_copies:
                    copy.start()


    @pl.when(outer + core > 0)
    def _():
        lat_sum[...] = dot_nt(hidden[mine, :], right[...])
        exchange(lat_sum, lg_own, lg_got, lg_send, lg_sem, 0)


    def pick(kind, s):
        block, low_right, low_left = kind
        if s < last:
            return block.at[s]
        return low_right if s == last else low_left

    away = (away_b, away_r, away_l)
    own = (own_b, own_r, own_l)
    cored = (core_b, core_r, core_l)
    far = (far_b, far_r, far_l)
    near = (near_b, near_r, near_l)
    ended = (end_b, end_r, end_l)
    fin = (fin_b, fin_r, fin_l)
    segments = range(last + 2)

    def kind_of(s):
        return min(max(s - last + 1, 0), 2)

    def core_slot(s, p):
        return s - 1 if p < 2 else levels + 2 + kind_of(s)

    def mid_slot(s, p):
        return s - 1 if p == 0 else levels + 2 + kind_of(s)

    def core_copy(s, p):
        return remote(
            pick(away, s).at[p], pick(cored, s).at[p],
            core_send.at[kind_of(s) if s else 3], core_recv.at[core_slot(s, p)], twin, me,
        )

    def mid_copy(s, p):
        return remote(
            pick(far, s).at[p], pick(near, s).at[p],
            mid_send.at[kind_of(s)], mid_recv.at[mid_slot(s, p)], far_dp, me,
        )

    def end_copy(s):
        return remote(
            pick(ended, s), pick(fin, s), end_sem.at[kind_of(s)], end_sem.at[kind_of(s)],
            end_dp, me,
        )

    def put(s, total):
        if s < last:
            block_out[s] = total * scale
        elif s == last:
            right_out[...] = total * scale
        else:
            left_out[...] = total * scale

    back_copies = [
        remote(
            back_own.at[bit], back_got.at[bit], back_send, back_recv, dp, mate(1 << bit)
        )
        for bit in range(levels)
    ]

    def lg_step(t):
        arrived(lg_got.at[t - 1], lg_recv.at[t - 1])
        if t < levels:
            lat_sum[...] += lg_got[t - 1].astype(f32)
            exchange(lat_sum, lg_own, lg_got, lg_send, lg_sem, t)
        else:
            lg[mine, :] = (lat_sum[...] + lg_got[t - 1].astype(f32)).astype(bf16)

    def send_back():
        for bit in range(levels):
            back_own[bit] = dot_nn(hidden[mine, :], w[bit + 1]).astype(bf16)
            back_copies[bit].start()

    def back_ready():
        total = dot_nn(hidden[mine, :], w[0]) + dot_nt(lg[mine, :], left[...])
        arrived(back_got, back_recv)
        for bit in range(levels):
            total = total + back_got[bit].astype(f32)
        in_out[...] = total.astype(bf16)

    def sent():
        left_here(x.at[pl.ds(1, levels), mine], x_send)
        left_here(lat_own, lat_send)
        left_here(back_own, back_send)

    @pl.when(is_end)
    def _():
        def send_near():
            for j in range(levels):
                for p in range(2, chips):
                    up_h[j][p].start()

        @pl.when(gathers)
        def _():
            send_near()
            arrived(lg_got, lg_recv.at[0])
            total = lat_sum[...]
            for k in range(n_width - 1):
                total = total + lg_got[k].astype(f32)
            lg[mine, :] = total.astype(bf16)

        @pl.when(outer + core > 0)
        def _():
            for t in range(1, levels + 1):
                lg_step(t)
                if t == 1:
                    send_near()

        up_lg.start()
        keep_pace()
        send_back()
        back_ready()
        sent()

        @pl.when(gathers)
        def _():
            left_here(lg_got, lg_send)

        @pl.when(outer + core > 0)
        def _():
            left_here(lg_own, lg_send)

        for i, view in enumerate(up_views):
            left_here(view, up_sem.at[i])
        arrived(fin_b, end_sem.at[0])
        for s in range(last):
            put(s, fin_b[s].astype(f32))
        for s in range(last, last + 2):
            arrived(pick(fin, s), end_sem.at[kind_of(s)])
            put(s, pick(fin, s)[...].astype(f32))

    @pl.when(is_hub)
    def _():
        def turn(ref, which, p, size):
            tall = ref[which, span(p, size)].astype(f32).T.astype(bf16)
            return tall.reshape(2, size // 2, rows)

        def stack(ref, which, positions):
            return jnp.concatenate([ref[p, which] for p in positions], axis=0)

        def own_rows(s, which, positions):
            if s < last:
                return dot_nn(stack(h_t, which, positions), x[s, mine])
            if s == last:
                return dot_nn(stack(lat_t, which, [shard(p) for p in positions]), hidden[mine, :])
            return dot_nn(stack(x_t, which, positions), lg[mine, :])

        def their_rows(s, which, positions):
            if s < last:
                return dot_nn(stack(h_u, which, positions), x[s, theirs])
            if s == last:
                return dot_nn(stack(lat_u, which, [shard(p) for p in positions]), hidden[theirs, :])
            return dot_nn(stack(x_u, which, positions), lg[theirs, :])

        def put_terms(s, positions, to_other, to_own):
            shape = pick(own, s).shape[1:]
            for i, p in enumerate(positions):
                these = slice(i * shape[0], (i + 1) * shape[0])
                pick(away, s)[p] = to_other[these].astype(bf16)
                core_copy(s, p).start()
            for i, p in enumerate(positions):
                these = slice(i * shape[0], (i + 1) * shape[0])
                pick(own, s)[p] = to_own[these]

        def terms(s, positions):
            first = own_rows(s, other_core, positions) + their_rows(s, other_core, positions)
            put_terms(
                s, positions, first, own_rows(s, core, positions) + their_rows(s, core, positions)
            )

        def far_terms(s, positions):
            size = len(positions) * ob
            held = slice(positions[0], positions[0] + len(positions))
            first = far_acc[s, held].reshape(size, far_acc.shape[3])
            second = own_b[s, held].reshape(size, far_acc.shape[3])
            put_terms(
                s, positions, first + their_rows(s, other_core, positions),
                second + their_rows(s, core, positions),
            )

        def pair(s, p):
            return pick(own, s)[p] + pick(cored, s)[p].astype(f32)

        def core_here(s, p):
            both = pl.ds(0, 2)
            if p > 1:
                view = pick(cored, s).at[pl.ds(2, 2)] if s >= last else core_b.at[:, pl.ds(2, 2)]
            else:
                view = pick(cored, s).at[both]
            arrived(view, core_recv.at[core_slot(s, p)])

        def send_far(s, p):
            pick(far, s)[p] = pair(s, p).astype(bf16)
            mid_copy(s, p).start()

        for p in range(2):
            h_t[p] = turn(hidden, mine, p, 2 * ob)
        for s in range(1, last):
            shape = (2, ob, far_acc.shape[3])
            far_acc[s] = own_rows(s, other_core, range(2)).reshape(shape)
            own_b[s, 0:2] = own_rows(s, core, range(2)).reshape(shape)
        for p in range(2):
            arrived(up_views[3 + p], up_sem.at[3 + p])
            over_h(theirs, p).start()
            h_u[p] = turn(hidden, theirs, p, 2 * ob)
        arrived(x.at[pl.ds(1, levels), theirs], side_recv)
        for bit in range(levels):
            far_terms(bit + 1, [0, 1])
        for t in range(1, levels):
            lg_step(t)
        send_back()
        for s in range(1, last):
            core_here(s, 0)
            send_far(s, 0)
        arrived(up_views[1], up_sem.at[1])
        lat_t[...] = lat[mine, :].astype(f32).T.astype(bf16).reshape(lat_t.shape)
        lat_u[...] = lat[theirs, :].astype(f32).T.astype(bf16).reshape(lat_t.shape)
        arrived(up_views[5], up_sem.at[5])
        terms(last, range(2))
        for p in range(2, chips):
            h_t[p] = turn(hidden, mine, p, 2 * ob)
            h_u[p] = turn(hidden, theirs, p, 2 * ob)
        for s in range(1, last):
            terms(s, range(2, chips))
        terms(last, range(2, chips))
        core_here(last, 0)
        send_far(last, 0)
        arrived(x_far, over_recv.at[0])
        arrived(h_far, over_recv.at[1])
        for i in range(2):
            cols = pl.ds(2 * ob * i, 2 * ob)
            for these, ref in ((mine, h_v), (theirs, h_w)):
                ref[i] = h_far[these, cols].astype(f32).T.astype(bf16).reshape(2, ob, rows)

        def near_zero(which):
            total = own_rows(0, which, range(2, chips)) + their_rows(0, which, range(2, chips))
            total = total + dot_nn(stack(h_v, which, range(2)), x_far[mine, :])
            return total + dot_nn(stack(h_w, which, range(2)), x_far[theirs, :])

        put_terms(0, range(2, chips), near_zero(other_core), near_zero(core))
        for p in range(chips):
            x_t[p] = turn(x.at[0], mine, p, 2 * ib)
            x_u[p] = turn(x.at[0], theirs, p, 2 * ib)
        lg_step(levels)
        own_first = own_rows(last + 1, other_core, range(chips))
        own_second = own_rows(last + 1, core, range(chips))

        def send_end(s):
            total = pair(s, 2)
            if s > 0:
                arrived(pick(near, s).at[0], mid_recv.at[mid_slot(s, 0)])
                total = total + pick(near, s)[0].astype(f32)
            pick(ended, s)[...] = total.astype(bf16)
            end_copy(s).start()

        def keep(s):
            total = pair(s, 3)
            put(s, total + pick(near, s)[1].astype(f32) if s > 0 else total)

        core_here(0, 2)
        send_end(0)
        arrived(up_views[2], up_sem.at[2])
        def left_terms(part):
            held = slice(part[0] * ib, (part[-1] + 1) * ib)
            to_other = own_first[held] + their_rows(last + 1, other_core, part)
            for i, p in enumerate(part):
                away_l[p] = to_other[i * ib : (i + 1) * ib].astype(bf16)
                core_copy(last + 1, p).start()
            to_own = own_second[held] + their_rows(last + 1, core, part)
            for i, p in enumerate(part):
                own_l[p] = to_own[i * ib : (i + 1) * ib]

        def send_left():
            core_here(last + 1, 0)
            send_far(last + 1, 0)

        left_terms(range(2))
        pl.when(side + other_core == 2)(send_left)
        left_terms(range(2, chips))
        send_end(1)
        pl.when(side + other_core < 2)(send_left)
        for s in range(1, last + 2):
            send_far(s, 1)
        for s in range(2, last):
            send_end(s)
        core_here(last, 2)
        send_end(last)
        back_ready()
        sent()
        left_here(lg_own, lg_send)
        left_here(x.at[pl.ds(1, levels), theirs], side_send)
        left_here(away_b.at[0, pl.ds(2, 2)], core_send.at[3])
        left_here(away_b.at[pl.ds(1, levels)], core_send.at[0])
        left_here(away_r, core_send.at[1])
        left_here(away_l, core_send.at[2])
        left_here(x_far, over_send.at[0])
        left_here(h_far, over_send.at[1])
        core_here(last + 1, 2)
        send_end(last + 1)
        keep(0)
        arrived(near_b.at[pl.ds(1, levels), 1], mid_recv.at[mid_slot(1, 1)])
        for s in range(1, last):
            keep(s)
        for s in (last, last + 1):
            arrived(pick(near, s).at[1], mid_recv.at[mid_slot(s, 1)])
            keep(s)
        for i in range(3):
            left_here(far_b.at[pl.ds(1, levels)] if i == 0 else far[i], mid_send.at[i])
            left_here(ended[i], end_sem.at[i])


def hand_over(*refs):
    copies = [pltpu.make_async_copy(refs[i], refs[5 + i], refs[10].at[i]) for i in range(5)]
    for copy in copies:
        copy.start()
    for copy in copies:
        copy.wait()


def shards(inputs, block_weights, low_left, low_right, out_grad):
    n_dp, n_width = lax.axis_size("dp"), lax.axis_size("width")
    levels = n_width.bit_length() - 1
    rows, _, width_in = inputs.shape
    width_out = block_weights.shape[1]
    rank = low_left.shape[2]
    ob, ib, rb = width_out // n_dp, width_in // n_dp, rank // n_dp
    fits = n_dp == 2 * chips_in_line and rows % (16 * n_width) == 0 and rows % 32 == 0 and width_in == width_out
    if not fits or ob % 64 or ib % 64 or rb % 16 or levels < 2 or rows % (16 * levels) or rank % 128:
        return plain_shards(inputs, block_weights, low_left, low_right, out_grad)
    chips = n_dp // 2
    scale = 1.0 / math.sqrt(rows * n_dp)
    vm, dma = pltpu.VMEM, pltpu.SemaphoreType.DMA

    def line_scratch(lead, r, c):
        return [
            vm((*lead, chips, r, c), bf16),
            vm((*lead, chips, r, c), f32),
            vm((*lead, chips, r, c), bf16),
            vm((*lead, 2, r, c), bf16),
            vm((*lead, 2, r, c), bf16),
            vm((*lead, r, c), bf16),
            vm((*lead, r, c), bf16),
        ]

    outs = pl.pallas_call(
        functools.partial(step_kernel, n_dp, n_width, scale),
        out_shape=(
            jax.ShapeDtypeStruct((rows, width_out), bf16),
            jax.ShapeDtypeStruct((rows, width_in), bf16),
            jax.ShapeDtypeStruct((levels + 1, ob, width_in), f32),
            jax.ShapeDtypeStruct((ib, rank), f32),
            jax.ShapeDtypeStruct((rb, width_out), f32),
        ),
        in_specs=[pl.BlockSpec(memory_space=pltpu.HBM)] * 5,
        out_specs=(pl.BlockSpec(memory_space=pltpu.VMEM),) * 5,
        scratch_shapes=[
            vm((levels + 1, 2 * rows, width_in), bf16),
            vm((levels + 1, width_out, width_in), bf16),
            vm((width_in, rank), bf16),
            vm((rank, width_out), bf16),
            vm((rows, width_out), bf16),
            vm((rows, rank), f32),
            vm((levels, rows, rank), bf16),
            vm((levels, rows, rank), bf16),
            vm((2 * rows, rank), bf16),
            vm((levels, rows, rank), bf16),
            vm((n_width - 1, rows, rank), bf16),
            vm((2 * rows, rank), bf16),
            vm((2 * rows, width_out), bf16),
            vm((chips, 2, ib, rows), bf16),
            vm((chips, 2, ib, rows), bf16),
            vm((chips, 2, ob, rows), bf16),
            vm((chips, 2, ob, rows), bf16),
            vm((chips, 2, rb, rows), bf16),
            vm((chips, 2, rb, rows), bf16),
            vm((levels + 1, 2, ob, width_in), f32),
            vm((2 * rows, width_in), bf16),
            vm((2 * rows, 4 * ob), bf16),
            vm((2, 2, ob, rows), bf16),
            vm((2, 2, ob, rows), bf16),
            vm((levels, rows, width_in), bf16),
            vm((levels, rows, width_in), bf16),
            vm((rows, width_out), f32),
            *line_scratch((levels + 1,), ob, width_in),
            *line_scratch((), rb, width_out),
            *line_scratch((), ib, rank),
            dma((5,)),
            dma,
            dma((levels,)),
            dma,
            dma((2 * levels - 1,)),
            dma,
            dma((levels,)),
            dma,
            dma,
            dma((7,)),
            dma,
            dma,
            dma((4,)),
            dma((levels + 5,)),
            dma((3,)),
            dma((levels + 5,)),
            dma((3,)),
            pltpu.SemaphoreType.REGULAR,
            dma((2,)),
            dma((2,)),
        ],
        compiler_params=pltpu.CompilerParams(
            collective_id=0, has_side_effects=True, vmem_limit_bytes=40 * 1024 * 1024
        ),
    )(
        *(
            pltpu.with_memory_space_constraint(array, pltpu.HBM)
            for array in (
                inputs[:, 0],
                block_weights[0].transpose(1, 0, 2),
                low_left[0],
                low_right[0],
                out_grad[:, 0],
            )
        )
    )
    act, in_grad, block, left, right = pl.pallas_call(
        hand_over,
        out_shape=tuple(jax.ShapeDtypeStruct(out.shape, out.dtype) for out in outs),
        in_specs=[pl.BlockSpec(memory_space=pltpu.VMEM)] * 5,
        out_specs=(pl.BlockSpec(memory_space=pl.ANY),) * 5,
        scratch_shapes=[dma((5,))],
        compiler_params=pltpu.CompilerParams(vmem_limit_bytes=4 * 1024 * 1024),
    )(*outs)
    return (
        act[:, None],
        in_grad[:, None],
        block.transpose(1, 0, 2)[None],
        left[None],
        right[None],
    )


def solution(mesh):
    placed = (
        P("dp", "width", None),
        P("width", None, None, None),
        P("width", None, None),
        P("width", None, None),
        P("dp", "width", None),
    )
    return jax.shard_map(
        shards,
        mesh=mesh,
        in_specs=placed,
        out_specs=(
            P("dp", "width", None),
            P("dp", "width", None),
            P("width", "dp", None, None),
            P("width", "dp", None),
            P("width", "dp", None),
        ),
        check_vma=False,
    )
```
